128 devices in a mesh: seq: 16 (over y, x), exp: 8 (over z, core).
Axes of the slice: x: 4, y: 4, z: 4, core: 2. Of those that a mesh axis runs over, the one named last changes fastest.
Arguments:
- stream: bfloat16 [2048, 4096], P('seq', 'exp'), may hold values from -6 to 6
- mixer_in: bfloat16 [2048, 8192], P('seq', 'exp'), may hold values from -6 to 6
- gate_in: bfloat16 [2048, 8192], P('seq', 'exp'), may hold values from -6 to 6
- dt_raw: bfloat16 [2048, 8192], P('seq', 'exp'), may hold values from -2 to 13
- dt_bias: float32 [8192], P('exp'), may hold values from -13 to -2
- a_log: float32 [8192, 16], P('exp'), may hold values from -1.2 to 0.7
- conv_weight: float32 [8192, 4], P('exp'), may hold values from -3 to 3
- conv_bias: float32 [8192], P('exp'), may hold values from -6 to 6
- b_proj: float32 [2048, 16], P('seq'), may hold values from -6 to 6
- c_proj: float32 [2048, 16], P('seq'), may hold values from -6 to 6
- d_skip: float32 [8192], P('exp'), may hold values from 0.3 to 3
- w_out: bfloat16 [8192, 4096], P('exp', 'seq'), may hold values from -0.0625 to 0.0625
- expert_index: int32 [2048, 2], P('seq'), may hold values from 0 to 7, all different within a row; in each aligned block of 128 rows (0 to 127, 128 to 255, ...) at most 48 rows name the same one
- gate_weights: float32 [2048, 2], P('seq'), may hold values from 0.05 to 0.6
- norm_gain: float32 [4096], replicated, may hold values from 0.1 to 1.9
- w_gate: bfloat16 [8, 4096, 12288], P('exp', None, 'seq'), may hold values from -0.09375 to 0.09375
- w_up: bfloat16 [8, 4096, 12288], P('exp', None, 'seq'), may hold values from -0.09375 to 0.09375
- w_down: bfloat16 [8, 12288, 4096], P('exp', 'seq'), may hold values from -0.0546875 to 0.0546875
Outputs:
- block_out: bfloat16 [2048, 4096], P('seq', 'exp')
The draws below stay inside these ranges and needn't reach their ends.
Inputs may be any that keep to these rules, and one draw needn't show every extreme that they name: `expert_index`: the two experts of a position differ. Among the 128 positions of one seq shard (aligned blocks), no expert is chosen by more than 48 routes, and in every draw some expert is chosen by exactly 48.
All inputs are finite; a program needn't handle non-finite values.
Results may differ from the reference program's by a relative error of at most 0.012.
Values may be sent and summed in bfloat16 or wider, within the bound.
No kernel may reach another device: no remote copies, remote signals or barrier semaphores. Data moves between devices by JAX's collectives and lax.ppermute only.
A program may use at most 192 MiB of HBM per device.

```python
import math
import jax
import jax.numpy as jnp
import numpy as np
from jax import lax

D = 4096
E = 8192
FF = 12288
DSTATE = 16
KCONV = 4
TOK_DEV = 128
EXPERTS = 8
LENGTH = 2048
CAP = 48
N_SEQ = 16


def log_rates(key):
    lowest = math.log(0.1 / LENGTH)
    highest = math.log(0.05)
    return jax.random.uniform(jax.random.fold_in(key, 71), (E,), jnp.float32, lowest, highest)


def draw_dt_bias(key, part):
    return log_rates(key)


def draw_dt_raw(key, part):
    exponent_additive = log_rates(key)
    jitter = jnp.clip(0.5 * jax.random.normal(jax.random.fold_in(key, 72), (LENGTH, E), jnp.float32), -1.5, 1.5)
    bucket_indices = jax.random.randint(jax.random.fold_in(key, 73), (6,), 0, LENGTH)
    destination_lines = jax.random.uniform(jax.random.fold_in(key, 74), (6, E), jnp.float32, 0.3, 0.7)
    packet_batches = jnp.log(jnp.expm1(destination_lines)) - exponent_additive[None, :]
    element_index = jnp.arange(LENGTH)[:, None]
    layer_response = jitter
    for packet_count in range(6):
        layer_response = jnp.where(element_index == bucket_indices[packet_count], packet_batches[packet_count][None, :], layer_response)
    return layer_response.astype(jnp.bfloat16)


def steps_of(own_key, shape, split, low, high):
    level = 1.0
    for position, shards_of in split:
        heights = jax.random.uniform(jax.random.fold_in(jax.random.fold_in(own_key, 6), position), (shards_of,), jnp.float32, low / len(split), high / len(split))
        level = level * jnp.repeat(jnp.exp(heights), shape[position] // shards_of).reshape((-1,) + (1,) * (len(shape) - 1 - position))
    return level


def routed_block(stream_key, own, number, rows, number_of, top, bound, lean):
    sequence = jax.random.permutation(stream_key, number_of)
    packed, common = load_shares(number_of, rows * top, bound, lean, True), load_shares(number_of, rows * top, bound, lean, False)
    places = jnp.arange(number_of)

    def named(lengths, offset_by):
        used = int((lengths > 0).sum())
        fixed = max(1, used // 4)
        moved = fixed + (places - fixed + offset_by * (used - fixed)) % max(1, number_of - fixed)
        return jnp.zeros((number_of,), jnp.int32).at[sequence[jnp.where(places < fixed, places, moved)]].set(jnp.asarray(lengths, jnp.int32))

    lengths = jnp.where(number % 4 == 0, named(packed, number // 4), named(common, number - number // 4 - 1))
    mixed = jax.random.permutation(jax.random.fold_in(own, 3), number_of)
    donor, receiver = mixed[0:number_of // 2 * 2:2], mixed[1:number_of // 2 * 2:2]
    margin = jnp.minimum(lengths[donor] - 1, bound - lengths[receiver]) // 2
    margin = jnp.where((donor == sequence[0]) | (receiver == sequence[0]) | (lengths[receiver] == 0), 0, jnp.maximum(margin, 0))
    moved = jax.random.randint(jax.random.fold_in(own, 4), (number_of // 2,), 0, 1 << 20) % (margin + 1)
    lengths = lengths.at[donor].add(-moved).at[receiver].add(moved)
    members = jnp.searchsorted(jnp.cumsum(lengths), jnp.arange(rows * top), side="right").astype(jnp.int32)
    table = members.reshape(top, rows).T
    table = table[jax.random.permutation(jax.random.fold_in(own, 1), rows)]
    offset_by = jax.random.randint(jax.random.fold_in(own, 2), (rows, 1), 0, top)
    return jnp.take_along_axis(table, (jnp.arange(top)[None, :] + offset_by) % top, axis=1)


def load_shares(amount, total, bound, skew, full):
    loads = [(1 << 20) // math.isqrt(rank ** skew) + 1 for rank in range(1, amount + 1)]
    largest = bound if full else min(bound, max(-(-total // amount), total * loads[0] // sum(loads)))
    least = 1 if total - largest >= amount - 1 else 0
    given, rest = [largest] + [least] * (amount - 1), total - largest - least * (amount - 1)
    while rest > 0:
        free = [i for i in range(1, amount) if given[i] < largest] or [i for i in range(1, amount) if given[i] < bound]
        pool, left = sum([loads[i] for i in free]), rest
        for i in free:
            addition = min(bound - given[i], max(1, left * loads[i] // pool), rest)
            given[i] = given[i] + addition
            rest = rest - addition
    return np.array(given)


def gaussian(key, extent, scale, limit, cuts=(), held_as=jnp.bfloat16):
    drawn = scale * jax.random.normal(key, extent, jnp.float32)
    if cuts:
        drawn = drawn * steps_of(key, extent, cuts, -0.22, 0.18)
    return jnp.clip(drawn, -limit, limit).astype(held_as)


def setup_inputs(seed: int = 0) -> dict:
    seeds = jax.random.split(jax.random.key(seed), 19)
    stream = gaussian(seeds[0], (LENGTH, D), 1.0, 6.0, ((0, 16), (1, 8)))
    mixer_in = gaussian(seeds[1], (LENGTH, E), 1.0, 6.0, ((0, 16), (1, 8)))
    gate_in = gaussian(seeds[2], (LENGTH, E), 1.0, 6.0, ((0, 16), (1, 8)))
    dt_raw = draw_dt_raw(jax.random.fold_in(seeds[18], 71), 0)
    dt_bias = draw_dt_bias(jax.random.fold_in(seeds[18], 71), 0)
    a_log = jnp.clip(-1.2 + 1.90000004 * jax.random.uniform(seeds[5], (E, DSTATE), jnp.float32) ** steps_of(seeds[5], (E, DSTATE), ((0, 8),), -0.2, 0.2), -1.2, 0.7)
    conv_weight = gaussian(seeds[6], (E, KCONV), KCONV ** -0.5, 3.0, ((0, 8),), jnp.float32)
    conv_bias = gaussian(seeds[7], (E,), 1.0, 6.0, ((0, 8),), jnp.float32)
    b_proj = gaussian(seeds[8], (LENGTH, DSTATE), 1.0, 6.0, ((0, 16),), jnp.float32)
    c_proj = gaussian(seeds[9], (LENGTH, DSTATE), 1.0, 6.0, ((0, 16),), jnp.float32)
    d_skip = jnp.clip(jnp.exp(math.log(3.0) - 2.3025851 * jax.random.uniform(seeds[10], (E,), jnp.float32) ** steps_of(seeds[10], (E,), ((0, 8),), -0.2, 0.2)), 0.3, 3.0)
    w_out = gaussian(seeds[11], (E, D), E ** -0.5, 0.0625, ((0, 8), (1, 16)))
    expert_index_keys = jax.random.split(jax.random.fold_in(seeds[12], 1), LENGTH // TOK_DEV)
    expert_index_turns = jax.random.permutation(jax.random.fold_in(seeds[12], 3), LENGTH // TOK_DEV)
    expert_index = jax.vmap(lambda own, number: routed_block(jax.random.fold_in(seeds[12], 2), own, number, TOK_DEV, EXPERTS, 2, CAP, 2))(expert_index_keys, expert_index_turns).reshape((LENGTH, 2))
    gate_weights = jnp.clip(0.05 + 0.55 * jax.random.uniform(seeds[13], (LENGTH, 2), jnp.float32) ** steps_of(seeds[13], (LENGTH, 2), ((0, 16),), -0.2, 0.2), 0.05, 0.6)
    norm_gain = jnp.clip(1.0 + 0.18 * jax.random.normal(seeds[14], (D,), jnp.float32), 0.1, 1.9)
    w_gate = gaussian(seeds[15], (EXPERTS, D, FF), D ** -0.5, 0.09375, ((0, 8), (2, 16)))
    w_up = gaussian(seeds[16], (EXPERTS, D, FF), D ** -0.5, 0.09375, ((0, 8), (2, 16)))
    w_down = gaussian(seeds[17], (EXPERTS, FF, D), FF ** -0.5, 0.0546875, ((0, 8), (1, 16)))
    return dict(stream=stream, mixer_in=mixer_in, gate_in=gate_in, dt_raw=dt_raw, dt_bias=dt_bias, a_log=a_log, conv_weight=conv_weight, conv_bias=conv_bias, b_proj=b_proj, c_proj=c_proj, d_skip=d_skip, w_out=w_out, expert_index=expert_index, gate_weights=gate_weights, norm_gain=norm_gain, w_gate=w_gate, w_up=w_up, w_down=w_down)


def reference(stream, mixer_in, gate_in, dt_raw, dt_bias, a_log, conv_weight, conv_bias, b_proj, c_proj, d_skip, w_out, expert_index, gate_weights, norm_gain, w_gate, w_up, w_down):
    inputs = mixer_in.astype(jnp.float32)
    padded = jnp.concatenate([jnp.zeros((KCONV - 1, E), jnp.float32), inputs], 0)
    conv_sum = conv_bias[None, :] + sum((conv_weight[:, offset][None, :] * padded[offset:offset + LENGTH] for offset in range(KCONV)))
    activated = jax.nn.silu(conv_sum)
    step_size = jax.nn.softplus(dt_raw.astype(jnp.float32) + dt_bias[None, :])
    rate_table = jnp.exp(a_log)

    def advance(carry_state, inputs_now):
        step_row, act_row, b_row, c_row = inputs_now
        carry_state = jnp.exp(-step_row[:, None] * rate_table) * carry_state + step_row[:, None] * b_row[None, :] * act_row[:, None]
        return (carry_state, lax.optimization_barrier(jnp.sum(carry_state * c_row[None, :], axis=1)))
    _, scanned = lax.scan(advance, jnp.zeros((E, DSTATE), jnp.float32), (step_size, activated, b_proj, c_proj))
    mixed = ((scanned + d_skip[None, :] * activated) * jax.nn.silu(gate_in.astype(jnp.float32))).astype(jnp.bfloat16)
    projected = jnp.dot(mixed, w_out, preferred_element_type=jnp.float32)
    middle = (stream.astype(jnp.float32) + projected).astype(jnp.bfloat16)
    middle_f = middle.astype(jnp.float32)
    mean_square = lax.optimization_barrier(jnp.mean(middle_f * middle_f, axis=1, keepdims=True))
    normed = (middle_f * lax.rsqrt(mean_square + 1e-05) * norm_gain[None, :]).astype(jnp.bfloat16)
    flat_exp = expert_index.reshape(N_SEQ, TOK_DEV * 2).astype(jnp.int32)
    onehot = (flat_exp[:, :, None] == jnp.arange(EXPERTS, dtype=jnp.int32)[None, None, :]).astype(jnp.int32)
    ranks = jnp.cumsum(onehot, axis=1) - onehot
    slots = lax.optimization_barrier(jnp.sum(ranks * onehot, axis=2)).astype(jnp.int32)
    shard_ids = jnp.broadcast_to(jnp.arange(N_SEQ, dtype=jnp.int32)[:, None], (N_SEQ, TOK_DEV * 2))
    token_ids = (shard_ids * TOK_DEV + jnp.arange(TOK_DEV * 2, dtype=jnp.int32)[None, :] // 2).astype(jnp.int32)
    slot_table = jnp.zeros((N_SEQ, EXPERTS, CAP, D), jnp.bfloat16).at[shard_ids, flat_exp, slots].set(normed[token_ids])
    shard_width = FF // N_SEQ
    results = []
    for expert in range(EXPERTS):
        rows_in = slot_table[:, expert].reshape(N_SEQ * CAP, D)
        gate_proj = jnp.dot(rows_in, w_gate[expert], preferred_element_type=jnp.float32)
        up_proj = jnp.dot(rows_in, w_up[expert], preferred_element_type=jnp.float32)
        hidden = (jax.nn.silu(gate_proj) * up_proj).astype(jnp.bfloat16)
        total = jnp.zeros((N_SEQ * CAP, D), jnp.float32)
        for shard in range(N_SEQ):
            lower = shard * shard_width
            partial_out = jnp.dot(hidden[:, lower:lower + shard_width], w_down[expert, lower:lower + shard_width], preferred_element_type=jnp.float32)
            total = total + partial_out.astype(jnp.bfloat16).astype(jnp.float32)
        results.append(total.reshape(N_SEQ, CAP, D))
    expert_rows = jnp.stack(results, axis=1)
    picked = expert_rows[shard_ids, flat_exp, slots].reshape(LENGTH, 2, D)
    expert_sum = lax.optimization_barrier(jnp.sum(gate_weights[:, :, None] * picked, axis=1))
    return (middle_f + expert_sum).astype(jnp.bfloat16)
```

```python
import jax
import jax.numpy as jnp
from jax import lax
from jax.experimental import pallas as pl
from jax.experimental.pallas import tpu as pltpu
from jax.sharding import PartitionSpec as P

KCONV = 4
SIDE = 4
STATES = 16
LOG2E = 1.4426950408889634
F32 = jnp.float32
BF16 = jnp.bfloat16


def shift(value, axis, distance):
    cells = [(y, x) for y in range(SIDE) for x in range(SIDE)]
    if axis == "x":
        route = [(y * SIDE + x, y * SIDE + (x + distance) % SIDE) for y, x in cells]
    else:
        route = [(y * SIDE + x, (y + distance) % SIDE * SIDE + x) for y, x in cells]
    return lax.ppermute(value, "seq", route)


def ring_gather(block, axis):
    half = block.shape[-2] // 2
    before = shift(block, axis, 1)
    after = shift(block, axis, -1)
    first = shift(before[..., :half, :], axis, 1)
    second = shift(after[..., half:, :], axis, -1)
    return [block, before, after, jnp.concatenate([first, second], -2)]


def ring_scatter(blocks, axis):
    own, minus, plus, far = blocks
    half = far.shape[-2] // 2
    far = far.astype(BF16)
    via_plus = shift(far[..., :half, :], axis, 1).astype(F32)
    via_minus = shift(far[..., half:, :], axis, -1).astype(F32)
    plus = plus.astype(F32)
    minus = minus.astype(F32)
    plus = jnp.concatenate([plus[..., :half, :] + via_plus, plus[..., half:, :]], -2)
    minus = jnp.concatenate([minus[..., :half, :], minus[..., half:, :] + via_minus], -2)
    from_minus = shift(plus.astype(BF16), axis, 1).astype(F32)
    from_plus = shift(minus.astype(BF16), axis, -1).astype(F32)
    return own.astype(F32) + from_minus + from_plus


def first_pass(x_ref, rim_ref, dt_ref, dtb_ref, cw_ref, cb_ref, rate_ref, b_ref,
               step_ref, act_ref, fin_ref, pad_ref):
    tokens, channels = x_ref.shape
    lanes = 128
    pad_ref[8 : 8 + tokens, :] = x_ref[...].astype(F32)
    pad_ref[0:8, :] = rim_ref[...].astype(F32)
    for k in range(channels // lanes):
        cols = slice(k * lanes, (k + 1) * lanes)
        total = cb_ref[:, cols]
        for tap in range(KCONV):
            low = 8 - (KCONV - 1) + tap
            total = total + cw_ref[tap : tap + 1, cols] * pad_ref[low : low + tokens, cols]
        act_ref[:, k, :] = total * jax.nn.sigmoid(total)
        raw = dt_ref[:, cols].astype(F32) + dtb_ref[:, cols]
        step_ref[:, k, :] = jnp.maximum(raw, 0.0) + jnp.log1p(jnp.exp(-jnp.abs(raw)))

    def advance(t, carry):
        states, summed = carry
        step = step_ref[t]
        source = step * act_ref[t]
        states = tuple(
            jnp.exp2(step * rate_ref[n]) * states[n] + b_ref[t, n] * source for n in range(STATES)
        )
        return states, summed + step

    zero = jnp.zeros((8, lanes), F32)
    states, summed = lax.fori_loop(0, tokens, advance, ((zero,) * STATES, zero), unroll=2)
    for n in range(STATES):
        fin_ref[n] = states[n]
    fin_ref[STATES] = summed


def second_pass(step_ref, act_ref, gate_ref, enter_ref, rate_ref, skip_ref, b_ref, c_ref,
                out_ref, y_ref):
    tokens, channels = gate_ref.shape
    lanes = 128
    skip = skip_ref[...]

    def advance(t, states):
        step = step_ref[t]
        act = act_ref[t]
        source = step * act
        sums = [skip * act, None]
        after = []
        for n in range(STATES):
            state = jnp.exp2(step * rate_ref[n]) * states[n] + b_ref[t, n] * source
            term = c_ref[t, n] * state
            sums[n % 2] = term if sums[n % 2] is None else sums[n % 2] + term
            after.append(state)
        y_ref[t] = sums[0] + sums[1]
        return tuple(after)

    lax.fori_loop(0, tokens, advance, tuple(enter_ref[n] for n in range(STATES)), unroll=2)
    for k in range(channels // lanes):
        cols = slice(k * lanes, (k + 1) * lanes)
        gate = gate_ref[:, cols].astype(F32)
        out_ref[:, cols] = (y_ref[:, k, :] * (gate * jax.nn.sigmoid(gate))).astype(BF16)


def entering_state(final, rate):
    along_x = lax.axis_index("seq") % SIDE
    along_y = lax.axis_index("seq") // SIDE

    def chain(earlier, latter):
        decay = jnp.exp2(rate * latter[1])
        return decay * earlier[0] + latter[0], earlier[1] + latter[1]

    def masked(pair, reached):
        return jnp.where(reached, pair[0], 0.0), jnp.where(reached, pair[1], 0.0)

    def split(packed):
        return packed[:STATES], packed[STATES]

    def spread(packed, axis, place):
        others = [split(shift(packed, axis, d)) for d in range(1, SIDE)]
        before = masked(others[2], place >= 3)
        for d in (2, 1):
            before = chain(before, masked(others[d - 1], place >= d))
        return before, others

    own = split(final)
    before_x, others = spread(final, "x", along_x)
    total = chain(before_x, own)
    for d in (3, 2, 1):
        total = chain(total, masked(others[d - 1], along_x < d))
    packed = jnp.concatenate([total[0], total[1][None]], 0)
    before_y, _ = spread(packed, "y", along_y)
    return chain(before_y, before_x)[0]


def mixer(mixer_in, gate_in, dt_raw, dt_bias, a_log, conv_weight, conv_bias, b_proj, c_proj, d_skip):
    tokens, channels = mixer_in.shape
    count, index = lax.axis_size("seq"), lax.axis_index("seq")
    rim = lax.ppermute(mixer_in[tokens - 8 :], "seq", [(i, i + 1) for i in range(count - 1)])
    rate = (-LOG2E * jnp.exp(a_log)).T.reshape(STATES, 8, 128)
    vmem = pl.BlockSpec(memory_space=pltpu.VMEM)
    smem = pl.BlockSpec(memory_space=pltpu.SMEM)
    wide = jax.ShapeDtypeStruct((tokens, 8, 128), F32)
    step, act, final = pl.pallas_call(
        first_pass,
        out_shape=(wide, wide, jax.ShapeDtypeStruct((STATES + 1, 8, 128), F32)),
        in_specs=[vmem] * 7 + [smem],
        out_specs=[vmem] * 3,
        scratch_shapes=[pltpu.VMEM((tokens + 8, channels), F32)],
        compiler_params=pltpu.CompilerParams(vmem_limit_bytes=32 << 20),
        name="scan_state",
    )(mixer_in, rim, dt_raw, dt_bias[None, :], conv_weight.T, conv_bias[None, :], rate, b_proj)
    enter = entering_state(final, rate)
    return pl.pallas_call(
        second_pass,
        out_shape=jax.ShapeDtypeStruct((tokens, channels), BF16),
        in_specs=[vmem] * 6 + [smem] * 2,
        out_specs=vmem,
        scratch_shapes=[pltpu.VMEM((tokens, 8, 128), F32)],
        compiler_params=pltpu.CompilerParams(vmem_limit_bytes=32 << 20),
        name="scan_output",
    )(step, act, gate_in, enter, rate, d_skip.reshape(8, 128), b_proj, c_proj)


def local(
    stream,
    mixer_in,
    gate_in,
    dt_raw,
    dt_bias,
    a_log,
    conv_weight,
    conv_bias,
    b_proj,
    c_proj,
    d_skip,
    w_out,
    expert_index,
    gate_weights,
    norm_gain,
    w_gate,
    w_up,
    w_down,
):
    tokens = mixer_in.shape[0]
    experts = lax.axis_size("exp")
    groups = lax.axis_size("seq")
    capacity = 3 * tokens // experts
    width = stream.shape[1]
    all_out = lax.all_gather(w_out, "seq", axis=0)
    mixed = mixer(
        mixer_in, gate_in, dt_raw, dt_bias, a_log, conv_weight, conv_bias, b_proj, c_proj, d_skip
    )
    proj = jnp.einsum("tc,jcd->jtd", mixed, all_out, preferred_element_type=F32).astype(BF16)
    proj = proj.reshape(experts, groups // experts, tokens, -1)
    proj = lax.all_to_all(proj, "exp", split_axis=0, concat_axis=0)
    projected = jnp.sum(proj.astype(F32), axis=0).transpose(1, 0, 2).reshape(tokens, width)
    middle = (stream.astype(F32) + projected).astype(BF16)

    flat_exp = expert_index.reshape(-1)
    onehot = (flat_exp[:, None] == jnp.arange(experts, dtype=jnp.int32)[None, :]).astype(jnp.int32)
    ranks = jnp.cumsum(onehot, axis=0) - onehot
    slots = jnp.sum(ranks * onehot, axis=1)
    slot_id = (flat_exp * capacity + slots).reshape(tokens, 2)
    places = jnp.arange(experts * capacity, dtype=jnp.int32)
    chosen = (
        (slot_id[:, 0][None, :] == places[:, None]) | (slot_id[:, 1][None, :] == places[:, None])
    ).astype(BF16)
    outgoing = jnp.dot(chosen, middle, preferred_element_type=F32).astype(BF16)
    outgoing = outgoing.reshape(experts, capacity, width)
    arrived = lax.all_to_all(outgoing, "exp", split_axis=0, concat_axis=2, tiled=True)[0].astype(F32)
    mean_square = jnp.mean(arrived * arrived, axis=1, keepdims=True)
    normed = (arrived * lax.rsqrt(mean_square + 1e-05) * norm_gain[None, :]).astype(BF16)

    half = capacity // 2
    parts = []
    for rows, order in ((normed[:half], "xy"), (normed[half:], "yx")):
        near = jnp.stack(ring_gather(rows, order[0]))
        parts.append(ring_gather(near, order[1]))

    def feed(rows):
        flat = rows.reshape(-1, rows.shape[-1])
        gate_proj = jnp.dot(flat, w_gate[0], preferred_element_type=F32)
        up_proj = jnp.dot(flat, w_up[0], preferred_element_type=F32)
        hidden = (jax.nn.silu(gate_proj) * up_proj).astype(BF16)
        out = jnp.dot(hidden, w_down[0], preferred_element_type=F32).astype(BF16)
        return out.reshape(rows.shape)

    fed = [feed(jnp.stack([a, b])) for a, b in zip(*parts)]
    sums = []
    for which, order in ((0, "yx"), (1, "xy")):
        near = ring_scatter([f[which] for f in fed], order[0])
        sums.append(ring_scatter([near[i] for i in range(SIDE)], order[1]))
    summed = jnp.concatenate(sums, 0).astype(BF16)
    returned = lax.all_to_all(summed[None], "exp", split_axis=2, concat_axis=0, tiled=True)
    returned = returned.reshape(experts * capacity, width)
    expert_sum = 0.0
    for k in range(2):
        pick = (slot_id[:, k][:, None] == places[None, :]).astype(BF16)
        picked = jnp.dot(pick, returned, preferred_element_type=F32)
        expert_sum = expert_sum + gate_weights[:, k][:, None] * picked
    return (middle.astype(F32) + expert_sum).astype(BF16)


def solution(mesh):
    return jax.shard_map(
        local,
        mesh=mesh,
        in_specs=(
            P("seq", "exp"),
            P("seq", "exp"),
            P("seq", "exp"),
            P("seq", "exp"),
            P("exp"),
            P("exp", None),
            P("exp", None),
            P("exp"),
            P("seq", None),
            P("seq", None),
            P("exp"),
            P("exp", "seq"),
            P("seq", None),
            P("seq", None),
            P(),
            P("exp", None, "seq"),
            P("exp", None, "seq"),
            P("exp", "seq", None),
        ),
        out_specs=P("seq", "exp"),
        check_vma=False,
    )
```

```python
import jax
import jax.numpy as jnp
from jax import lax
from jax.experimental import pallas as pl
from jax.experimental.pallas import tpu as pltpu
from jax.sharding import PartitionSpec as P

KCONV = 4
SIDE = 4
STATES = 16
LOG2E = 1.4426950408889634
F32 = jnp.float32
BF16 = jnp.bfloat16


def shift(value, axis, distance):
    cells = [(y, x) for y in range(SIDE) for x in range(SIDE)]
    if axis == "x":
        route = [(y * SIDE + x, y * SIDE + (x + distance) % SIDE) for y, x in cells]
    else:
        route = [(y * SIDE + x, (y + distance) % SIDE * SIDE + x) for y, x in cells]
    return lax.ppermute(value, "seq", route)


def ring_gather(block, axis):
    return [block] + [shift(block, axis, distance) for distance in range(1, SIDE)]


def grid_gather(block, order):
    near = jnp.stack(ring_gather(block, order[0]))
    return ring_gather(near, order[1])


def ring_scatter(blocks, axis):
    total = blocks[0].astype(F32)
    for k in (1, 3, 2):
        total = total + shift(blocks[k].astype(BF16), axis, -k).astype(F32)
    return total


def first_pass(x_ref, rim_ref, dt_ref, dtb_ref, cw_ref, cb_ref, rate_ref, b_ref,
               step_ref, act_ref, fin_ref, pad_ref):
    tokens, channels = x_ref.shape
    lanes = 128
    pad_ref[8 : 8 + tokens, :] = x_ref[...].astype(F32)
    pad_ref[0:8, :] = rim_ref[...].astype(F32)
    for k in range(channels // lanes):
        cols = slice(k * lanes, (k + 1) * lanes)
        total = cb_ref[:, cols]
        for tap in range(KCONV):
            low = 8 - (KCONV - 1) + tap
            total = total + cw_ref[tap : tap + 1, cols] * pad_ref[low : low + tokens, cols]
        act_ref[:, k, :] = total * jax.nn.sigmoid(total)
        raw = dt_ref[:, cols].astype(F32) + dtb_ref[:, cols]
        step_ref[:, k, :] = jnp.maximum(raw, 0.0) + jnp.log1p(jnp.exp(-jnp.abs(raw)))

    def advance(t, carry):
        states, summed = carry
        step = step_ref[t]
        source = step * act_ref[t]
        states = tuple(
            jnp.exp2(step * rate_ref[n]) * states[n] + b_ref[t, n] * source for n in range(STATES)
        )
        return states, summed + step

    zero = jnp.zeros((8, lanes), F32)
    states, summed = lax.fori_loop(0, tokens, advance, ((zero,) * STATES, zero), unroll=2)
    for n in range(STATES):
        fin_ref[n] = states[n]
    fin_ref[STATES] = summed


def second_pass(step_ref, act_ref, gate_ref, enter_ref, rate_ref, skip_ref, b_ref, c_ref,
                out_ref, y_ref):
    tokens, channels = gate_ref.shape
    lanes = 128
    skip = skip_ref[...]

    def advance(t, states):
        step = step_ref[t]
        act = act_ref[t]
        source = step * act
        sums = [skip * act, None]
        after = []
        for n in range(STATES):
            state = jnp.exp2(step * rate_ref[n]) * states[n] + b_ref[t, n] * source
            term = c_ref[t, n] * state
            sums[n % 2] = term if sums[n % 2] is None else sums[n % 2] + term
            after.append(state)
        y_ref[t] = sums[0] + sums[1]
        return tuple(after)

    lax.fori_loop(0, tokens, advance, tuple(enter_ref[n] for n in range(STATES)), unroll=2)
    for k in range(channels // lanes):
        cols = slice(k * lanes, (k + 1) * lanes)
        gate = gate_ref[:, cols].astype(F32)
        out_ref[:, cols] = (y_ref[:, k, :] * (gate * jax.nn.sigmoid(gate))).astype(BF16)


def entering_state(final, rate):
    along_x = lax.axis_index("seq") % SIDE
    along_y = lax.axis_index("seq") // SIDE

    def chain(earlier, latter):
        decay = jnp.exp2(rate * latter[1])
        return decay * earlier[0] + latter[0], earlier[1] + latter[1]

    def masked(pair, reached):
        return jnp.where(reached, pair[0], 0.0), jnp.where(reached, pair[1], 0.0)

    def split(packed):
        return packed[:STATES], packed[STATES]

    def spread(packed, axis, place):
        others = [split(shift(packed, axis, d)) for d in range(1, SIDE)]
        before = masked(others[2], place >= 3)
        for d in (2, 1):
            before = chain(before, masked(others[d - 1], place >= d))
        return before, others

    own = split(final)
    before_x, others = spread(final, "x", along_x)
    total = chain(before_x, own)
    for d in (3, 2, 1):
        total = chain(total, masked(others[d - 1], along_x < d))
    packed = jnp.concatenate([total[0], total[1][None]], 0)
    before_y, _ = spread(packed, "y", along_y)
    return chain(before_y, before_x)[0]


def mixer(mixer_in, gate_in, dt_raw, dt_bias, a_log, conv_weight, conv_bias, b_proj, c_proj, d_skip):
    tokens, channels = mixer_in.shape
    count, index = lax.axis_size("seq"), lax.axis_index("seq")
    rim = lax.ppermute(mixer_in[tokens - 8 :], "seq", [(i, i + 1) for i in range(count - 1)])
    rate = (-LOG2E * jnp.exp(a_log)).T.reshape(STATES, 8, 128)
    vmem = pl.BlockSpec(memory_space=pltpu.VMEM)
    smem = pl.BlockSpec(memory_space=pltpu.SMEM)
    wide = jax.ShapeDtypeStruct((tokens, 8, 128), F32)
    step, act, final = pl.pallas_call(
        first_pass,
        out_shape=(wide, wide, jax.ShapeDtypeStruct((STATES + 1, 8, 128), F32)),
        in_specs=[vmem] * 7 + [smem],
        out_specs=[vmem] * 3,
        scratch_shapes=[pltpu.VMEM((tokens + 8, channels), F32)],
        compiler_params=pltpu.CompilerParams(vmem_limit_bytes=32 << 20),
        name="scan_state",
    )(mixer_in, rim, dt_raw, dt_bias[None, :], conv_weight.T, conv_bias[None, :], rate, b_proj)
    enter = entering_state(final, rate)
    return pl.pallas_call(
        second_pass,
        out_shape=jax.ShapeDtypeStruct((tokens, channels), BF16),
        in_specs=[vmem] * 6 + [smem] * 2,
        out_specs=vmem,
        scratch_shapes=[pltpu.VMEM((tokens, 8, 128), F32)],
        compiler_params=pltpu.CompilerParams(vmem_limit_bytes=32 << 20),
        name="scan_output",
    )(step, act, gate_in, enter, rate, d_skip.reshape(8, 128), b_proj, c_proj)


def project_kernel(place_ref, mixed_ref, fixed_ref, *refs):
    parts, out_ref = (refs[:SIDE], refs[SIDE : 2 * SIDE]), refs[2 * SIDE]
    depth = fixed_ref.shape[1]
    part = parts[0][0].shape[1]
    y, x = place_ref[0], place_ref[1]
    for i in range(SIDE):
        for j in range(SIDE):
            row = lax.rem(y - i + SIDE, SIDE)
            col = lax.rem(x - j + SIDE, SIDE)
            home = row * SIDE + col
            total = jnp.dot(
                mixed_ref[:, :depth], fixed_ref[home], preferred_element_type=F32
            )
            total += jnp.dot(
                mixed_ref[:, depth : depth + part], parts[0][i][j], preferred_element_type=F32
            )
            total += jnp.dot(
                mixed_ref[:, depth + part :], parts[1][j][i], preferred_element_type=F32
            )
            out_ref[home] = total.astype(BF16)


def project(mixed, w_out_parts):
    fixed, first, second = w_out_parts
    place = lax.axis_index("seq")
    place = jnp.stack([place // SIDE, place % SIDE]).astype(jnp.int32)
    vmem = pl.BlockSpec(memory_space=pltpu.VMEM)
    return pl.pallas_call(
        project_kernel,
        out_shape=jax.ShapeDtypeStruct((SIDE * SIDE, mixed.shape[0], fixed.shape[2]), BF16),
        in_specs=[pl.BlockSpec(memory_space=pltpu.SMEM)] + [vmem] * (2 + 2 * SIDE),
        out_specs=vmem,
        compiler_params=pltpu.CompilerParams(vmem_limit_bytes=40 << 20),
        name="project",
    )(place, mixed, fixed, *first, *second)


def local(
    stream,
    mixer_in,
    gate_in,
    dt_raw,
    dt_bias,
    a_log,
    conv_weight,
    conv_bias,
    b_proj,
    c_proj,
    d_skip,
    w_out,
    expert_index,
    gate_weights,
    norm_gain,
    w_gate,
    w_up,
    w_down,
):
    tokens = mixer_in.shape[0]
    experts = lax.axis_size("exp")
    groups = lax.axis_size("seq")
    capacity = 3 * tokens // experts
    width = stream.shape[1]
    depth = w_out.shape[0] // 2
    part = depth // 2
    out_parts = (
        lax.all_gather(w_out[:depth], "seq", axis=0),
        grid_gather(w_out[depth : depth + part], "xy"),
        grid_gather(w_out[depth + part :], "yx"),
    )
    mixed = mixer(
        mixer_in, gate_in, dt_raw, dt_bias, a_log, conv_weight, conv_bias, b_proj, c_proj, d_skip
    )
    proj = project(mixed, out_parts)
    proj = proj.reshape(experts, groups // experts, tokens, -1)
    proj = lax.all_to_all(proj, "exp", split_axis=0, concat_axis=0)
    projected = jnp.sum(proj.astype(F32), axis=0).transpose(1, 0, 2).reshape(tokens, width)
    middle = (stream.astype(F32) + projected).astype(BF16)

    flat_exp = expert_index.reshape(-1)
    onehot = (flat_exp[:, None] == jnp.arange(experts, dtype=jnp.int32)[None, :]).astype(jnp.int32)
    ranks = jnp.cumsum(onehot, axis=0) - onehot
    slots = jnp.sum(ranks * onehot, axis=1)
    slot_id = (flat_exp * capacity + slots).reshape(tokens, 2)
    places = jnp.arange(experts * capacity, dtype=jnp.int32)
    chosen = (
        (slot_id[:, 0][None, :] == places[:, None]) | (slot_id[:, 1][None, :] == places[:, None])
    ).astype(BF16)
    outgoing = jnp.dot(chosen, middle, preferred_element_type=F32).astype(BF16)
    outgoing = outgoing.reshape(experts, capacity, width)
    arrived = lax.all_to_all(outgoing, "exp", split_axis=0, concat_axis=2, tiled=True)[0].astype(F32)
    mean_square = jnp.mean(arrived * arrived, axis=1, keepdims=True)
    normed = (arrived * lax.rsqrt(mean_square + 1e-05) * norm_gain[None, :]).astype(BF16)

    half = capacity // 2
    first = grid_gather(normed[:half], "xy")
    second = grid_gather(normed[half:], "yx")

    def feed(offsets):
        rows = jnp.stack([part[k] for part in (first, second) for k in offsets])
        flat = rows.reshape(-1, rows.shape[-1])
        gate_proj = jnp.dot(flat, w_gate[0], preferred_element_type=F32)
        up_proj = jnp.dot(flat, w_up[0], preferred_element_type=F32)
        hidden = lax.optimization_barrier((jax.nn.silu(gate_proj) * up_proj).astype(BF16))
        out = jnp.dot(hidden, w_down[0], preferred_element_type=F32).astype(BF16)
        return out.reshape((2, len(offsets)) + rows.shape[1:])

    fed = {}
    for offsets in ((0,), (1, 3), (2,)):
        out = feed(offsets)
        for at, k in enumerate(offsets):
            fed[k] = out[:, at]
    sums = []
    for which, order in ((0, "yx"), (1, "xy")):
        near = ring_scatter([fed[k][which] for k in range(SIDE)], order[0])
        sums.append(ring_scatter([near[k] for k in range(SIDE)], order[1]))
    summed = jnp.concatenate(sums, 0).astype(BF16)
    summed = summed.reshape(capacity, experts, width).transpose(1, 0, 2)
    returned = lax.all_to_all(summed, "exp", split_axis=0, concat_axis=0)
    returned = returned.reshape(experts * capacity, width)
    expert_sum = 0.0
    for k in range(2):
        pick = (slot_id[:, k][:, None] == places[None, :]).astype(BF16)
        picked = jnp.dot(pick, returned, preferred_element_type=F32)
        expert_sum = expert_sum + gate_weights[:, k][:, None] * picked
    return (middle.astype(F32) + expert_sum).astype(BF16)


def solution(mesh):
    return jax.shard_map(
        local,
        mesh=mesh,
        in_specs=(
            P("seq", "exp"),
            P("seq", "exp"),
            P("seq", "exp"),
            P("seq", "exp"),
            P("exp"),
            P("exp", None),
            P("exp", None),
            P("exp"),
            P("seq", None),
            P("seq", None),
            P("exp"),
            P("exp", "seq"),
            P("seq", None),
            P("seq", None),
            P(),
            P("exp", None, "seq"),
            P("exp", None, "seq"),
            P("exp", "seq", None),
        ),
        out_specs=P("seq", "exp"),
        check_vma=False,
    )
```

```python
import jax
import jax.numpy as jnp
from jax import lax
from jax.experimental import pallas as pl
from jax.experimental.pallas import tpu as pltpu
from jax.sharding import PartitionSpec as P

KCONV = 4
SIDE = 4
STATES = 16
LOG2E = 1.4426950408889634
F32 = jnp.float32
BF16 = jnp.bfloat16


def shift(value, axis, distance):
    cells = [(y, x) for y in range(SIDE) for x in range(SIDE)]
    if axis == "x":
        route = [(y * SIDE + x, y * SIDE + (x + distance) % SIDE) for y, x in cells]
    else:
        route = [(y * SIDE + x, (y + distance) % SIDE * SIDE + x) for y, x in cells]
    return lax.ppermute(value, "seq", route)


def keeper_shift(value, axis, distance):
    route = []
    for y in range(SIDE):
        for x in range(SIDE):
            for z in range(SIDE):
                start = [y, x, z, x // 2]
                end = [y, x, z, x // 2]
                if axis == "core":
                    start[3] = 1 - start[3]
                else:
                    at = "yxz".index(axis)
                    end[at] = (end[at] + distance) % SIDE
                route.append(tuple((v[0] * SIDE + v[1]) * 2 * SIDE + v[2] * 2 + v[3] for v in (start, end)))
    return lax.ppermute(value, ("seq", "exp"), route)


def ring_gather(block, axis):
    return [block] + [shift(block, axis, distance) for distance in range(1, SIDE)]


def grid_gather(block, order):
    near = jnp.stack(ring_gather(block, order[0]))
    return ring_gather(near, order[1])


def ring_scatter(blocks, axis):
    total = blocks[0].astype(F32)
    for k in (1, 3, 2):
        total = total + shift(blocks[k].astype(BF16), axis, -k).astype(F32)
    return total


def first_pass(x_ref, rim_ref, dt_ref, dtb_ref, cw_ref, cb_ref, rate_ref, b_ref,
               step_ref, act_ref, fin_ref, pad_ref):
    tokens, channels = x_ref.shape
    lanes = 128
    pad_ref[8 : 8 + tokens, :] = x_ref[...].astype(F32)
    pad_ref[0:8, :] = rim_ref[...].astype(F32)
    for k in range(channels // lanes):
        cols = slice(k * lanes, (k + 1) * lanes)
        total = cb_ref[:, cols]
        for tap in range(KCONV):
            low = 8 - (KCONV - 1) + tap
            total = total + cw_ref[tap : tap + 1, cols] * pad_ref[low : low + tokens, cols]
        act_ref[:, k, :] = total * jax.nn.sigmoid(total)
        raw = dt_ref[:, cols].astype(F32) + dtb_ref[:, cols]
        step_ref[:, k, :] = jnp.maximum(raw, 0.0) + jnp.log1p(jnp.exp(-jnp.abs(raw)))

    def advance(t, carry):
        states, summed = carry
        step = step_ref[t]
        source = step * act_ref[t]
        states = tuple(
            jnp.exp2(step * rate_ref[n]) * states[n] + b_ref[t, n] * source for n in range(STATES)
        )
        return states, summed + step

    zero = jnp.zeros((8, lanes), F32)
    states, summed = lax.fori_loop(0, tokens, advance, ((zero,) * STATES, zero), unroll=2)
    for n in range(STATES):
        fin_ref[n] = states[n]
    fin_ref[STATES] = summed


def second_pass(step_ref, act_ref, gate_ref, enter_ref, rate_ref, skip_ref, b_ref, c_ref,
                out_ref, y_ref):
    tokens, channels = gate_ref.shape
    lanes = 128
    skip = skip_ref[...]

    def advance(t, states):
        step = step_ref[t]
        act = act_ref[t]
        source = step * act
        sums = [skip * act, None]
        after = []
        for n in range(STATES):
            state = jnp.exp2(step * rate_ref[n]) * states[n] + b_ref[t, n] * source
            term = c_ref[t, n] * state
            sums[n % 2] = term if sums[n % 2] is None else sums[n % 2] + term
            after.append(state)
        y_ref[t] = sums[0] + sums[1]
        return tuple(after)

    lax.fori_loop(0, tokens, advance, tuple(enter_ref[n] for n in range(STATES)), unroll=2)
    for k in range(channels // lanes):
        cols = slice(k * lanes, (k + 1) * lanes)
        gate = gate_ref[:, cols].astype(F32)
        out_ref[:, cols] = (y_ref[:, k, :] * (gate * jax.nn.sigmoid(gate))).astype(BF16)


def entering_state(final, rate):
    along_x = lax.axis_index("seq") % SIDE
    along_y = lax.axis_index("seq") // SIDE

    def chain(earlier, latter):
        decay = jnp.exp2(rate * latter[1])
        return decay * earlier[0] + latter[0], earlier[1] + latter[1]

    def masked(pair, reached):
        return jnp.where(reached, pair[0], 0.0), jnp.where(reached, pair[1], 0.0)

    def split(packed):
        return packed[:STATES], packed[STATES]

    def spread(packed, axis, place):
        others = [split(shift(packed, axis, d)) for d in range(1, SIDE)]
        before = masked(others[2], place >= 3)
        for d in (2, 1):
            before = chain(before, masked(others[d - 1], place >= d))
        return before, others

    own = split(final)
    before_x, others = spread(final, "x", along_x)
    total = chain(before_x, own)
    for d in (3, 2, 1):
        total = chain(total, masked(others[d - 1], along_x < d))
    packed = jnp.concatenate([total[0], total[1][None]], 0)
    before_y, _ = spread(packed, "y", along_y)
    return chain(before_y, before_x)[0]


def mixer(mixer_in, gate_in, dt_raw, dt_bias, a_log, conv_weight, conv_bias, b_proj, c_proj, d_skip):
    tokens, channels = mixer_in.shape
    count, index = lax.axis_size("seq"), lax.axis_index("seq")
    rim = lax.ppermute(mixer_in[tokens - 8 :], "seq", [(i, i + 1) for i in range(count - 1)])
    rate = (-LOG2E * jnp.exp(a_log)).T.reshape(STATES, 8, 128)
    vmem = pl.BlockSpec(memory_space=pltpu.VMEM)
    smem = pl.BlockSpec(memory_space=pltpu.SMEM)
    wide = jax.ShapeDtypeStruct((tokens, 8, 128), F32)
    step, act, final = pl.pallas_call(
        first_pass,
        out_shape=(wide, wide, jax.ShapeDtypeStruct((STATES + 1, 8, 128), F32)),
        in_specs=[vmem] * 7 + [smem],
        out_specs=[vmem] * 3,
        scratch_shapes=[pltpu.VMEM((tokens + 8, channels), F32)],
        compiler_params=pltpu.CompilerParams(vmem_limit_bytes=32 << 20),
        name="scan_state",
    )(mixer_in, rim, dt_raw, dt_bias[None, :], conv_weight.T, conv_bias[None, :], rate, b_proj)
    enter = entering_state(final, rate)
    return pl.pallas_call(
        second_pass,
        out_shape=jax.ShapeDtypeStruct((tokens, channels), BF16),
        in_specs=[vmem] * 6 + [smem] * 2,
        out_specs=vmem,
        scratch_shapes=[pltpu.VMEM((tokens, 8, 128), F32)],
        compiler_params=pltpu.CompilerParams(vmem_limit_bytes=32 << 20),
        name="scan_output",
    )(step, act, gate_in, enter, rate, d_skip.reshape(8, 128), b_proj, c_proj)


def project_kernel(place_ref, *refs):
    rows, columns, out_ref = refs[:SIDE], refs[SIDE : 2 * SIDE], refs[2 * SIDE]
    y, z = place_ref[0], place_ref[1]
    for i in range(SIDE):
        far = lax.rem(y - i - z + 2 * SIDE, SIDE)
        for j in range(SIDE):
            out_ref[far, j] = jnp.dot(
                rows[j][...], columns[i][...], preferred_element_type=F32
            ).astype(BF16)


def project(mixed, w_out_blocks):
    rows = ring_gather(mixed, "x")
    place = jnp.stack([lax.axis_index("seq") // SIDE, lax.axis_index("exp") // 2]).astype(jnp.int32)
    vmem = pl.BlockSpec(memory_space=pltpu.VMEM)
    tokens, columns = mixed.shape[0], w_out_blocks[0].shape[1]
    partial = pl.pallas_call(
        project_kernel,
        out_shape=jax.ShapeDtypeStruct((SIDE, SIDE, tokens, columns), BF16),
        in_specs=[pl.BlockSpec(memory_space=pltpu.SMEM)] + [vmem] * (2 * SIDE),
        out_specs=vmem,
        compiler_params=pltpu.CompilerParams(vmem_limit_bytes=40 << 20),
        name="project",
    )(place, *rows, *w_out_blocks)
    total = partial.astype(F32) + keeper_shift(partial, "core", 0).astype(F32)
    near = total[0]
    for d in range(1, SIDE):
        near = near + keeper_shift(total[d].astype(BF16), "z", d).astype(F32)
    x, core = lax.axis_index("seq") % SIDE, lax.axis_index("exp") % 2
    near = near.astype(BF16)
    got = [jnp.where(core == x // 2, near[0], jnp.zeros_like(near[0]))]
    got += [keeper_shift(near[k], "x", -k) for k in range(1, SIDE)]
    even, odd = got[0] + got[2], got[1] + got[3]
    return jnp.concatenate(
        [jnp.where(x % 2 == 0, even, odd), jnp.where(x % 2 == 0, odd, even)], axis=1
    ).astype(F32)


def local(
    stream,
    mixer_in,
    gate_in,
    dt_raw,
    dt_bias,
    a_log,
    conv_weight,
    conv_bias,
    b_proj,
    c_proj,
    d_skip,
    w_out,
    expert_index,
    gate_weights,
    norm_gain,
    w_gate,
    w_up,
    w_down,
):
    tokens = mixer_in.shape[0]
    experts = lax.axis_size("exp")
    groups = lax.axis_size("seq")
    capacity = 3 * tokens // experts
    width = stream.shape[1]
    out_blocks = ring_gather(w_out, "y")
    mixed = mixer(
        mixer_in, gate_in, dt_raw, dt_bias, a_log, conv_weight, conv_bias, b_proj, c_proj, d_skip
    )
    projected = project(mixed, out_blocks)
    middle = (stream.astype(F32) + projected).astype(BF16)

    flat_exp = expert_index.reshape(-1)
    onehot = (flat_exp[:, None] == jnp.arange(experts, dtype=jnp.int32)[None, :]).astype(jnp.int32)
    ranks = jnp.cumsum(onehot, axis=0) - onehot
    slots = jnp.sum(ranks * onehot, axis=1)
    slot_id = (flat_exp * capacity + slots).reshape(tokens, 2)
    places = jnp.arange(experts * capacity, dtype=jnp.int32)
    chosen = (
        (slot_id[:, 0][None, :] == places[:, None]) | (slot_id[:, 1][None, :] == places[:, None])
    ).astype(BF16)
    outgoing = jnp.dot(chosen, middle, preferred_element_type=F32).astype(BF16)
    outgoing = outgoing.reshape(experts, capacity, width)
    arrived = lax.all_to_all(outgoing, "exp", split_axis=0, concat_axis=2, tiled=True)[0].astype(F32)
    mean_square = jnp.mean(arrived * arrived, axis=1, keepdims=True)
    normed = (arrived * lax.rsqrt(mean_square + 1e-05) * norm_gain[None, :]).astype(BF16)

    half = capacity // 2
    first = grid_gather(normed[:half], "xy")
    second = grid_gather(normed[half:], "yx")

    def feed(offsets):
        rows = jnp.stack([part[k] for part in (first, second) for k in offsets])
        flat = rows.reshape(-1, rows.shape[-1])
        gate_proj = jnp.dot(flat, w_gate[0], preferred_element_type=F32)
        up_proj = jnp.dot(flat, w_up[0], preferred_element_type=F32)
        hidden = lax.optimization_barrier((jax.nn.silu(gate_proj) * up_proj).astype(BF16))
        out = jnp.dot(hidden, w_down[0], preferred_element_type=F32).astype(BF16)
        return out.reshape((2, len(offsets)) + rows.shape[1:])

    fed = {}
    for offsets in ((0,), (1, 3), (2,)):
        out = feed(offsets)
        for at, k in enumerate(offsets):
            fed[k] = out[:, at]
    sums = []
    for which, order in ((0, "yx"), (1, "xy")):
        near = ring_scatter([fed[k][which] for k in range(SIDE)], order[0])
        sums.append(ring_scatter([near[k] for k in range(SIDE)], order[1]))
    summed = jnp.concatenate(sums, 0).astype(BF16)
    summed = summed.reshape(capacity, experts, width).transpose(1, 0, 2)
    returned = lax.all_to_all(summed, "exp", split_axis=0, concat_axis=0)
    returned = returned.reshape(experts * capacity, width)
    expert_sum = 0.0
    for k in range(2):
        pick = (slot_id[:, k][:, None] == places[None, :]).astype(BF16)
        picked = jnp.dot(pick, returned, preferred_element_type=F32)
        expert_sum = expert_sum + gate_weights[:, k][:, None] * picked
    return (middle.astype(F32) + expert_sum).astype(BF16)


def solution(mesh):
    return jax.shard_map(
        local,
        mesh=mesh,
        in_specs=(
            P("seq", "exp"),
            P("seq", "exp"),
            P("seq", "exp"),
            P("seq", "exp"),
            P("exp"),
            P("exp", None),
            P("exp", None),
            P("exp"),
            P("seq", None),
            P("seq", None),
            P("exp"),
            P("exp", "seq"),
            P("seq", None),
            P("seq", None),
            P(),
            P("exp", None, "seq"),
            P("exp", None, "seq"),
            P("exp", "seq", None),
        ),
        out_specs=P("seq", "exp"),
        check_vma=False,
    )
```

```python
import jax
import jax.numpy as jnp
from jax import lax
from jax.experimental import pallas as pl
from jax.experimental.pallas import tpu as pltpu
from jax.sharding import PartitionSpec as P

KCONV = 4
SIDE = 4
STATES = 16
LOG2E = 1.4426950408889634
F32 = jnp.float32
BF16 = jnp.bfloat16


def shift(value, axis, distance):
    cells = [(y, x) for y in range(SIDE) for x in range(SIDE)]
    if axis == "x":
        route = [(y * SIDE + x, y * SIDE + (x + distance) % SIDE) for y, x in cells]
    else:
        route = [(y * SIDE + x, (y + distance) % SIDE * SIDE + x) for y, x in cells]
    return lax.ppermute(value, "seq", route)


def partner(value):
    cells = range(SIDE * SIDE)
    return lax.ppermute(value, "seq", [(i, i ^ 1) for i in cells])


def ring_gather(block, axis):
    return [block] + [shift(block, axis, distance) for distance in range(1, SIDE)]


def grid_gather(block, order):
    near = jnp.stack(ring_gather(block, order[0]))
    return ring_gather(near, order[1])


def ring_scatter(blocks, axis):
    total = blocks[0].astype(F32)
    for k in (1, 3, 2):
        total = total + shift(blocks[k].astype(BF16), axis, -k).astype(F32)
    return total


def first_pass(x_ref, rim_ref, dt_ref, dtb_ref, cw_ref, cb_ref, rate_ref, b_ref,
               step_ref, act_ref, fin_ref, pad_ref):
    tokens, channels = x_ref.shape
    lanes = 128
    pad_ref[8 : 8 + tokens, :] = x_ref[...].astype(F32)
    pad_ref[0:8, :] = rim_ref[...].astype(F32)
    for k in range(channels // lanes):
        cols = slice(k * lanes, (k + 1) * lanes)
        total = cb_ref[:, cols]
        for tap in range(KCONV):
            low = 8 - (KCONV - 1) + tap
            total = total + cw_ref[tap : tap + 1, cols] * pad_ref[low : low + tokens, cols]
        act_ref[:, k, :] = total * jax.nn.sigmoid(total)
        raw = dt_ref[:, cols].astype(F32) + dtb_ref[:, cols]
        step_ref[:, k, :] = jnp.maximum(raw, 0.0) + jnp.log1p(jnp.exp(-jnp.abs(raw)))

    def advance(t, carry):
        states, summed = carry
        step = step_ref[t]
        source = step * act_ref[t]
        states = tuple(
            jnp.exp2(step * rate_ref[n]) * states[n] + b_ref[t, n] * source for n in range(STATES)
        )
        return states, summed + step

    zero = jnp.zeros((8, lanes), F32)
    states, summed = lax.fori_loop(0, tokens, advance, ((zero,) * STATES, zero), unroll=2)
    for n in range(STATES):
        fin_ref[n] = states[n]
    fin_ref[STATES] = summed


def second_pass(step_ref, act_ref, gate_ref, enter_ref, rate_ref, skip_ref, b_ref, c_ref,
                out_ref, y_ref):
    tokens, channels = gate_ref.shape
    lanes = 128
    skip = skip_ref[...]

    def advance(t, states):
        step = step_ref[t]
        act = act_ref[t]
        source = step * act
        sums = [skip * act, None]
        after = []
        for n in range(STATES):
            state = jnp.exp2(step * rate_ref[n]) * states[n] + b_ref[t, n] * source
            term = c_ref[t, n] * state
            sums[n % 2] = term if sums[n % 2] is None else sums[n % 2] + term
            after.append(state)
        y_ref[t] = sums[0] + sums[1]
        return tuple(after)

    lax.fori_loop(0, tokens, advance, tuple(enter_ref[n] for n in range(STATES)), unroll=2)
    for k in range(channels // lanes):
        cols = slice(k * lanes, (k + 1) * lanes)
        gate = gate_ref[:, cols].astype(F32)
        out_ref[:, cols] = (y_ref[:, k, :] * (gate * jax.nn.sigmoid(gate))).astype(BF16)


def entering_state(final, rate):
    along_x = lax.axis_index("seq") % SIDE
    along_y = lax.axis_index("seq") // SIDE

    def chain(earlier, latter):
        decay = jnp.exp2(rate * latter[1])
        return decay * earlier[0] + latter[0], earlier[1] + latter[1]

    def masked(pair, reached):
        return jnp.where(reached, pair[0], 0.0), jnp.where(reached, pair[1], 0.0)

    def split(packed):
        return packed[:STATES], packed[STATES]

    def spread(packed, axis, place):
        others = [split(shift(packed, axis, d)) for d in range(1, SIDE)]
        before = masked(others[2], place >= 3)
        for d in (2, 1):
            before = chain(before, masked(others[d - 1], place >= d))
        return before, others

    own = split(final)
    before_x, others = spread(final, "x", along_x)
    total = chain(before_x, own)
    for d in (3, 2, 1):
        total = chain(total, masked(others[d - 1], along_x < d))
    packed = jnp.concatenate([total[0], total[1][None]], 0)
    before_y, _ = spread(packed, "y", along_y)
    return chain(before_y, before_x)[0]


def mixer(mixer_in, gate_in, dt_raw, dt_bias, a_log, conv_weight, conv_bias, b_proj, c_proj, d_skip):
    tokens, channels = mixer_in.shape
    count, index = lax.axis_size("seq"), lax.axis_index("seq")
    rim = lax.ppermute(mixer_in[tokens - 8 :], "seq", [(i, i + 1) for i in range(count - 1)])
    rate = (-LOG2E * jnp.exp(a_log)).T.reshape(STATES, 8, 128)
    vmem = pl.BlockSpec(memory_space=pltpu.VMEM)
    smem = pl.BlockSpec(memory_space=pltpu.SMEM)
    wide = jax.ShapeDtypeStruct((tokens, 8, 128), F32)
    step, act, final = pl.pallas_call(
        first_pass,
        out_shape=(wide, wide, jax.ShapeDtypeStruct((STATES + 1, 8, 128), F32)),
        in_specs=[vmem] * 7 + [smem],
        out_specs=[vmem] * 3,
        scratch_shapes=[pltpu.VMEM((tokens + 8, channels), F32)],
        compiler_params=pltpu.CompilerParams(vmem_limit_bytes=32 << 20),
        name="scan_state",
    )(mixer_in, rim, dt_raw, dt_bias[None, :], conv_weight.T, conv_bias[None, :], rate, b_proj)
    enter = entering_state(final, rate)
    return pl.pallas_call(
        second_pass,
        out_shape=jax.ShapeDtypeStruct((tokens, channels), BF16),
        in_specs=[vmem] * 6 + [smem] * 2,
        out_specs=vmem,
        scratch_shapes=[pltpu.VMEM((tokens, 8, 128), F32)],
        compiler_params=pltpu.CompilerParams(vmem_limit_bytes=32 << 20),
        name="scan_output",
    )(step, act, gate_in, enter, rate, d_skip.reshape(8, 128), b_proj, c_proj)


def project_kernel(own_ref, other_ref, weight_ref, out_ref):
    for k, rows in enumerate((own_ref, other_ref)):
        out_ref[0, k] = jnp.dot(rows[...], weight_ref[0], preferred_element_type=F32).astype(BF16)


def project(mixed, weights):
    owners, channels, columns = weights.shape
    tokens = mixed.shape[0]
    whole = pl.BlockSpec((tokens, channels), lambda e: (0, 0))
    partial = pl.pallas_call(
        project_kernel,
        grid=(owners,),
        out_shape=jax.ShapeDtypeStruct((owners, 2, tokens, columns), BF16),
        in_specs=[whole, whole, pl.BlockSpec((1, channels, columns), lambda e: (e, 0, 0))],
        out_specs=pl.BlockSpec((1, 2, tokens, columns), lambda e: (e, 0, 0, 0)),
        name="project",
    )(mixed, partner(mixed), weights)
    partial = lax.all_to_all(partial, "exp", split_axis=0, concat_axis=0)
    total = jnp.sum(partial.astype(F32), axis=0)
    other = partner(total[1].astype(BF16)).astype(F32)
    is_even = lax.axis_index("seq") % 2 == 0
    return jnp.concatenate(
        [jnp.where(is_even, total[0], other), jnp.where(is_even, other, total[0])], axis=1
    )


def local(
    stream,
    mixer_in,
    gate_in,
    dt_raw,
    dt_bias,
    a_log,
    conv_weight,
    conv_bias,
    b_proj,
    c_proj,
    d_skip,
    w_out,
    expert_index,
    gate_weights,
    norm_gain,
    w_gate,
    w_up,
    w_down,
):
    tokens = mixer_in.shape[0]
    experts = lax.axis_size("exp")
    groups = lax.axis_size("seq")
    capacity = 3 * tokens // experts
    width = stream.shape[1]
    parity = [[i for i in range(groups) if i % 2 == p] for p in range(2)]
    out_blocks = lax.all_gather(w_out, "seq", axis=0, axis_index_groups=parity)
    mixed = mixer(
        mixer_in, gate_in, dt_raw, dt_bias, a_log, conv_weight, conv_bias, b_proj, c_proj, d_skip
    )
    projected = project(mixed, out_blocks)
    middle = (stream.astype(F32) + projected).astype(BF16)

    flat_exp = expert_index.reshape(-1)
    onehot = (flat_exp[:, None] == jnp.arange(experts, dtype=jnp.int32)[None, :]).astype(jnp.int32)
    ranks = jnp.cumsum(onehot, axis=0) - onehot
    slots = jnp.sum(ranks * onehot, axis=1)
    slot_id = (flat_exp * capacity + slots).reshape(tokens, 2)
    places = jnp.arange(experts * capacity, dtype=jnp.int32)
    chosen = (
        (slot_id[:, 0][None, :] == places[:, None]) | (slot_id[:, 1][None, :] == places[:, None])
    ).astype(BF16)
    outgoing = jnp.dot(chosen, middle, preferred_element_type=F32).astype(BF16)
    outgoing = outgoing.reshape(experts, capacity, width)
    arrived = lax.all_to_all(outgoing, "exp", split_axis=0, concat_axis=2, tiled=True)[0].astype(F32)
    mean_square = jnp.mean(arrived * arrived, axis=1, keepdims=True)
    normed = (arrived * lax.rsqrt(mean_square + 1e-05) * norm_gain[None, :]).astype(BF16)

    half = capacity // 2
    first = grid_gather(normed[:half], "xy")
    second = grid_gather(normed[half:], "yx")

    def feed(offsets):
        rows = jnp.stack([part[k] for part in (first, second) for k in offsets])
        flat = rows.reshape(-1, rows.shape[-1])
        gate_proj = jnp.dot(flat, w_gate[0], preferred_element_type=F32)
        up_proj = jnp.dot(flat, w_up[0], preferred_element_type=F32)
        hidden = lax.optimization_barrier((jax.nn.silu(gate_proj) * up_proj).astype(BF16))
        out = jnp.dot(hidden, w_down[0], preferred_element_type=F32).astype(BF16)
        return out.reshape((2, len(offsets)) + rows.shape[1:])

    fed = {}
    for offsets in ((0,), (1, 3), (2,)):
        out = feed(offsets)
        for at, k in enumerate(offsets):
            fed[k] = out[:, at]
    sums = []
    for which, order in ((0, "yx"), (1, "xy")):
        near = ring_scatter([fed[k][which] for k in range(SIDE)], order[0])
        sums.append(ring_scatter([near[k] for k in range(SIDE)], order[1]))
    summed = jnp.concatenate(sums, 0).astype(BF16)
    summed = summed.reshape(capacity, experts, width).transpose(1, 0, 2)
    returned = lax.all_to_all(summed, "exp", split_axis=0, concat_axis=0)
    returned = returned.reshape(experts * capacity, width)
    expert_sum = 0.0
    for k in range(2):
        pick = (slot_id[:, k][:, None] == places[None, :]).astype(BF16)
        picked = jnp.dot(pick, returned, preferred_element_type=F32)
        expert_sum = expert_sum + gate_weights[:, k][:, None] * picked
    return (middle.astype(F32) + expert_sum).astype(BF16)


def solution(mesh):
    return jax.shard_map(
        local,
        mesh=mesh,
        in_specs=(
            P("seq", "exp"),
            P("seq", "exp"),
            P("seq", "exp"),
            P("seq", "exp"),
            P("exp"),
            P("exp", None),
            P("exp", None),
            P("exp"),
            P("seq", None),
            P("seq", None),
            P("exp"),
            P("exp", "seq"),
            P("seq", None),
            P("seq", None),
            P(),
            P("exp", None, "seq"),
            P("exp", None, "seq"),
            P("exp", "seq", None),
        ),
        out_specs=P("seq", "exp"),
        check_vma=False,
    )
```

```python
import jax
import jax.numpy as jnp
from jax import lax
from jax.experimental import pallas as pl
from jax.experimental.pallas import tpu as pltpu
from jax.sharding import PartitionSpec as P

KCONV = 4
SIDE = 4
STATES = 16
LOG2E = 1.4426950408889634
F32 = jnp.float32
BF16 = jnp.bfloat16


def shift(value, axis, distance):
    cells = [(y, x) for y in range(SIDE) for x in range(SIDE)]
    if axis == "x":
        route = [(y * SIDE + x, y * SIDE + (x + distance) % SIDE) for y, x in cells]
    else:
        route = [(y * SIDE + x, (y + distance) % SIDE * SIDE + x) for y, x in cells]
    return lax.ppermute(value, "seq", route)


def partner(value):
    cells = range(SIDE * SIDE)
    return lax.ppermute(value, "seq", [(i, i ^ 1) for i in cells])


def ring_gather(block, axis):
    return [block] + [shift(block, axis, distance) for distance in range(1, SIDE)]


def grid_gather(block, order):
    near = jnp.stack(ring_gather(block, order[0]))
    return ring_gather(near, order[1])


def ring_scatter(blocks, axis):
    total = blocks[0].astype(F32)
    for k in (1, 3, 2):
        total = total + shift(blocks[k].astype(BF16), axis, -k).astype(F32)
    return total


def first_pass(x_ref, rim_ref, dt_ref, dtb_ref, cw_ref, cb_ref, rate_ref, b_ref,
               step_ref, act_ref, fin_ref, pad_ref):
    tokens, channels = x_ref.shape
    lanes = 128
    pad_ref[8 : 8 + tokens, :] = x_ref[...].astype(F32)
    pad_ref[0:8, :] = rim_ref[...].astype(F32)
    for k in range(channels // lanes):
        cols = slice(k * lanes, (k + 1) * lanes)
        total = cb_ref[:, cols]
        for tap in range(KCONV):
            low = 8 - (KCONV - 1) + tap
            total = total + cw_ref[tap : tap + 1, cols] * pad_ref[low : low + tokens, cols]
        act_ref[:, k, :] = total * jax.nn.sigmoid(total)
        raw = dt_ref[:, cols].astype(F32) + dtb_ref[:, cols]
        step_ref[:, k, :] = jnp.maximum(raw, 0.0) + jnp.log1p(jnp.exp(-jnp.abs(raw)))

    def advance(t, carry):
        states, summed = carry
        step = step_ref[t]
        source = step * act_ref[t]
        states = tuple(
            jnp.exp2(step * rate_ref[n]) * states[n] + b_ref[t, n] * source for n in range(STATES)
        )
        return states, summed + step

    zero = jnp.zeros((8, lanes), F32)
    states, summed = lax.fori_loop(0, tokens, advance, ((zero,) * STATES, zero), unroll=2)
    for n in range(STATES):
        fin_ref[n] = states[n]
    fin_ref[STATES] = summed


def second_pass(step_ref, act_ref, gate_ref, enter_ref, rate_ref, skip_ref, b_ref, c_ref,
                out_ref, y_ref):
    tokens, channels = gate_ref.shape
    lanes = 128
    skip = skip_ref[...]

    def advance(t, states):
        step = step_ref[t]
        act = act_ref[t]
        source = step * act
        sums = [skip * act, None]
        after = []
        for n in range(STATES):
            state = jnp.exp2(step * rate_ref[n]) * states[n] + b_ref[t, n] * source
            term = c_ref[t, n] * state
            sums[n % 2] = term if sums[n % 2] is None else sums[n % 2] + term
            after.append(state)
        y_ref[t] = sums[0] + sums[1]
        return tuple(after)

    lax.fori_loop(0, tokens, advance, tuple(enter_ref[n] for n in range(STATES)), unroll=2)
    for k in range(channels // lanes):
        cols = slice(k * lanes, (k + 1) * lanes)
        gate = gate_ref[:, cols].astype(F32)
        out_ref[:, cols] = (y_ref[:, k, :] * (gate * jax.nn.sigmoid(gate))).astype(BF16)


def entering_state(final, rate, ahead):
    along_x = lax.axis_index("seq") % SIDE
    along_y = lax.axis_index("seq") // SIDE

    def chain(earlier, latter):
        decay = jnp.exp2(rate * latter[1])
        return decay * earlier[0] + latter[0], earlier[1] + latter[1]

    def masked(pair, reached):
        return jnp.where(reached, pair[0], 0.0), jnp.where(reached, pair[1], 0.0)

    def split(packed):
        return packed[:STATES], packed[STATES]

    def spread(packed, axis, place):
        others = [split(shift(packed, axis, d)) for d in range(1, SIDE)]
        before = masked(others[2], place >= 3)
        for d in (2, 1):
            before = chain(before, masked(others[d - 1], place >= d))
        return before, others

    own = split(final)
    before_x, others = spread(final, "x", along_x)
    total = chain(before_x, own)
    for d in (3, 2, 1):
        total = chain(total, masked(others[d - 1], along_x < d))
    packed = jnp.concatenate([total[0], total[1][None]], 0)
    packed, ahead = lax.optimization_barrier((packed, ahead))
    before_y, _ = spread(packed, "y", along_y)
    return chain(before_y, before_x)[0], ahead


def mixer(
    mixer_in, gate_in, dt_raw, dt_bias, a_log, conv_weight, conv_bias, b_proj, c_proj, d_skip, w_out
):
    tokens, channels = mixer_in.shape
    count, index = lax.axis_size("seq"), lax.axis_index("seq")
    rim = lax.ppermute(mixer_in[tokens - 8 :], "seq", [(i, i + 1) for i in range(count - 1)])
    split = 3 * channels // 8
    low, high = w_out[:split], w_out[split:]
    low_pair = jnp.stack([low, shift(low, "x", 2)])
    dt_raw, low_pair = lax.optimization_barrier((dt_raw, low_pair))
    high_ring = ring_gather(high, "y")
    rate = (-LOG2E * jnp.exp(a_log)).T.reshape(STATES, 8, 128)
    vmem = pl.BlockSpec(memory_space=pltpu.VMEM)
    smem = pl.BlockSpec(memory_space=pltpu.SMEM)
    wide = jax.ShapeDtypeStruct((tokens, 8, 128), F32)
    step, act, final = pl.pallas_call(
        first_pass,
        out_shape=(wide, wide, jax.ShapeDtypeStruct((STATES + 1, 8, 128), F32)),
        in_specs=[vmem] * 7 + [smem],
        out_specs=[vmem] * 3,
        scratch_shapes=[pltpu.VMEM((tokens + 8, channels), F32)],
        compiler_params=pltpu.CompilerParams(vmem_limit_bytes=32 << 20),
        name="scan_state",
    )(mixer_in, rim, dt_raw, dt_bias[None, :], conv_weight.T, conv_bias[None, :], rate, b_proj)
    final, high_ring = lax.optimization_barrier((final, high_ring))
    first = ring_gather(low_pair, "y")
    high_ring = jnp.stack(high_ring)
    second = [high_ring, shift(high_ring, "x", 2)]
    enter, first = entering_state(final, rate, first)
    mixed = pl.pallas_call(
        second_pass,
        out_shape=jax.ShapeDtypeStruct((tokens, channels), BF16),
        in_specs=[vmem] * 6 + [smem] * 2,
        out_specs=vmem,
        scratch_shapes=[pltpu.VMEM((tokens, 8, 128), F32)],
        compiler_params=pltpu.CompilerParams(vmem_limit_bytes=32 << 20),
        name="scan_output",
    )(step, act, gate_in, enter, rate, d_skip.reshape(8, 128), b_proj, c_proj)
    return mixed, (first, second)


def project_kernel(place_ref, own_ref, other_ref, *refs):
    first, second, out_ref = refs[:SIDE], refs[SIDE : SIDE + 2], refs[SIDE + 2]
    split = first[0].shape[1]
    y, side = place_ref[0], place_ref[1]
    for i in range(SIDE):
        for j in range(2):
            owner = lax.rem(y - i + SIDE, SIDE) * 2 + lax.rem(side + j, 2)
            for k, rows in enumerate((own_ref, other_ref)):
                total = jnp.dot(rows[:, :split], first[i][j], preferred_element_type=F32)
                total += jnp.dot(rows[:, split:], second[j][i], preferred_element_type=F32)
                out_ref[owner, k] = total.astype(BF16)


def project(mixed, weights):
    first, second = weights
    tokens, columns = mixed.shape[0], first[0].shape[2]
    index = lax.axis_index("seq")
    place = jnp.stack([index // SIDE, index % SIDE // 2]).astype(jnp.int32)
    vmem = pl.BlockSpec(memory_space=pltpu.VMEM)
    partial = pl.pallas_call(
        project_kernel,
        out_shape=jax.ShapeDtypeStruct((2 * SIDE, 2, tokens, columns), BF16),
        in_specs=[pl.BlockSpec(memory_space=pltpu.SMEM)] + [vmem] * (SIDE + 4),
        out_specs=vmem,
        compiler_params=pltpu.CompilerParams(vmem_limit_bytes=40 << 20),
        name="project",
    )(place, mixed, partner(mixed), *first, *second)
    partial = lax.all_to_all(partial, "exp", split_axis=0, concat_axis=0)
    total = jnp.sum(partial.astype(F32), axis=0)
    other = partner(total[1].astype(BF16)).astype(F32)
    is_even = lax.axis_index("seq") % 2 == 0
    return jnp.concatenate(
        [jnp.where(is_even, total[0], other), jnp.where(is_even, other, total[0])], axis=1
    )


def local(
    stream,
    mixer_in,
    gate_in,
    dt_raw,
    dt_bias,
    a_log,
    conv_weight,
    conv_bias,
    b_proj,
    c_proj,
    d_skip,
    w_out,
    expert_index,
    gate_weights,
    norm_gain,
    w_gate,
    w_up,
    w_down,
):
    tokens = mixer_in.shape[0]
    experts = lax.axis_size("exp")
    groups = lax.axis_size("seq")
    capacity = 3 * tokens // experts
    width = stream.shape[1]
    mixed, weights = mixer(
        mixer_in, gate_in, dt_raw, dt_bias, a_log, conv_weight, conv_bias, b_proj, c_proj, d_skip, w_out
    )
    projected = project(mixed, weights)
    middle = (stream.astype(F32) + projected).astype(BF16)

    flat_exp = expert_index.reshape(-1)
    onehot = (flat_exp[:, None] == jnp.arange(experts, dtype=jnp.int32)[None, :]).astype(jnp.int32)
    ranks = jnp.cumsum(onehot, axis=0) - onehot
    slots = jnp.sum(ranks * onehot, axis=1)
    slot_id = (flat_exp * capacity + slots).reshape(tokens, 2)
    places = jnp.arange(experts * capacity, dtype=jnp.int32)
    chosen = (
        (slot_id[:, 0][None, :] == places[:, None]) | (slot_id[:, 1][None, :] == places[:, None])
    ).astype(BF16)
    outgoing = jnp.dot(chosen, middle, preferred_element_type=F32).astype(BF16)
    outgoing = outgoing.reshape(experts, capacity, width)
    arrived = lax.all_to_all(outgoing, "exp", split_axis=0, concat_axis=2, tiled=True)[0].astype(F32)
    mean_square = jnp.mean(arrived * arrived, axis=1, keepdims=True)
    normed = (arrived * lax.rsqrt(mean_square + 1e-05) * norm_gain[None, :]).astype(BF16)

    half = capacity // 2
    first = grid_gather(normed[:half], "xy")
    second = grid_gather(normed[half:], "yx")

    def feed(offsets):
        rows = jnp.stack([part[k] for part in (first, second) for k in offsets])
        flat = rows.reshape(-1, rows.shape[-1])
        gate_proj = jnp.dot(flat, w_gate[0], preferred_element_type=F32)
        up_proj = jnp.dot(flat, w_up[0], preferred_element_type=F32)
        hidden = lax.optimization_barrier((jax.nn.silu(gate_proj) * up_proj).astype(BF16))
        out = jnp.dot(hidden, w_down[0], preferred_element_type=F32).astype(BF16)
        return out.reshape((2, len(offsets)) + rows.shape[1:])

    fed = {}
    for offsets in ((0,), (1, 3), (2,)):
        out = feed(offsets)
        for at, k in enumerate(offsets):
            fed[k] = out[:, at]
    sums = []
    for which, order in ((0, "yx"), (1, "xy")):
        near = ring_scatter([fed[k][which] for k in range(SIDE)], order[0])
        sums.append(ring_scatter([near[k] for k in range(SIDE)], order[1]))
    summed = jnp.concatenate(sums, 0).astype(BF16)
    summed = summed.reshape(capacity, experts, width).transpose(1, 0, 2)
    returned = lax.all_to_all(summed, "exp", split_axis=0, concat_axis=0)
    returned = returned.reshape(experts * capacity, width)
    expert_sum = 0.0
    for k in range(2):
        pick = (slot_id[:, k][:, None] == places[None, :]).astype(BF16)
        picked = jnp.dot(pick, returned, preferred_element_type=F32)
        expert_sum = expert_sum + gate_weights[:, k][:, None] * picked
    return (middle.astype(F32) + expert_sum).astype(BF16)


def solution(mesh):
    return jax.shard_map(
        local,
        mesh=mesh,
        in_specs=(
            P("seq", "exp"),
            P("seq", "exp"),
            P("seq", "exp"),
            P("seq", "exp"),
            P("exp"),
            P("exp", None),
            P("exp", None),
            P("exp"),
            P("seq", None),
            P("seq", None),
            P("exp"),
            P("exp", "seq"),
            P("seq", None),
            P("seq", None),
            P(),
            P("exp", None, "seq"),
            P("exp", None, "seq"),
            P("exp", "seq", None),
        ),
        out_specs=P("seq", "exp"),
        check_vma=False,
    )
```

```python
import jax
import jax.numpy as jnp
from jax import lax
from jax.experimental import pallas as pl
from jax.experimental.pallas import tpu as pltpu
from jax.sharding import PartitionSpec as P

KCONV = 4
SIDE = 4
STATES = 16
LOG2E = 1.4426950408889634
F32 = jnp.float32
BF16 = jnp.bfloat16


def shift(value, axis, distance):
    cells = [(y, x) for y in range(SIDE) for x in range(SIDE)]
    if axis == "x":
        route = [(y * SIDE + x, y * SIDE + (x + distance) % SIDE) for y, x in cells]
    else:
        route = [(y * SIDE + x, (y + distance) % SIDE * SIDE + x) for y, x in cells]
    return lax.ppermute(value, "seq", route)


def partner(value):
    cells = range(SIDE * SIDE)
    return lax.ppermute(value, "seq", [(i, i ^ 1) for i in cells])


def ring_gather(block, axis):
    return [block] + [shift(block, axis, distance) for distance in range(1, SIDE)]


def grid_gather(block, order):
    near = jnp.stack(ring_gather(block, order[0]))
    return ring_gather(near, order[1])


def ring_scatter(blocks, axis):
    total = blocks[0].astype(F32)
    for k in (1, 3, 2):
        total = total + shift(blocks[k].astype(BF16), axis, -k).astype(F32)
    return total


def first_pass(x_ref, rim_ref, dt_ref, dtb_ref, cw_ref, cb_ref, rate_ref, b_ref,
               step_ref, act_ref, fin_ref, pad_ref):
    tokens, channels = x_ref.shape
    lanes = 128
    pad_ref[8 : 8 + tokens, :] = x_ref[...].astype(F32)
    pad_ref[0:8, :] = rim_ref[...].astype(F32)
    for k in range(channels // lanes):
        cols = slice(k * lanes, (k + 1) * lanes)
        total = cb_ref[:, cols]
        for tap in range(KCONV):
            low = 8 - (KCONV - 1) + tap
            total = total + cw_ref[tap : tap + 1, cols] * pad_ref[low : low + tokens, cols]
        act_ref[:, k, :] = total * jax.nn.sigmoid(total)
        raw = dt_ref[:, cols].astype(F32) + dtb_ref[:, cols]
        step_ref[:, k, :] = jnp.maximum(raw, 0.0) + jnp.log1p(jnp.exp(-jnp.abs(raw)))

    def advance(t, carry):
        states, summed = carry
        step = step_ref[t]
        source = step * act_ref[t]
        states = tuple(
            jnp.exp2(step * rate_ref[n]) * states[n] + b_ref[t, n] * source for n in range(STATES)
        )
        return states, summed + step

    zero = jnp.zeros((8, lanes), F32)
    states, summed = lax.fori_loop(0, tokens, advance, ((zero,) * STATES, zero), unroll=2)
    for n in range(STATES):
        fin_ref[n] = states[n]
    fin_ref[STATES] = summed


def second_pass(step_ref, act_ref, gate_ref, enter_ref, rate_ref, skip_ref, b_ref, c_ref,
                out_ref, y_ref):
    tokens, channels = gate_ref.shape
    lanes = 128
    skip = skip_ref[...]

    def advance(t, states):
        step = step_ref[t]
        act = act_ref[t]
        source = step * act
        sums = [skip * act, None]
        after = []
        for n in range(STATES):
            state = jnp.exp2(step * rate_ref[n]) * states[n] + b_ref[t, n] * source
            term = c_ref[t, n] * state
            sums[n % 2] = term if sums[n % 2] is None else sums[n % 2] + term
            after.append(state)
        y_ref[t] = sums[0] + sums[1]
        return tuple(after)

    lax.fori_loop(0, tokens, advance, tuple(enter_ref[n] for n in range(STATES)), unroll=2)
    for k in range(channels // lanes):
        cols = slice(k * lanes, (k + 1) * lanes)
        gate = gate_ref[:, cols].astype(F32)
        out_ref[:, cols] = (y_ref[:, k, :] * (gate * jax.nn.sigmoid(gate))).astype(BF16)


def entering_state(final, rate, ahead, after):
    along_x = lax.axis_index("seq") % SIDE
    along_y = lax.axis_index("seq") // SIDE

    def chain(earlier, latter):
        decay = jnp.exp2(rate * latter[1])
        return decay * earlier[0] + latter[0], earlier[1] + latter[1]

    def masked(pair, reached):
        return jnp.where(reached, pair[0], 0.0), jnp.where(reached, pair[1], 0.0)

    def split(packed):
        return packed[:STATES], packed[STATES]

    def spread(packed, axis, place):
        others = [split(shift(packed, axis, d)) for d in range(1, SIDE)]
        before = masked(others[2], place >= 3)
        for d in (2, 1):
            before = chain(before, masked(others[d - 1], place >= d))
        return before, others

    own = split(final)
    before_x, others = spread(final, "x", along_x)
    total = chain(before_x, own)
    for d in (3, 2, 1):
        total = chain(total, masked(others[d - 1], along_x < d))
    packed = jnp.concatenate([total[0], total[1][None]], 0)
    packed, after = lax.optimization_barrier((packed, after))
    far = shift(after, "x", 2)
    packed, ahead = lax.optimization_barrier((packed, ahead))
    before_y, _ = spread(packed, "y", along_y)
    return chain(before_y, before_x)[0], ahead, [after, far]


def mixer(
    mixer_in, gate_in, dt_raw, dt_bias, a_log, conv_weight, conv_bias, b_proj, c_proj, d_skip, w_out
):
    tokens, channels = mixer_in.shape
    count, index = lax.axis_size("seq"), lax.axis_index("seq")
    rim = lax.ppermute(mixer_in[tokens - 8 :], "seq", [(i, i + 1) for i in range(count - 1)])
    split = 7 * channels // 16
    low, high = w_out[:split], w_out[split:]
    low_pair = jnp.stack([low, shift(low, "x", 2)])
    dt_raw, low_pair = lax.optimization_barrier((dt_raw, low_pair))
    high_ring = ring_gather(high, "y")
    rate = (-LOG2E * jnp.exp(a_log)).T.reshape(STATES, 8, 128)
    vmem = pl.BlockSpec(memory_space=pltpu.VMEM)
    smem = pl.BlockSpec(memory_space=pltpu.SMEM)
    wide = jax.ShapeDtypeStruct((tokens, 8, 128), F32)
    step, act, final = pl.pallas_call(
        first_pass,
        out_shape=(wide, wide, jax.ShapeDtypeStruct((STATES + 1, 8, 128), F32)),
        in_specs=[vmem] * 7 + [smem],
        out_specs=[vmem] * 3,
        scratch_shapes=[pltpu.VMEM((tokens + 8, channels), F32)],
        compiler_params=pltpu.CompilerParams(vmem_limit_bytes=32 << 20),
        name="scan_state",
    )(mixer_in, rim, dt_raw, dt_bias[None, :], conv_weight.T, conv_bias[None, :], rate, b_proj)
    final, high_ring = lax.optimization_barrier((final, high_ring))
    first = ring_gather(low_pair, "y")
    high_ring = jnp.stack(high_ring)
    enter, first, second = entering_state(final, rate, first, high_ring)
    mixed = pl.pallas_call(
        second_pass,
        out_shape=jax.ShapeDtypeStruct((tokens, channels), BF16),
        in_specs=[vmem] * 6 + [smem] * 2,
        out_specs=vmem,
        scratch_shapes=[pltpu.VMEM((tokens, 8, 128), F32)],
        compiler_params=pltpu.CompilerParams(vmem_limit_bytes=32 << 20),
        name="scan_output",
    )(step, act, gate_in, enter, rate, d_skip.reshape(8, 128), b_proj, c_proj)
    return mixed, (first, second)


def project_kernel(place_ref, own_ref, other_ref, *refs):
    first, second, out_ref, rows = refs[:SIDE], refs[SIDE : SIDE + 2], refs[SIDE + 2], refs[SIDE + 3]
    tokens = own_ref.shape[0]
    rows[:tokens] = own_ref[...]
    rows[tokens:] = other_ref[...]
    split = first[0].shape[1]
    y, side = place_ref[0], place_ref[1]
    for i in range(SIDE):
        for j in range(2):
            owner = lax.rem(y - i + SIDE, SIDE) * 2 + lax.rem(side + j, 2)
            total = jnp.dot(rows[:, :split], first[i][j], preferred_element_type=F32)
            total += jnp.dot(rows[:, split:], second[j][i], preferred_element_type=F32)
            total = total.astype(BF16)
            out_ref[owner, 0] = total[:tokens]
            out_ref[owner, 1] = total[tokens:]


def project(mixed, weights):
    first, second = weights
    tokens, columns = mixed.shape[0], first[0].shape[2]
    index = lax.axis_index("seq")
    place = jnp.stack([index // SIDE, index % SIDE // 2]).astype(jnp.int32)
    vmem = pl.BlockSpec(memory_space=pltpu.VMEM)
    partial = pl.pallas_call(
        project_kernel,
        out_shape=jax.ShapeDtypeStruct((2 * SIDE, 2, tokens, columns), BF16),
        in_specs=[pl.BlockSpec(memory_space=pltpu.SMEM)] + [vmem] * (SIDE + 4),
        out_specs=vmem,
        scratch_shapes=[pltpu.VMEM((2 * tokens, mixed.shape[1]), BF16)],
        compiler_params=pltpu.CompilerParams(vmem_limit_bytes=40 << 20),
        name="project",
    )(place, mixed, partner(mixed), *first, *second)
    partial = lax.all_to_all(partial, "exp", split_axis=0, concat_axis=0)
    total = jnp.sum(partial.astype(F32), axis=0)
    other = partner(total[1].astype(BF16)).astype(F32)
    is_even = lax.axis_index("seq") % 2 == 0
    return jnp.concatenate(
        [jnp.where(is_even, total[0], other), jnp.where(is_even, other, total[0])], axis=1
    )


def local(
    stream,
    mixer_in,
    gate_in,
    dt_raw,
    dt_bias,
    a_log,
    conv_weight,
    conv_bias,
    b_proj,
    c_proj,
    d_skip,
    w_out,
    expert_index,
    gate_weights,
    norm_gain,
    w_gate,
    w_up,
    w_down,
):
    tokens = mixer_in.shape[0]
    experts = lax.axis_size("exp")
    groups = lax.axis_size("seq")
    capacity = 3 * tokens // experts
    width = stream.shape[1]
    mixed, weights = mixer(
        mixer_in, gate_in, dt_raw, dt_bias, a_log, conv_weight, conv_bias, b_proj, c_proj, d_skip, w_out
    )
    projected = project(mixed, weights)
    middle = (stream.astype(F32) + projected).astype(BF16)

    flat_exp = expert_index.reshape(-1)
    onehot = (flat_exp[:, None] == jnp.arange(experts, dtype=jnp.int32)[None, :]).astype(jnp.int32)
    ranks = jnp.cumsum(onehot, axis=0) - onehot
    slots = jnp.sum(ranks * onehot, axis=1)
    slot_id = (flat_exp * capacity + slots).reshape(tokens, 2)
    places = jnp.arange(experts * capacity, dtype=jnp.int32)
    chosen = (
        (slot_id[:, 0][None, :] == places[:, None]) | (slot_id[:, 1][None, :] == places[:, None])
    ).astype(BF16)
    outgoing = jnp.dot(chosen, middle, preferred_element_type=F32).astype(BF16)
    outgoing = outgoing.reshape(experts, capacity, width)
    arrived = lax.all_to_all(outgoing, "exp", split_axis=0, concat_axis=2, tiled=True)[0].astype(F32)
    mean_square = jnp.mean(arrived * arrived, axis=1, keepdims=True)
    normed = (arrived * lax.rsqrt(mean_square + 1e-05) * norm_gain[None, :]).astype(BF16)

    half = capacity // 2
    first = grid_gather(normed[:half], "xy")
    second = grid_gather(normed[half:], "yx")

    def feed(offsets):
        rows = jnp.stack([part[k] for part in (first, second) for k in offsets])
        flat = rows.reshape(-1, rows.shape[-1])
        gate_proj = jnp.dot(flat, w_gate[0], preferred_element_type=F32)
        up_proj = jnp.dot(flat, w_up[0], preferred_element_type=F32)
        hidden = lax.optimization_barrier((jax.nn.silu(gate_proj) * up_proj).astype(BF16))
        out = jnp.dot(hidden, w_down[0], preferred_element_type=F32).astype(BF16)
        return out.reshape((2, len(offsets)) + rows.shape[1:])

    fed = {}
    for offsets in ((0,), (1, 3), (2,)):
        out = feed(offsets)
        for at, k in enumerate(offsets):
            fed[k] = out[:, at]
    sums = []
    for which, order in ((0, "yx"), (1, "xy")):
        near = ring_scatter([fed[k][which] for k in range(SIDE)], order[0])
        sums.append(ring_scatter([near[k] for k in range(SIDE)], order[1]))
    summed = jnp.concatenate(sums, 0).astype(BF16)
    summed = summed.reshape(capacity, experts, width).transpose(1, 0, 2)
    returned = lax.all_to_all(summed, "exp", split_axis=0, concat_axis=0)
    returned = returned.reshape(experts * capacity, width)
    expert_sum = 0.0
    for k in range(2):
        pick = (slot_id[:, k][:, None] == places[None, :]).astype(BF16)
        picked = jnp.dot(pick, returned, preferred_element_type=F32)
        expert_sum = expert_sum + gate_weights[:, k][:, None] * picked
    return (middle.astype(F32) + expert_sum).astype(BF16)


def solution(mesh):
    return jax.shard_map(
        local,
        mesh=mesh,
        in_specs=(
            P("seq", "exp"),
            P("seq", "exp"),
            P("seq", "exp"),
            P("seq", "exp"),
            P("exp"),
            P("exp", None),
            P("exp", None),
            P("exp"),
            P("seq", None),
            P("seq", None),
            P("exp"),
            P("exp", "seq"),
            P("seq", None),
            P("seq", None),
            P(),
            P("exp", None, "seq"),
            P("exp", None, "seq"),
            P("exp", "seq", None),
        ),
        out_specs=P("seq", "exp"),
        check_vma=False,
    )
```

```python
import jax
import jax.numpy as jnp
from jax import lax
from jax.experimental import pallas as pl
from jax.experimental.pallas import tpu as pltpu
from jax.sharding import PartitionSpec as P

KCONV = 4
SIDE = 4
STATES = 16
LOG2E = 1.4426950408889634
F32 = jnp.float32
BF16 = jnp.bfloat16


def shift(value, axis, distance):
    cells = [(y, x) for y in range(SIDE) for x in range(SIDE)]
    if axis == "x":
        route = [(y * SIDE + x, y * SIDE + (x + distance) % SIDE) for y, x in cells]
    else:
        route = [(y * SIDE + x, (y + distance) % SIDE * SIDE + x) for y, x in cells]
    return lax.ppermute(value, "seq", route)


def partner(value):
    cells = range(SIDE * SIDE)
    return lax.ppermute(value, "seq", [(i, i ^ 1) for i in cells])


def ring_gather(block, axis):
    return [block] + [shift(block, axis, distance) for distance in range(1, SIDE)]


def relay_gather(blocks, axis):
    half = blocks.shape[0] // 2
    before = shift(blocks, axis, 1)
    after = shift(blocks, axis, -1)
    far = [shift(before[:half], axis, 1), shift(after[half:], axis, -1)]
    return [blocks, before, jnp.concatenate(far), after]


def grid_gather(block, order):
    near = jnp.stack(ring_gather(block, order[0]))
    return relay_gather(near, order[1])


def ring_scatter(blocks, axis):
    total = blocks[0].astype(F32)
    for k in (1, 3, 2):
        total = total + shift(blocks[k].astype(BF16), axis, -k).astype(F32)
    return total


def first_pass(x_ref, rim_ref, dt_ref, dtb_ref, cw_ref, cb_ref, rate_ref, b_ref,
               step_ref, act_ref, fin_ref, pad_ref):
    tokens, channels = x_ref.shape
    lanes = 128
    pad_ref[8 : 8 + tokens, :] = x_ref[...].astype(F32)
    pad_ref[0:8, :] = rim_ref[...].astype(F32)
    for k in range(channels // lanes):
        cols = slice(k * lanes, (k + 1) * lanes)
        total = cb_ref[:, cols]
        for tap in range(KCONV):
            low = 8 - (KCONV - 1) + tap
            total = total + cw_ref[tap : tap + 1, cols] * pad_ref[low : low + tokens, cols]
        act_ref[:, k, :] = total * jax.nn.sigmoid(total)
        raw = dt_ref[:, cols].astype(F32) + dtb_ref[:, cols]
        step_ref[:, k, :] = jnp.maximum(raw, 0.0) + jnp.log1p(jnp.exp(-jnp.abs(raw)))

    def advance(t, carry):
        states, summed = carry
        step = step_ref[t]
        source = step * act_ref[t]
        states = tuple(
            jnp.exp2(step * rate_ref[n]) * states[n] + b_ref[t, n] * source for n in range(STATES)
        )
        return states, summed + step

    zero = jnp.zeros((8, lanes), F32)
    states, summed = lax.fori_loop(0, tokens, advance, ((zero,) * STATES, zero), unroll=2)
    for n in range(STATES):
        fin_ref[n] = states[n]
    fin_ref[STATES] = summed


def second_pass(step_ref, act_ref, gate_ref, enter_ref, rate_ref, skip_ref, b_ref, c_ref,
                out_ref, y_ref):
    tokens, channels = gate_ref.shape
    lanes = 128
    skip = skip_ref[...]

    def advance(t, states):
        step = step_ref[t]
        act = act_ref[t]
        source = step * act
        sums = [skip * act, None]
        after = []
        for n in range(STATES):
            state = jnp.exp2(step * rate_ref[n]) * states[n] + b_ref[t, n] * source
            term = c_ref[t, n] * state
            sums[n % 2] = term if sums[n % 2] is None else sums[n % 2] + term
            after.append(state)
        y_ref[t] = sums[0] + sums[1]
        return tuple(after)

    lax.fori_loop(0, tokens, advance, tuple(enter_ref[n] for n in range(STATES)), unroll=2)
    for k in range(channels // lanes):
        cols = slice(k * lanes, (k + 1) * lanes)
        gate = gate_ref[:, cols].astype(F32)
        out_ref[:, cols] = (y_ref[:, k, :] * (gate * jax.nn.sigmoid(gate))).astype(BF16)


def entering_state(final, rate, ahead, after):
    along_x = lax.axis_index("seq") % SIDE
    along_y = lax.axis_index("seq") // SIDE

    def chain(earlier, latter):
        decay = jnp.exp2(rate * latter[1])
        return decay * earlier[0] + latter[0], earlier[1] + latter[1]

    def masked(pair, reached):
        return jnp.where(reached, pair[0], 0.0), jnp.where(reached, pair[1], 0.0)

    def split(packed):
        return packed[:STATES], packed[STATES]

    def spread(packed, axis, place):
        others = [split(shift(packed, axis, d)) for d in range(1, SIDE)]
        before = masked(others[2], place >= 3)
        for d in (2, 1):
            before = chain(before, masked(others[d - 1], place >= d))
        return before, others

    own = split(final)
    before_x, others = spread(final, "x", along_x)
    total = chain(before_x, own)
    for d in (3, 2, 1):
        total = chain(total, masked(others[d - 1], along_x < d))
    packed = jnp.concatenate([total[0], total[1][None]], 0)
    packed, after = lax.optimization_barrier((packed, after))
    far = shift(after, "x", 2)
    packed, ahead = lax.optimization_barrier((packed, ahead))
    before_y, _ = spread(packed, "y", along_y)
    return chain(before_y, before_x)[0], ahead, [after, far]


def mixer(
    mixer_in, gate_in, dt_raw, dt_bias, a_log, conv_weight, conv_bias, b_proj, c_proj, d_skip, w_out
):
    tokens, channels = mixer_in.shape
    count, index = lax.axis_size("seq"), lax.axis_index("seq")
    rim = lax.ppermute(mixer_in[tokens - 8 :], "seq", [(i, i + 1) for i in range(count - 1)])
    rim, w_out = lax.optimization_barrier((rim, w_out))
    split = 3 * channels // 8
    low, high = w_out[:split], w_out[split:]
    low_pair = jnp.stack([low, shift(low, "x", 2)])
    dt_raw, low_pair = lax.optimization_barrier((dt_raw, low_pair))
    high_ring = ring_gather(high, "y")
    rate = (-LOG2E * jnp.exp(a_log)).T.reshape(STATES, 8, 128)
    vmem = pl.BlockSpec(memory_space=pltpu.VMEM)
    smem = pl.BlockSpec(memory_space=pltpu.SMEM)
    wide = jax.ShapeDtypeStruct((tokens, 8, 128), F32)
    step, act, final = pl.pallas_call(
        first_pass,
        out_shape=(wide, wide, jax.ShapeDtypeStruct((STATES + 1, 8, 128), F32)),
        in_specs=[vmem] * 7 + [smem],
        out_specs=[vmem] * 3,
        scratch_shapes=[pltpu.VMEM((tokens + 8, channels), F32)],
        compiler_params=pltpu.CompilerParams(vmem_limit_bytes=32 << 20),
        name="scan_state",
    )(mixer_in, rim, dt_raw, dt_bias[None, :], conv_weight.T, conv_bias[None, :], rate, b_proj)
    final, high_ring = lax.optimization_barrier((final, high_ring))
    first = ring_gather(low_pair, "y")
    high_ring = jnp.stack(high_ring)
    enter, first, second = entering_state(final, rate, first, high_ring)
    mixed = pl.pallas_call(
        second_pass,
        out_shape=jax.ShapeDtypeStruct((tokens, channels), BF16),
        in_specs=[vmem] * 6 + [smem] * 2,
        out_specs=vmem,
        scratch_shapes=[pltpu.VMEM((tokens, 8, 128), F32)],
        compiler_params=pltpu.CompilerParams(vmem_limit_bytes=32 << 20),
        name="scan_output",
    )(step, act, gate_in, enter, rate, d_skip.reshape(8, 128), b_proj, c_proj)
    return mixed, (first, second)


def project_kernel(place_ref, own_ref, other_ref, *refs):
    first, second, out_ref, rows = refs[:SIDE], refs[SIDE : SIDE + 2], refs[SIDE + 2], refs[SIDE + 3]
    tokens = own_ref.shape[0]
    rows[:tokens] = own_ref[...]
    rows[tokens:] = other_ref[...]
    split = first[0].shape[1]
    y, side = place_ref[0], place_ref[1]
    for i in range(SIDE):
        for j in range(2):
            owner = lax.rem(y - i + SIDE, SIDE) * 2 + lax.rem(side + j, 2)
            total = jnp.dot(rows[:, :split], first[i][j], preferred_element_type=F32)
            total += jnp.dot(rows[:, split:], second[j][i], preferred_element_type=F32)
            total = total.astype(BF16)
            out_ref[owner, 0] = total[:tokens]
            out_ref[owner, 1] = total[tokens:]


def project(mixed, weights):
    first, second = weights
    tokens, columns = mixed.shape[0], first[0].shape[2]
    index = lax.axis_index("seq")
    place = jnp.stack([index // SIDE, index % SIDE // 2]).astype(jnp.int32)
    vmem = pl.BlockSpec(memory_space=pltpu.VMEM)
    partial = pl.pallas_call(
        project_kernel,
        out_shape=jax.ShapeDtypeStruct((2 * SIDE, 2, tokens, columns), BF16),
        in_specs=[pl.BlockSpec(memory_space=pltpu.SMEM)] + [vmem] * (SIDE + 4),
        out_specs=vmem,
        scratch_shapes=[pltpu.VMEM((2 * tokens, mixed.shape[1]), BF16)],
        compiler_params=pltpu.CompilerParams(vmem_limit_bytes=40 << 20),
        name="project",
    )(place, mixed, partner(mixed), *first, *second)
    partial = lax.all_to_all(partial, "exp", split_axis=0, concat_axis=0)
    total = jnp.sum(partial.astype(F32), axis=0)
    other = partner(total[1].astype(BF16)).astype(F32)
    is_even = lax.axis_index("seq") % 2 == 0
    return jnp.concatenate(
        [jnp.where(is_even, total[0], other), jnp.where(is_even, other, total[0])], axis=1
    )


def local(
    stream,
    mixer_in,
    gate_in,
    dt_raw,
    dt_bias,
    a_log,
    conv_weight,
    conv_bias,
    b_proj,
    c_proj,
    d_skip,
    w_out,
    expert_index,
    gate_weights,
    norm_gain,
    w_gate,
    w_up,
    w_down,
):
    tokens = mixer_in.shape[0]
    experts = lax.axis_size("exp")
    groups = lax.axis_size("seq")
    capacity = 3 * tokens // experts
    width = stream.shape[1]
    mixed, weights = mixer(
        mixer_in, gate_in, dt_raw, dt_bias, a_log, conv_weight, conv_bias, b_proj, c_proj, d_skip, w_out
    )
    projected = project(mixed, weights)
    middle = (stream.astype(F32) + projected).astype(BF16)

    flat_exp = expert_index.reshape(-1)
    onehot = (flat_exp[:, None] == jnp.arange(experts, dtype=jnp.int32)[None, :]).astype(jnp.int32)
    ranks = jnp.cumsum(onehot, axis=0) - onehot
    slots = jnp.sum(ranks * onehot, axis=1)
    slot_id = (flat_exp * capacity + slots).reshape(tokens, 2)
    places = jnp.arange(experts * capacity, dtype=jnp.int32)
    chosen = (
        (slot_id[:, 0][None, :] == places[:, None]) | (slot_id[:, 1][None, :] == places[:, None])
    ).astype(BF16)
    outgoing = jnp.dot(chosen, middle, preferred_element_type=F32).astype(BF16)
    outgoing = outgoing.reshape(experts, capacity, width)
    arrived = lax.all_to_all(outgoing, "exp", split_axis=0, concat_axis=2, tiled=True)[0].astype(F32)
    mean_square = jnp.mean(arrived * arrived, axis=1, keepdims=True)
    normed = (arrived * lax.rsqrt(mean_square + 1e-05) * norm_gain[None, :]).astype(BF16)

    half = capacity // 2
    first = grid_gather(normed[:half], "xy")
    second = grid_gather(normed[half:], "yx")

    def feed(offsets):
        rows = jnp.stack([part[k] for part in (first, second) for k in offsets])
        flat = rows.reshape(-1, rows.shape[-1])
        gate_proj = jnp.dot(flat, w_gate[0], preferred_element_type=F32)
        up_proj = jnp.dot(flat, w_up[0], preferred_element_type=F32)
        hidden = lax.optimization_barrier((jax.nn.silu(gate_proj) * up_proj).astype(BF16))
        out = jnp.dot(hidden, w_down[0], preferred_element_type=F32).astype(BF16)
        return out.reshape((2, len(offsets)) + rows.shape[1:])

    fed = {}
    for offsets in ((0,), (1, 3), (2,)):
        out = feed(offsets)
        for at, k in enumerate(offsets):
            fed[k] = out[:, at]
    sums = []
    for which, order in ((0, "yx"), (1, "xy")):
        near = ring_scatter([fed[k][which] for k in range(SIDE)], order[0])
        sums.append(ring_scatter([near[k] for k in range(SIDE)], order[1]))
    summed = jnp.concatenate(sums, 0).astype(BF16)
    summed = summed.reshape(capacity, experts, width).transpose(1, 0, 2)
    returned = lax.all_to_all(summed, "exp", split_axis=0, concat_axis=0)
    returned = returned.reshape(experts * capacity, width)
    expert_sum = 0.0
    for k in range(2):
        pick = (slot_id[:, k][:, None] == places[None, :]).astype(BF16)
        picked = jnp.dot(pick, returned, preferred_element_type=F32)
        expert_sum = expert_sum + gate_weights[:, k][:, None] * picked
    return (middle.astype(F32) + expert_sum).astype(BF16)


def solution(mesh):
    return jax.shard_map(
        local,
        mesh=mesh,
        in_specs=(
            P("seq", "exp"),
            P("seq", "exp"),
            P("seq", "exp"),
            P("seq", "exp"),
            P("exp"),
            P("exp", None),
            P("exp", None),
            P("exp"),
            P("seq", None),
            P("seq", None),
            P("exp"),
            P("exp", "seq"),
            P("seq", None),
            P("seq", None),
            P(),
            P("exp", None, "seq"),
            P("exp", None, "seq"),
            P("exp", "seq", None),
        ),
        out_specs=P("seq", "exp"),
        check_vma=False,
    )
```

```python
import jax
import jax.numpy as jnp
from jax import lax
from jax.experimental import pallas as pl
from jax.experimental.pallas import tpu as pltpu
from jax.sharding import PartitionSpec as P

KCONV = 4
SIDE = 4
STATES = 16
LOG2E = 1.4426950408889634
F32 = jnp.float32
BF16 = jnp.bfloat16


def shift(value, axis, distance):
    cells = [(y, x) for y in range(SIDE) for x in range(SIDE)]
    if axis == "x":
        route = [(y * SIDE + x, y * SIDE + (x + distance) % SIDE) for y, x in cells]
    else:
        route = [(y * SIDE + x, (y + distance) % SIDE * SIDE + x) for y, x in cells]
    return lax.ppermute(value, "seq", route)


def partner(value):
    cells = range(SIDE * SIDE)
    return lax.ppermute(value, "seq", [(i, i ^ 1) for i in cells])


def ring_gather(block, axis):
    return [block] + [shift(block, axis, distance) for distance in range(1, SIDE)]


def relay_gather(blocks, axis):
    half = blocks.shape[0] // 2
    before = shift(blocks, axis, 1)
    after = shift(blocks, axis, -1)
    far = [shift(before[:half], axis, 1), shift(after[half:], axis, -1)]
    return [blocks, before, jnp.concatenate(far), after]


def grid_gather(block, order):
    near = jnp.stack(ring_gather(block, order[0]))
    return relay_gather(near, order[1])


def ring_scatter(blocks, axis):
    total = blocks[0].astype(F32)
    for k in (1, 3, 2):
        total = total + shift(blocks[k].astype(BF16), axis, -k).astype(F32)
    return total


def relay_scatter(blocks, axis):
    own, minus, far, plus = blocks
    half = far.shape[0] // 2
    via_plus = shift(far[:half], axis, 1).astype(F32)
    via_minus = shift(far[half:], axis, -1).astype(F32)
    plus = jnp.concatenate([(plus[:half].astype(F32) + via_plus).astype(BF16), plus[half:]])
    minus = jnp.concatenate([minus[:half], (minus[half:].astype(F32) + via_minus).astype(BF16)])
    total = own.astype(F32) + shift(plus, axis, 1).astype(F32)
    return total + shift(minus, axis, -1).astype(F32)


def fetch(sources, targets, semaphores):
    copies = [
        pltpu.make_async_copy(source, target, semaphores.at[i])
        for i, (source, target) in enumerate(zip(sources, targets))
    ]
    for copy in copies:
        copy.start()
    for copy in copies:
        copy.wait()


def copies_of(arrays):
    return [pltpu.VMEM(array.shape, array.dtype) for array in arrays] + [
        pltpu.SemaphoreType.DMA((len(arrays),))
    ]


def first_pass(x_hbm, dt_hbm, rim_ref, dtb_ref, cw_ref, cb_ref, rate_ref, b_ref,
               step_ref, act_ref, fin_ref, pad_ref, x_ref, dt_ref, semaphores):
    tokens, channels = x_ref.shape
    fetch((x_hbm, dt_hbm), (x_ref, dt_ref), semaphores)
    lanes = 128
    pad_ref[8 : 8 + tokens, :] = x_ref[...].astype(F32)
    pad_ref[0:8, :] = rim_ref[...].astype(F32)
    for k in range(channels // lanes):
        cols = slice(k * lanes, (k + 1) * lanes)
        total = cb_ref[:, cols]
        for tap in range(KCONV):
            low = 8 - (KCONV - 1) + tap
            total = total + cw_ref[tap : tap + 1, cols] * pad_ref[low : low + tokens, cols]
        act_ref[:, k, :] = total * jax.nn.sigmoid(total)
        raw = dt_ref[:, cols].astype(F32) + dtb_ref[:, cols]
        step_ref[:, k, :] = jnp.maximum(raw, 0.0) + jnp.log1p(jnp.exp(-jnp.abs(raw)))

    def advance(t, carry):
        states, summed = carry
        step = step_ref[t]
        source = step * act_ref[t]
        states = tuple(
            jnp.exp2(step * rate_ref[n]) * states[n] + b_ref[t, n] * source for n in range(STATES)
        )
        return states, summed + step

    zero = jnp.zeros((8, lanes), F32)
    states, summed = lax.fori_loop(0, tokens, advance, ((zero,) * STATES, zero), unroll=2)
    for n in range(STATES):
        fin_ref[n] = states[n]
    fin_ref[STATES] = summed


def second_pass(step_hbm, act_hbm, gate_hbm, enter_ref, rate_ref, skip_ref, b_ref, c_ref,
                out_ref, y_ref, step_ref, act_ref, gate_ref, semaphores):
    tokens, channels = gate_ref.shape
    fetch((step_hbm, act_hbm, gate_hbm), (step_ref, act_ref, gate_ref), semaphores)
    lanes = 128
    skip = skip_ref[...]

    def advance(t, states):
        step = step_ref[t]
        act = act_ref[t]
        source = step * act
        sums = [skip * act, None]
        after = []
        for n in range(STATES):
            state = jnp.exp2(step * rate_ref[n]) * states[n] + b_ref[t, n] * source
            term = c_ref[t, n] * state
            sums[n % 2] = term if sums[n % 2] is None else sums[n % 2] + term
            after.append(state)
        y_ref[t] = sums[0] + sums[1]
        return tuple(after)

    lax.fori_loop(0, tokens, advance, tuple(enter_ref[n] for n in range(STATES)), unroll=2)
    for k in range(channels // lanes):
        cols = slice(k * lanes, (k + 1) * lanes)
        gate = gate_ref[:, cols].astype(F32)
        out_ref[:, cols] = (y_ref[:, k, :] * (gate * jax.nn.sigmoid(gate))).astype(BF16)


def entering_state(final, rate, ahead, after):
    along_x = lax.axis_index("seq") % SIDE
    along_y = lax.axis_index("seq") // SIDE

    def chain(earlier, latter):
        decay = jnp.exp2(rate * latter[1])
        return decay * earlier[0] + latter[0], earlier[1] + latter[1]

    def masked(pair, reached):
        return jnp.where(reached, pair[0], 0.0), jnp.where(reached, pair[1], 0.0)

    def split(packed):
        return packed[:STATES], packed[STATES]

    def spread(packed, axis, place):
        others = [split(shift(packed, axis, d)) for d in range(1, SIDE)]
        before = masked(others[2], place >= 3)
        for d in (2, 1):
            before = chain(before, masked(others[d - 1], place >= d))
        return before, others

    own = split(final)
    before_x, others = spread(final, "x", along_x)
    total = chain(before_x, own)
    for d in (3, 2, 1):
        total = chain(total, masked(others[d - 1], along_x < d))
    packed = jnp.concatenate([total[0], total[1][None]], 0)
    packed, after = lax.optimization_barrier((packed, after))
    far = shift(after, "x", 2)
    packed, ahead = lax.optimization_barrier((packed, ahead))
    before_y, _ = spread(packed, "y", along_y)
    return chain(before_y, before_x)[0], ahead, [after, far]


def mixer(
    mixer_in, gate_in, dt_raw, dt_bias, a_log, conv_weight, conv_bias, b_proj, c_proj, d_skip, w_out
):
    tokens, channels = mixer_in.shape
    count, index = lax.axis_size("seq"), lax.axis_index("seq")
    rim = lax.ppermute(mixer_in[tokens - 8 :], "seq", [(i, i + 1) for i in range(count - 1)])
    split = 7 * channels // 16
    low, high = w_out[:split], w_out[split:]
    low_pair = jnp.stack([low, shift(low, "x", 2)])
    dt_raw, low_pair = lax.optimization_barrier((dt_raw, low_pair))
    high_ring = ring_gather(high, "y")
    rate = (-LOG2E * jnp.exp(a_log)).T.reshape(STATES, 8, 128)
    smem = pl.BlockSpec(memory_space=pltpu.SMEM)
    wide = jax.ShapeDtypeStruct((tokens, 8, 128), F32)
    ends = jax.ShapeDtypeStruct((STATES + 1, 8, 128), F32)
    vmem = pl.BlockSpec(memory_space=pltpu.VMEM)
    stay = pl.BlockSpec(memory_space=pltpu.HBM)
    step, act, final = pl.pallas_call(
        first_pass,
        out_shape=(wide, wide, ends),
        in_specs=[stay] * 2 + [vmem] * 5 + [smem],
        out_specs=[vmem] * 3,
        scratch_shapes=[pltpu.VMEM((tokens + 8, channels), F32), *copies_of((mixer_in, dt_raw))],
        compiler_params=pltpu.CompilerParams(vmem_limit_bytes=58 << 20),
        name="scan_state",
    )(mixer_in, dt_raw, rim, dt_bias[None, :], conv_weight.T, conv_bias[None, :], rate, b_proj)
    final, high_ring = lax.optimization_barrier((final, high_ring))
    first = ring_gather(low_pair, "y")
    high_ring = jnp.stack(high_ring)
    enter, first, second = entering_state(final, rate, first, high_ring)
    mixed = pl.pallas_call(
        second_pass,
        out_shape=jax.ShapeDtypeStruct((tokens, channels), BF16),
        in_specs=[stay] * 3 + [vmem] * 3 + [smem] * 2,
        out_specs=vmem,
        scratch_shapes=[pltpu.VMEM((tokens, 8, 128), F32), *copies_of((step, act, gate_in))],
        compiler_params=pltpu.CompilerParams(vmem_limit_bytes=58 << 20),
        name="scan_output",
    )(step, act, gate_in, enter, rate, d_skip.reshape(8, 128), b_proj, c_proj)
    return mixed, (first, second)


def project_kernel(place_ref, own_ref, other_ref, *refs):
    count = SIDE + 2
    out_ref, rows, semaphores = refs[count], refs[count + 1], refs[-1]
    first, second = refs[count + 2 : count + 2 + SIDE], refs[count + 2 + SIDE : -1]
    fetch(refs[:count], (*first, *second), semaphores)
    tokens = own_ref.shape[0]
    rows[:tokens] = own_ref[...]
    rows[tokens:] = other_ref[...]
    split = first[0].shape[1]
    y, side = place_ref[0], place_ref[1]
    for i in range(SIDE):
        for j in range(2):
            owner = lax.rem(y - i + SIDE, SIDE) * 2 + lax.rem(side + j, 2)
            total = jnp.dot(rows[:, :split], first[i][j], preferred_element_type=F32)
            total += jnp.dot(rows[:, split:], second[j][i], preferred_element_type=F32)
            total = total.astype(BF16)
            out_ref[owner, 0] = total[:tokens]
            out_ref[owner, 1] = total[tokens:]


def project(mixed, weights):
    first, second = weights
    tokens, columns = mixed.shape[0], first[0].shape[2]
    index = lax.axis_index("seq")
    place = jnp.stack([index // SIDE, index % SIDE // 2]).astype(jnp.int32)
    vmem = pl.BlockSpec(memory_space=pltpu.VMEM)
    stay = pl.BlockSpec(memory_space=pltpu.HBM)
    partial = pl.pallas_call(
        project_kernel,
        out_shape=jax.ShapeDtypeStruct((2 * SIDE, 2, tokens, columns), BF16),
        in_specs=[pl.BlockSpec(memory_space=pltpu.SMEM)] + [vmem] * 2 + [stay] * (SIDE + 2),
        out_specs=vmem,
        scratch_shapes=[
            pltpu.VMEM((2 * tokens, mixed.shape[1]), BF16), *copies_of((*first, *second))
        ],
        compiler_params=pltpu.CompilerParams(vmem_limit_bytes=58 << 20),
        name="project",
    )(place, mixed, partner(mixed), *first, *second)
    partial = lax.all_to_all(partial, "exp", split_axis=0, concat_axis=0)
    total = jnp.sum(partial.astype(F32), axis=0)
    other = partner(total[1].astype(BF16)).astype(F32)
    is_even = lax.axis_index("seq") % 2 == 0
    return jnp.concatenate(
        [jnp.where(is_even, total[0], other), jnp.where(is_even, other, total[0])], axis=1
    )


def local(
    stream,
    mixer_in,
    gate_in,
    dt_raw,
    dt_bias,
    a_log,
    conv_weight,
    conv_bias,
    b_proj,
    c_proj,
    d_skip,
    w_out,
    expert_index,
    gate_weights,
    norm_gain,
    w_gate,
    w_up,
    w_down,
):
    tokens = mixer_in.shape[0]
    experts = lax.axis_size("exp")
    groups = lax.axis_size("seq")
    capacity = 3 * tokens // experts
    width = stream.shape[1]
    mixed, weights = mixer(
        mixer_in, gate_in, dt_raw, dt_bias, a_log, conv_weight, conv_bias, b_proj, c_proj, d_skip, w_out
    )
    projected = project(mixed, weights)
    middle = (stream.astype(F32) + projected).astype(BF16)

    flat_exp = expert_index.reshape(-1)
    onehot = (flat_exp[:, None] == jnp.arange(experts, dtype=jnp.int32)[None, :]).astype(jnp.int32)
    ranks = jnp.cumsum(onehot, axis=0) - onehot
    slots = jnp.sum(ranks * onehot, axis=1)
    slot_id = (flat_exp * capacity + slots).reshape(tokens, 2)
    places = jnp.arange(experts * capacity, dtype=jnp.int32)
    chosen = (
        (slot_id[:, 0][None, :] == places[:, None]) | (slot_id[:, 1][None, :] == places[:, None])
    ).astype(BF16)
    outgoing = jnp.dot(chosen, middle, preferred_element_type=F32).astype(BF16)
    outgoing = outgoing.reshape(experts, capacity, width)
    arrived = lax.all_to_all(outgoing, "exp", split_axis=0, concat_axis=2, tiled=True)[0].astype(F32)
    mean_square = jnp.mean(arrived * arrived, axis=1, keepdims=True)
    normed = (arrived * lax.rsqrt(mean_square + 1e-05) * norm_gain[None, :]).astype(BF16)

    half = capacity // 2
    first = grid_gather(normed[:half], "xy")
    second = grid_gather(normed[half:], "yx")

    def feed(offsets):
        rows = jnp.stack([part[k] for part in (first, second) for k in offsets])
        flat = rows.reshape(-1, rows.shape[-1])
        gate_proj = jnp.dot(flat, w_gate[0], preferred_element_type=F32)
        up_proj = jnp.dot(flat, w_up[0], preferred_element_type=F32)
        hidden = lax.optimization_barrier((jax.nn.silu(gate_proj) * up_proj).astype(BF16))
        out = jnp.dot(hidden, w_down[0], preferred_element_type=F32).astype(BF16)
        return out.reshape((2, len(offsets)) + rows.shape[1:])

    fed = {}
    for offsets in ((0,), (1, 3), (2,)):
        out = feed(offsets)
        for at, k in enumerate(offsets):
            fed[k] = out[:, at]
    sums = []
    for which, order in ((0, "yx"), (1, "xy")):
        near = relay_scatter([fed[k][which] for k in range(SIDE)], order[0])
        sums.append(ring_scatter([near[k] for k in range(SIDE)], order[1]))
    summed = jnp.concatenate(sums, 0).astype(BF16)
    summed = summed.reshape(capacity, experts, width).transpose(1, 0, 2)
    returned = lax.all_to_all(summed, "exp", split_axis=0, concat_axis=0)
    returned = returned.reshape(experts * capacity, width)
    expert_sum = 0.0
    for k in range(2):
        pick = (slot_id[:, k][:, None] == places[None, :]).astype(BF16)
        picked = jnp.dot(pick, returned, preferred_element_type=F32)
        expert_sum = expert_sum + gate_weights[:, k][:, None] * picked
    return (middle.astype(F32) + expert_sum).astype(BF16)


def solution(mesh):
    return jax.shard_map(
        local,
        mesh=mesh,
        in_specs=(
            P("seq", "exp"),
            P("seq", "exp"),
            P("seq", "exp"),
            P("seq", "exp"),
            P("exp"),
            P("exp", None),
            P("exp", None),
            P("exp"),
            P("seq", None),
            P("seq", None),
            P("exp"),
            P("exp", "seq"),
            P("seq", None),
            P("seq", None),
            P(),
            P("exp", None, "seq"),
            P("exp", None, "seq"),
            P("exp", "seq", None),
        ),
        out_specs=P("seq", "exp"),
        check_vma=False,
    )
```

```python
import jax
import jax.numpy as jnp
from jax import lax
from jax.experimental import pallas as pl
from jax.experimental.pallas import tpu as pltpu
from jax.sharding import PartitionSpec as P

KCONV = 4
SIDE = 4
STATES = 16
LOG2E = 1.4426950408889634
F32 = jnp.float32
BF16 = jnp.bfloat16


def shift(value, axis, distance):
    cells = [(y, x) for y in range(SIDE) for x in range(SIDE)]
    if axis == "x":
        route = [(y * SIDE + x, y * SIDE + (x + distance) % SIDE) for y, x in cells]
    else:
        route = [(y * SIDE + x, (y + distance) % SIDE * SIDE + x) for y, x in cells]
    return lax.ppermute(value, "seq", route)


def partner(value):
    cells = range(SIDE * SIDE)
    return lax.ppermute(value, "seq", [(i, i ^ 1) for i in cells])


def ring_gather(block, axis):
    return [block] + [shift(block, axis, distance) for distance in range(1, SIDE)]


def relay_gather(blocks, axis):
    half = blocks.shape[0] // 2
    before = shift(blocks, axis, 1)
    after = shift(blocks, axis, -1)
    far = [shift(before[:half], axis, 1), shift(after[half:], axis, -1)]
    return [blocks, before, jnp.concatenate(far), after]


def grid_gather(block, order):
    near = jnp.stack(ring_gather(block, order[0]))
    return relay_gather(near, order[1])


def ring_scatter(blocks, axis):
    total = blocks[0].astype(F32)
    for k in (1, 3, 2):
        total = total + shift(blocks[k].astype(BF16), axis, -k).astype(F32)
    return total


def relay_scatter(blocks, axis):
    own, minus, far, plus = blocks
    half = far.shape[0] // 2
    via_plus = shift(far[:half], axis, 1).astype(F32)
    via_minus = shift(far[half:], axis, -1).astype(F32)
    plus = jnp.concatenate([(plus[:half].astype(F32) + via_plus).astype(BF16), plus[half:]])
    minus = jnp.concatenate([minus[:half], (minus[half:].astype(F32) + via_minus).astype(BF16)])
    total = own.astype(F32) + shift(plus, axis, 1).astype(F32)
    return total + shift(minus, axis, -1).astype(F32)


def fetch(sources, targets, semaphores):
    copies = [
        pltpu.make_async_copy(source, target, semaphores.at[i])
        for i, (source, target) in enumerate(zip(sources, targets))
    ]
    for copy in copies:
        copy.start()
    for copy in copies:
        copy.wait()


def copies_of(arrays):
    return [pltpu.VMEM(array.shape, array.dtype) for array in arrays] + [
        pltpu.SemaphoreType.DMA((len(arrays),))
    ]


def first_pass(x_hbm, dt_hbm, rim_ref, dtb_ref, cw_ref, cb_ref, rate_ref, b_ref,
               step_ref, act_ref, fin_ref, pad_ref, x_ref, dt_ref, semaphores):
    tokens, channels = x_ref.shape
    fetch((x_hbm, dt_hbm), (x_ref, dt_ref), semaphores)
    lanes = 128
    pad_ref[8 : 8 + tokens, :] = x_ref[...].astype(F32)
    pad_ref[0:8, :] = rim_ref[...].astype(F32)

    def columns(k, carry):
        cols = pl.ds(pl.multiple_of(k * lanes, lanes), lanes)
        total = cb_ref[:, cols]
        for tap in range(KCONV):
            low = 8 - (KCONV - 1) + tap
            total = total + cw_ref[tap : tap + 1, cols] * pad_ref[low : low + tokens, cols]
        act_ref[:, k, :] = total * jax.nn.sigmoid(total)
        raw = dt_ref[:, cols].astype(F32) + dtb_ref[:, cols]
        step_ref[:, k, :] = jnp.maximum(raw, 0.0) + jnp.log1p(jnp.exp(-jnp.abs(raw)))
        return carry

    lax.fori_loop(0, channels // lanes, columns, 0)

    def advance(t, carry):
        states, summed = carry
        step = step_ref[t]
        source = step * act_ref[t]
        states = tuple(
            jnp.exp2(step * rate_ref[n]) * states[n] + b_ref[t, n] * source for n in range(STATES)
        )
        return states, summed + step

    zero = jnp.zeros((8, lanes), F32)
    states, summed = lax.fori_loop(0, tokens, advance, ((zero,) * STATES, zero), unroll=2)
    for n in range(STATES):
        fin_ref[n] = states[n]
    fin_ref[STATES] = summed


def second_pass(step_hbm, act_hbm, gate_hbm, enter_ref, rate_ref, skip_ref, b_ref, c_ref,
                out_ref, y_ref, step_ref, act_ref, gate_ref, semaphores):
    tokens, channels = gate_ref.shape
    fetch((step_hbm, act_hbm, gate_hbm), (step_ref, act_ref, gate_ref), semaphores)
    lanes = 128
    skip = skip_ref[...]

    def advance(t, states):
        step = step_ref[t]
        act = act_ref[t]
        source = step * act
        sums = [skip * act, None]
        after = []
        for n in range(STATES):
            state = jnp.exp2(step * rate_ref[n]) * states[n] + b_ref[t, n] * source
            term = c_ref[t, n] * state
            sums[n % 2] = term if sums[n % 2] is None else sums[n % 2] + term
            after.append(state)
        y_ref[t] = sums[0] + sums[1]
        return tuple(after)

    lax.fori_loop(0, tokens, advance, tuple(enter_ref[n] for n in range(STATES)), unroll=2)

    def columns(k, carry):
        cols = pl.ds(pl.multiple_of(k * lanes, lanes), lanes)
        gate = gate_ref[:, cols].astype(F32)
        out_ref[:, cols] = (y_ref[:, k, :] * (gate * jax.nn.sigmoid(gate))).astype(BF16)
        return carry

    lax.fori_loop(0, channels // lanes, columns, 0)


def entering_state(final, rate, ahead, after):
    along_x = lax.axis_index("seq") % SIDE
    along_y = lax.axis_index("seq") // SIDE

    def chain(earlier, latter):
        decay = jnp.exp2(rate * latter[1])
        return decay * earlier[0] + latter[0], earlier[1] + latter[1]

    def masked(pair, reached):
        return jnp.where(reached, pair[0], 0.0), jnp.where(reached, pair[1], 0.0)

    def split(packed):
        return packed[:STATES], packed[STATES]

    def spread(packed, axis, place):
        others = [split(shift(packed, axis, d)) for d in range(1, SIDE)]
        before = masked(others[2], place >= 3)
        for d in (2, 1):
            before = chain(before, masked(others[d - 1], place >= d))
        return before, others

    own = split(final)
    before_x, others = spread(final, "x", along_x)
    total = chain(before_x, own)
    for d in (3, 2, 1):
        total = chain(total, masked(others[d - 1], along_x < d))
    packed = jnp.concatenate([total[0], total[1][None]], 0)
    packed, after = lax.optimization_barrier((packed, after))
    far = shift(after, "x", 2)
    packed, ahead = lax.optimization_barrier((packed, ahead))
    before_y, _ = spread(packed, "y", along_y)
    return chain(before_y, before_x)[0], ahead, [after, far]


def mixer(
    mixer_in, gate_in, dt_raw, dt_bias, a_log, conv_weight, conv_bias, b_proj, c_proj, d_skip, w_out
):
    tokens, channels = mixer_in.shape
    count, index = lax.axis_size("seq"), lax.axis_index("seq")
    rim = lax.ppermute(mixer_in[tokens - 8 :], "seq", [(i, i + 1) for i in range(count - 1)])
    split = 7 * channels // 16
    low, high = w_out[:split], w_out[split:]
    low_pair = jnp.stack([low, shift(low, "x", 2)])
    dt_raw, low_pair = lax.optimization_barrier((dt_raw, low_pair))
    high_ring = ring_gather(high, "y")
    rate = (-LOG2E * jnp.exp(a_log)).T.reshape(STATES, 8, 128)
    smem = pl.BlockSpec(memory_space=pltpu.SMEM)
    wide = jax.ShapeDtypeStruct((tokens, 8, 128), F32)
    ends = jax.ShapeDtypeStruct((STATES + 1, 8, 128), F32)
    vmem = pl.BlockSpec(memory_space=pltpu.VMEM)
    stay = pl.BlockSpec(memory_space=pltpu.HBM)
    step, act, final = pl.pallas_call(
        first_pass,
        out_shape=(wide, wide, ends),
        in_specs=[stay] * 2 + [vmem] * 5 + [smem],
        out_specs=[vmem] * 3,
        scratch_shapes=[pltpu.VMEM((tokens + 8, channels), F32), *copies_of((mixer_in, dt_raw))],
        compiler_params=pltpu.CompilerParams(vmem_limit_bytes=58 << 20),
        name="scan_state",
    )(mixer_in, dt_raw, rim, dt_bias[None, :], conv_weight.T, conv_bias[None, :], rate, b_proj)
    final, high_ring = lax.optimization_barrier((final, high_ring))
    first = ring_gather(low_pair, "y")
    high_ring = jnp.stack(high_ring)
    enter, first, second = entering_state(final, rate, first, high_ring)
    mixed = pl.pallas_call(
        second_pass,
        out_shape=jax.ShapeDtypeStruct((tokens, channels), BF16),
        in_specs=[stay] * 3 + [vmem] * 3 + [smem] * 2,
        out_specs=vmem,
        scratch_shapes=[pltpu.VMEM((tokens, 8, 128), F32), *copies_of((step, act, gate_in))],
        compiler_params=pltpu.CompilerParams(vmem_limit_bytes=58 << 20),
        name="scan_output",
    )(step, act, gate_in, enter, rate, d_skip.reshape(8, 128), b_proj, c_proj)
    return mixed, (first, second)


def project_kernel(place_ref, own_ref, other_ref, *refs):
    count = SIDE + 2
    out_ref, rows, first, second, semaphores = refs[count:]
    targets = [first.at[i] for i in range(SIDE)] + [second.at[j] for j in range(2)]
    fetch(refs[:count], targets, semaphores)
    tokens = own_ref.shape[0]
    rows[:tokens] = own_ref[...]
    rows[tokens:] = other_ref[...]
    split = first.shape[2]
    y, side = place_ref[0], place_ref[1]

    def one(step, carry):
        i, j = step // 2, step % 2
        owner = lax.rem(y - i + SIDE, SIDE) * 2 + lax.rem(side + j, 2)
        total = jnp.dot(rows[:, :split], first[i, j], preferred_element_type=F32)
        total += jnp.dot(rows[:, split:], second[j, i], preferred_element_type=F32)
        total = total.astype(BF16)
        out_ref[owner, 0] = total[:tokens]
        out_ref[owner, 1] = total[tokens:]
        return carry

    lax.fori_loop(0, 2 * SIDE, one, 0)


def project(mixed, weights):
    first, second = weights
    tokens, columns = mixed.shape[0], first[0].shape[2]
    index = lax.axis_index("seq")
    place = jnp.stack([index // SIDE, index % SIDE // 2]).astype(jnp.int32)
    vmem = pl.BlockSpec(memory_space=pltpu.VMEM)
    stay = pl.BlockSpec(memory_space=pltpu.HBM)
    partial = pl.pallas_call(
        project_kernel,
        out_shape=jax.ShapeDtypeStruct((2 * SIDE, 2, tokens, columns), BF16),
        in_specs=[pl.BlockSpec(memory_space=pltpu.SMEM)] + [vmem] * 2 + [stay] * (SIDE + 2),
        out_specs=vmem,
        scratch_shapes=[
            pltpu.VMEM((2 * tokens, mixed.shape[1]), BF16),
            pltpu.VMEM((SIDE, *first[0].shape), BF16),
            pltpu.VMEM((2, *second[0].shape), BF16),
            pltpu.SemaphoreType.DMA((SIDE + 2,)),
        ],
        compiler_params=pltpu.CompilerParams(vmem_limit_bytes=58 << 20),
        name="project",
    )(place, mixed, partner(mixed), *first, *second)
    partial = lax.all_to_all(partial, "exp", split_axis=0, concat_axis=0)
    total = jnp.sum(partial.astype(F32), axis=0)
    other = partner(total[1].astype(BF16)).astype(F32)
    is_even = lax.axis_index("seq") % 2 == 0
    return jnp.concatenate(
        [jnp.where(is_even, total[0], other), jnp.where(is_even, other, total[0])], axis=1
    )


def local(
    stream,
    mixer_in,
    gate_in,
    dt_raw,
    dt_bias,
    a_log,
    conv_weight,
    conv_bias,
    b_proj,
    c_proj,
    d_skip,
    w_out,
    expert_index,
    gate_weights,
    norm_gain,
    w_gate,
    w_up,
    w_down,
):
    tokens = mixer_in.shape[0]
    experts = lax.axis_size("exp")
    groups = lax.axis_size("seq")
    capacity = 3 * tokens // experts
    width = stream.shape[1]
    mixed, weights = mixer(
        mixer_in, gate_in, dt_raw, dt_bias, a_log, conv_weight, conv_bias, b_proj, c_proj, d_skip, w_out
    )
    projected = project(mixed, weights)
    middle = (stream.astype(F32) + projected).astype(BF16)

    flat_exp = expert_index.reshape(-1)
    onehot = (flat_exp[:, None] == jnp.arange(experts, dtype=jnp.int32)[None, :]).astype(jnp.int32)
    ranks = jnp.cumsum(onehot, axis=0) - onehot
    slots = jnp.sum(ranks * onehot, axis=1)
    slot_id = (flat_exp * capacity + slots).reshape(tokens, 2)
    places = jnp.arange(experts * capacity, dtype=jnp.int32)
    chosen = (
        (slot_id[:, 0][None, :] == places[:, None]) | (slot_id[:, 1][None, :] == places[:, None])
    ).astype(BF16)
    outgoing = jnp.dot(chosen, middle, preferred_element_type=F32).astype(BF16)
    outgoing = outgoing.reshape(experts, capacity, width)
    arrived = lax.all_to_all(outgoing, "exp", split_axis=0, concat_axis=2, tiled=True)[0].astype(F32)
    mean_square = jnp.mean(arrived * arrived, axis=1, keepdims=True)
    normed = (arrived * lax.rsqrt(mean_square + 1e-05) * norm_gain[None, :]).astype(BF16)

    half = capacity // 2
    first = grid_gather(normed[:half], "xy")
    second = grid_gather(normed[half:], "yx")

    def feed(offsets):
        rows = jnp.stack([part[k] for part in (first, second) for k in offsets])
        flat = rows.reshape(-1, rows.shape[-1])
        gate_proj = jnp.dot(flat, w_gate[0], preferred_element_type=F32)
        up_proj = jnp.dot(flat, w_up[0], preferred_element_type=F32)
        hidden = lax.optimization_barrier((jax.nn.silu(gate_proj) * up_proj).astype(BF16))
        out = jnp.dot(hidden, w_down[0], preferred_element_type=F32).astype(BF16)
        return out.reshape((2, len(offsets)) + rows.shape[1:])

    fed = {}
    for offsets in ((0,), (1, 3), (2,)):
        out = feed(offsets)
        for at, k in enumerate(offsets):
            fed[k] = out[:, at]
    sums = []
    for which, order in ((0, "yx"), (1, "xy")):
        near = relay_scatter([fed[k][which] for k in range(SIDE)], order[0])
        sums.append(ring_scatter([near[k] for k in range(SIDE)], order[1]))
    summed = jnp.concatenate(sums, 0).astype(BF16)
    summed = summed.reshape(capacity, experts, width).transpose(1, 0, 2)
    returned = lax.all_to_all(summed, "exp", split_axis=0, concat_axis=0)
    returned = returned.reshape(experts * capacity, width)
    expert_sum = 0.0
    for k in range(2):
        pick = (slot_id[:, k][:, None] == places[None, :]).astype(BF16)
        picked = jnp.dot(pick, returned, preferred_element_type=F32)
        expert_sum = expert_sum + gate_weights[:, k][:, None] * picked
    return (middle.astype(F32) + expert_sum).astype(BF16)


def solution(mesh):
    return jax.shard_map(
        local,
        mesh=mesh,
        in_specs=(
            P("seq", "exp"),
            P("seq", "exp"),
            P("seq", "exp"),
            P("seq", "exp"),
            P("exp"),
            P("exp", None),
            P("exp", None),
            P("exp"),
            P("seq", None),
            P("seq", None),
            P("exp"),
            P("exp", "seq"),
            P("seq", None),
            P("seq", None),
            P(),
            P("exp", None, "seq"),
            P("exp", None, "seq"),
            P("exp", "seq", None),
        ),
        out_specs=P("seq", "exp"),
        check_vma=False,
    )
```

```python
import jax
import jax.numpy as jnp
from jax import lax
from jax.experimental import pallas as pl
from jax.experimental.pallas import tpu as pltpu
from jax.sharding import PartitionSpec as P

KCONV = 4
SIDE = 4
STATES = 16
LOG2E = 1.4426950408889634
F32 = jnp.float32
BF16 = jnp.bfloat16


def shift(value, axis, distance):
    cells = [(y, x) for y in range(SIDE) for x in range(SIDE)]
    if axis == "x":
        route = [(y * SIDE + x, y * SIDE + (x + distance) % SIDE) for y, x in cells]
    else:
        route = [(y * SIDE + x, (y + distance) % SIDE * SIDE + x) for y, x in cells]
    return lax.ppermute(value, "seq", route)


def partner(value):
    cells = range(SIDE * SIDE)
    return lax.ppermute(value, "seq", [(i, i ^ 1) for i in cells])


def ring_gather(block, axis):
    return [block] + [shift(block, axis, distance) for distance in range(1, SIDE)]


def relay_gather(blocks, axis):
    half = blocks.shape[0] // 2
    before = shift(blocks, axis, 1)
    after = shift(blocks, axis, -1)
    far = [shift(before[:half], axis, 1), shift(after[half:], axis, -1)]
    return [blocks, before, jnp.concatenate(far), after]


def grid_gather(block, order):
    near = jnp.stack(ring_gather(block, order[0]))
    return relay_gather(near, order[1])


def ring_scatter(blocks, axis):
    total = blocks[0].astype(F32)
    for k in (1, 3, 2):
        total = total + shift(blocks[k].astype(BF16), axis, -k).astype(F32)
    return total


def relay_scatter(blocks, axis):
    own, minus, far, plus = blocks
    half = far.shape[0] // 2
    via_plus = shift(far[:half], axis, 1).astype(F32)
    via_minus = shift(far[half:], axis, -1).astype(F32)
    plus = jnp.concatenate([(plus[:half].astype(F32) + via_plus).astype(BF16), plus[half:]])
    minus = jnp.concatenate([minus[:half], (minus[half:].astype(F32) + via_minus).astype(BF16)])
    total = own.astype(F32) + shift(plus, axis, 1).astype(F32)
    return total + shift(minus, axis, -1).astype(F32)


def fetch(sources, targets, semaphores):
    copies = [
        pltpu.make_async_copy(source, target, semaphores.at[i])
        for i, (source, target) in enumerate(zip(sources, targets))
    ]
    for copy in copies:
        copy.start()
    for copy in copies:
        copy.wait()


def copies_of(arrays):
    return [pltpu.VMEM(array.shape, array.dtype) for array in arrays] + [
        pltpu.SemaphoreType.DMA((len(arrays),))
    ]


def first_pass(x_hbm, dt_hbm, rim_ref, dtb_ref, cw_ref, cb_ref, rate_ref, b_ref,
               step_ref, act_ref, fin_ref, pad_ref, x_ref, dt_ref, semaphores):
    tokens, channels = x_ref.shape
    fetch((x_hbm, dt_hbm), (x_ref, dt_ref), semaphores)
    lanes = 128
    pad_ref[8 : 8 + tokens, :] = x_ref[...].astype(F32)
    pad_ref[0:8, :] = rim_ref[...].astype(F32)

    def columns(k, carry):
        cols = pl.ds(pl.multiple_of(k * lanes, lanes), lanes)
        total = cb_ref[:, cols]
        for tap in range(KCONV):
            low = 8 - (KCONV - 1) + tap
            total = total + cw_ref[tap : tap + 1, cols] * pad_ref[low : low + tokens, cols]
        act_ref[:, k, :] = total * jax.nn.sigmoid(total)
        raw = dt_ref[:, cols].astype(F32) + dtb_ref[:, cols]
        step_ref[:, k, :] = jnp.maximum(raw, 0.0) + jnp.log1p(jnp.exp(-jnp.abs(raw)))
        return carry

    lax.fori_loop(0, channels // lanes, columns, 0)

    def advance(t, carry):
        states, summed = carry
        step = step_ref[t]
        source = step * act_ref[t]
        states = tuple(
            jnp.exp2(step * rate_ref[n]) * states[n] + b_ref[t, n] * source for n in range(STATES)
        )
        return states, summed + step

    zero = jnp.zeros((8, lanes), F32)
    states, summed = lax.fori_loop(0, tokens, advance, ((zero,) * STATES, zero), unroll=2)
    for n in range(STATES):
        fin_ref[n] = states[n]
    fin_ref[STATES] = summed


def second_pass(step_hbm, act_hbm, gate_hbm, enter_ref, rate_ref, skip_ref, b_ref, c_ref,
                out_ref, y_ref, step_ref, act_ref, gate_ref, semaphores):
    tokens, channels = gate_ref.shape
    fetch((step_hbm, act_hbm, gate_hbm), (step_ref, act_ref, gate_ref), semaphores)
    lanes = 128
    skip = skip_ref[...]

    def advance(t, states):
        step = step_ref[t]
        act = act_ref[t]
        source = step * act
        sums = [skip * act, None]
        after = []
        for n in range(STATES):
            state = jnp.exp2(step * rate_ref[n]) * states[n] + b_ref[t, n] * source
            term = c_ref[t, n] * state
            sums[n % 2] = term if sums[n % 2] is None else sums[n % 2] + term
            after.append(state)
        y_ref[t] = sums[0] + sums[1]
        return tuple(after)

    lax.fori_loop(0, tokens, advance, tuple(enter_ref[n] for n in range(STATES)), unroll=2)

    def columns(k, carry):
        cols = pl.ds(pl.multiple_of(k * lanes, lanes), lanes)
        gate = gate_ref[:, cols].astype(F32)
        out_ref[:, cols] = (y_ref[:, k, :] * (gate * jax.nn.sigmoid(gate))).astype(BF16)
        return carry

    lax.fori_loop(0, channels // lanes, columns, 0)


def entering_state(final, rate, ahead, after):
    along_x = lax.axis_index("seq") % SIDE
    along_y = lax.axis_index("seq") // SIDE

    def chain(earlier, latter):
        decay = jnp.exp2(rate * latter[1])
        return decay * earlier[0] + latter[0], earlier[1] + latter[1]

    def masked(pair, reached):
        return jnp.where(reached, pair[0], 0.0), jnp.where(reached, pair[1], 0.0)

    def split(packed):
        return packed[:STATES], packed[STATES]

    def spread(packed, axis, place):
        others = [split(shift(packed, axis, d)) for d in range(1, SIDE)]
        before = masked(others[2], place >= 3)
        for d in (2, 1):
            before = chain(before, masked(others[d - 1], place >= d))
        return before, others

    own = split(final)
    before_x, others = spread(final, "x", along_x)
    total = chain(before_x, own)
    for d in (3, 2, 1):
        total = chain(total, masked(others[d - 1], along_x < d))
    packed = jnp.concatenate([total[0], total[1][None]], 0)
    packed, after = lax.optimization_barrier((packed, after))
    far = shift(after, "x", 2)
    packed, ahead = lax.optimization_barrier((packed, ahead))
    before_y, _ = spread(packed, "y", along_y)
    return chain(before_y, before_x)[0], ahead, [after, far]


def mixer(
    mixer_in, gate_in, dt_raw, dt_bias, a_log, conv_weight, conv_bias, b_proj, c_proj, d_skip, w_out
):
    tokens, channels = mixer_in.shape
    count, index = lax.axis_size("seq"), lax.axis_index("seq")
    rim = lax.ppermute(mixer_in[tokens - 8 :], "seq", [(i, i + 1) for i in range(count - 1)])
    split = 7 * channels // 16
    low, high = w_out[:split], w_out[split:]
    low_pair = jnp.stack([low, shift(low, "x", 2)])
    dt_raw, low_pair = lax.optimization_barrier((dt_raw, low_pair))
    high_ring = ring_gather(high, "y")
    rate = (-LOG2E * jnp.exp(a_log)).T.reshape(STATES, 8, 128)
    smem = pl.BlockSpec(memory_space=pltpu.SMEM)
    wide = jax.ShapeDtypeStruct((tokens, 8, 128), F32)
    ends = jax.ShapeDtypeStruct((STATES + 1, 8, 128), F32)
    vmem = pl.BlockSpec(memory_space=pltpu.VMEM)
    stay = pl.BlockSpec(memory_space=pltpu.HBM)
    step, act, final = pl.pallas_call(
        first_pass,
        out_shape=(wide, wide, ends),
        in_specs=[stay] * 2 + [vmem] * 5 + [smem],
        out_specs=[vmem] * 3,
        scratch_shapes=[pltpu.VMEM((tokens + 8, channels), F32), *copies_of((mixer_in, dt_raw))],
        compiler_params=pltpu.CompilerParams(vmem_limit_bytes=58 << 20),
        name="scan_state",
    )(mixer_in, dt_raw, rim, dt_bias[None, :], conv_weight.T, conv_bias[None, :], rate, b_proj)
    final, high_ring = lax.optimization_barrier((final, high_ring))
    first = ring_gather(low_pair, "y")
    high_ring = jnp.stack(high_ring)
    enter, first, second = entering_state(final, rate, first, high_ring)
    mixed = pl.pallas_call(
        second_pass,
        out_shape=jax.ShapeDtypeStruct((tokens, channels), BF16),
        in_specs=[stay] * 3 + [vmem] * 3 + [smem] * 2,
        out_specs=vmem,
        scratch_shapes=[pltpu.VMEM((tokens, 8, 128), F32), *copies_of((step, act, gate_in))],
        compiler_params=pltpu.CompilerParams(vmem_limit_bytes=58 << 20),
        name="scan_output",
    )(step, act, gate_in, enter, rate, d_skip.reshape(8, 128), b_proj, c_proj)
    return mixed, (first, second)


def project_kernel(place_ref, *refs):
    count = SIDE + 2
    out_ref, first, second, semaphores = refs[-4:]
    rows_ref, fixed = refs[count], refs[count + 1 : -4]
    targets = [first.at[i] for i in range(SIDE)] + [second.at[j] for j in range(2)]
    fetch(refs[:count], targets, semaphores)
    split = first.shape[2]
    y, side = place_ref[0], place_ref[1]
    if fixed:
        out_ref[:, 0] = fixed[0][...]

    def one(i, carry):
        for j in range(2):
            owner = lax.rem(y - i + SIDE, SIDE) * 2 + lax.rem(side + j, 2)
            total = jnp.dot(rows_ref[:, :split], first[i, j], preferred_element_type=F32)
            total += jnp.dot(rows_ref[:, split:], second[j, i], preferred_element_type=F32)
            if fixed:
                out_ref[owner, 1] = total.astype(BF16)
            else:
                out_ref[owner] = total.astype(BF16)
        return carry

    lax.fori_loop(0, SIDE, one, 0)


def project(mixed, weights):
    first, second = weights
    tokens, columns = mixed.shape[0], first[0].shape[2]
    index = lax.axis_index("seq")
    place = jnp.stack([index // SIDE, index % SIDE // 2]).astype(jnp.int32)
    vmem = pl.BlockSpec(memory_space=pltpu.VMEM)
    stay = pl.BlockSpec(memory_space=pltpu.HBM)

    def call(shape, *operands):
        return pl.pallas_call(
            project_kernel,
            out_shape=jax.ShapeDtypeStruct(shape, BF16),
            in_specs=[pl.BlockSpec(memory_space=pltpu.SMEM)]
            + [stay] * (SIDE + 2)
            + [vmem] * len(operands),
            out_specs=vmem,
            scratch_shapes=[
                pltpu.VMEM((SIDE, *first[0].shape), BF16),
                pltpu.VMEM((2, *second[0].shape), BF16),
                pltpu.SemaphoreType.DMA((SIDE + 2,)),
            ],
            compiler_params=pltpu.CompilerParams(vmem_limit_bytes=58 << 20),
            name="project",
        )(place, *first, *second, *operands)

    other = partner(mixed)
    own = call((2 * SIDE, tokens, columns), mixed)
    partial = call((2 * SIDE, 2, tokens, columns), other, own)
    partial = lax.all_to_all(partial, "exp", split_axis=0, concat_axis=0)
    total = jnp.sum(partial.astype(F32), axis=0)
    other = partner(total[1].astype(BF16)).astype(F32)
    is_even = lax.axis_index("seq") % 2 == 0
    return jnp.concatenate(
        [jnp.where(is_even, total[0], other), jnp.where(is_even, other, total[0])], axis=1
    )


def local(
    stream,
    mixer_in,
    gate_in,
    dt_raw,
    dt_bias,
    a_log,
    conv_weight,
    conv_bias,
    b_proj,
    c_proj,
    d_skip,
    w_out,
    expert_index,
    gate_weights,
    norm_gain,
    w_gate,
    w_up,
    w_down,
):
    tokens = mixer_in.shape[0]
    experts = lax.axis_size("exp")
    groups = lax.axis_size("seq")
    capacity = 3 * tokens // experts
    width = stream.shape[1]
    mixed, weights = mixer(
        mixer_in, gate_in, dt_raw, dt_bias, a_log, conv_weight, conv_bias, b_proj, c_proj, d_skip, w_out
    )
    projected = project(mixed, weights)
    middle = (stream.astype(F32) + projected).astype(BF16)

    flat_exp = expert_index.reshape(-1)
    onehot = (flat_exp[:, None] == jnp.arange(experts, dtype=jnp.int32)[None, :]).astype(jnp.int32)
    ranks = jnp.cumsum(onehot, axis=0) - onehot
    slots = jnp.sum(ranks * onehot, axis=1)
    slot_id = (flat_exp * capacity + slots).reshape(tokens, 2)
    places = jnp.arange(experts * capacity, dtype=jnp.int32)
    chosen = (
        (slot_id[:, 0][None, :] == places[:, None]) | (slot_id[:, 1][None, :] == places[:, None])
    ).astype(BF16)
    outgoing = jnp.dot(chosen, middle, preferred_element_type=F32).astype(BF16)
    outgoing = outgoing.reshape(experts, capacity, width)
    arrived = lax.all_to_all(outgoing, "exp", split_axis=0, concat_axis=2, tiled=True)[0].astype(F32)
    mean_square = jnp.mean(arrived * arrived, axis=1, keepdims=True)
    normed = (arrived * lax.rsqrt(mean_square + 1e-05) * norm_gain[None, :]).astype(BF16)

    half = capacity // 2
    first = grid_gather(normed[:half], "xy")
    second = grid_gather(normed[half:], "yx")

    def feed(offsets):
        rows = jnp.stack([part[k] for part in (first, second) for k in offsets])
        flat = rows.reshape(-1, rows.shape[-1])
        gate_proj = jnp.dot(flat, w_gate[0], preferred_element_type=F32)
        up_proj = jnp.dot(flat, w_up[0], preferred_element_type=F32)
        hidden = lax.optimization_barrier((jax.nn.silu(gate_proj) * up_proj).astype(BF16))
        out = jnp.dot(hidden, w_down[0], preferred_element_type=F32).astype(BF16)
        return out.reshape((2, len(offsets)) + rows.shape[1:])

    fed = {}
    for offsets in ((0,), (1, 3), (2,)):
        out = feed(offsets)
        for at, k in enumerate(offsets):
            fed[k] = out[:, at]
    sums = []
    for which, order in ((0, "yx"), (1, "xy")):
        near = relay_scatter([fed[k][which] for k in range(SIDE)], order[0])
        sums.append(ring_scatter([near[k] for k in range(SIDE)], order[1]))
    summed = jnp.concatenate(sums, 0).astype(BF16)
    summed = summed.reshape(capacity, experts, width).transpose(1, 0, 2)
    returned = lax.all_to_all(summed, "exp", split_axis=0, concat_axis=0)
    returned = returned.reshape(experts * capacity, width)
    expert_sum = 0.0
    for k in range(2):
        pick = (slot_id[:, k][:, None] == places[None, :]).astype(BF16)
        picked = jnp.dot(pick, returned, preferred_element_type=F32)
        expert_sum = expert_sum + gate_weights[:, k][:, None] * picked
    return (middle.astype(F32) + expert_sum).astype(BF16)


def solution(mesh):
    return jax.shard_map(
        local,
        mesh=mesh,
        in_specs=(
            P("seq", "exp"),
            P("seq", "exp"),
            P("seq", "exp"),
            P("seq", "exp"),
            P("exp"),
            P("exp", None),
            P("exp", None),
            P("exp"),
            P("seq", None),
            P("seq", None),
            P("exp"),
            P("exp", "seq"),
            P("seq", None),
            P("seq", None),
            P(),
            P("exp", None, "seq"),
            P("exp", None, "seq"),
            P("exp", "seq", None),
        ),
        out_specs=P("seq", "exp"),
        check_vma=False,
    )
```

```python
import jax
import jax.numpy as jnp
from jax import lax
from jax.experimental import pallas as pl
from jax.experimental.pallas import tpu as pltpu
from jax.sharding import PartitionSpec as P

KCONV = 4
SIDE = 4
STATES = 16
LOG2E = 1.4426950408889634
F32 = jnp.float32
BF16 = jnp.bfloat16


def shift(value, axis, distance):
    cells = [(y, x) for y in range(SIDE) for x in range(SIDE)]
    if axis == "x":
        route = [(y * SIDE + x, y * SIDE + (x + distance) % SIDE) for y, x in cells]
    else:
        route = [(y * SIDE + x, (y + distance) % SIDE * SIDE + x) for y, x in cells]
    return lax.ppermute(value, "seq", route)


def partner(value):
    cells = range(SIDE * SIDE)
    return lax.ppermute(value, "seq", [(i, i ^ 1) for i in cells])


def ring_gather(block, axis):
    return [block] + [shift(block, axis, distance) for distance in range(1, SIDE)]


def relay_gather(blocks, axis):
    half = blocks.shape[0] // 2
    before = shift(blocks, axis, 1)
    after = shift(blocks, axis, -1)
    far = [shift(before[:half], axis, 1), shift(after[half:], axis, -1)]
    return [blocks, before, jnp.concatenate(far), after]


def grid_gather(block, order):
    near = jnp.stack(ring_gather(block, order[0]))
    return relay_gather(near, order[1])


def ring_scatter(blocks, axis):
    total = blocks[0].astype(F32)
    for k in (1, 3, 2):
        total = total + shift(blocks[k].astype(BF16), axis, -k).astype(F32)
    return total


def relay_scatter(blocks, axis):
    own, minus, far, plus = blocks
    half = far.shape[0] // 2
    via_plus = shift(far[:half], axis, 1).astype(F32)
    via_minus = shift(far[half:], axis, -1).astype(F32)
    plus = jnp.concatenate([(plus[:half].astype(F32) + via_plus).astype(BF16), plus[half:]])
    minus = jnp.concatenate([minus[:half], (minus[half:].astype(F32) + via_minus).astype(BF16)])
    total = own.astype(F32) + shift(plus, axis, 1).astype(F32)
    return total + shift(minus, axis, -1).astype(F32)


def fetch(sources, targets, semaphores):
    copies = [
        pltpu.make_async_copy(source, target, semaphores.at[i])
        for i, (source, target) in enumerate(zip(sources, targets))
    ]
    for copy in copies:
        copy.start()
    for copy in copies:
        copy.wait()


def copies_of(arrays):
    return [pltpu.VMEM(array.shape, array.dtype) for array in arrays] + [
        pltpu.SemaphoreType.DMA((len(arrays),))
    ]


def first_pass(x_hbm, dt_hbm, rim_ref, dtb_ref, cw_ref, cb_ref, rate_ref, b_ref,
               step_ref, act_ref, fin_ref, pad_ref, x_ref, dt_ref, semaphores):
    tokens, channels = x_ref.shape
    fetch((x_hbm, dt_hbm), (x_ref, dt_ref), semaphores)
    lanes = 128
    pad_ref[8 : 8 + tokens, :] = x_ref[...].astype(F32)
    pad_ref[0:8, :] = rim_ref[...].astype(F32)

    def columns(k, carry):
        cols = pl.ds(pl.multiple_of(k * lanes, lanes), lanes)
        total = cb_ref[:, cols]
        for tap in range(KCONV):
            low = 8 - (KCONV - 1) + tap
            total = total + cw_ref[tap : tap + 1, cols] * pad_ref[low : low + tokens, cols]
        act_ref[:, k, :] = total * jax.nn.sigmoid(total)
        raw = dt_ref[:, cols].astype(F32) + dtb_ref[:, cols]
        step_ref[:, k, :] = jnp.maximum(raw, 0.0) + jnp.log1p(jnp.exp(-jnp.abs(raw)))
        return carry

    lax.fori_loop(0, channels // lanes, columns, 0)

    def advance(t, carry):
        states, summed = carry
        step = step_ref[t]
        source = step * act_ref[t]
        states = tuple(
            jnp.exp2(step * rate_ref[n]) * states[n] + b_ref[t, n] * source for n in range(STATES)
        )
        return states, summed + step

    zero = jnp.zeros((8, lanes), F32)
    states, summed = lax.fori_loop(0, tokens, advance, ((zero,) * STATES, zero), unroll=2)
    for n in range(STATES):
        fin_ref[n] = states[n]
    fin_ref[STATES] = summed


def second_pass(step_hbm, act_hbm, gate_hbm, enter_ref, rate_ref, skip_ref, b_ref, c_ref,
                out_ref, y_ref, step_ref, act_ref, gate_ref, semaphores):
    tokens, channels = gate_ref.shape
    fetch((step_hbm, act_hbm, gate_hbm), (step_ref, act_ref, gate_ref), semaphores)
    lanes = 128
    skip = skip_ref[...]

    def advance(t, states):
        step = step_ref[t]
        act = act_ref[t]
        source = step * act
        sums = [skip * act, None]
        after = []
        for n in range(STATES):
            state = jnp.exp2(step * rate_ref[n]) * states[n] + b_ref[t, n] * source
            term = c_ref[t, n] * state
            sums[n % 2] = term if sums[n % 2] is None else sums[n % 2] + term
            after.append(state)
        y_ref[t] = sums[0] + sums[1]
        return tuple(after)

    lax.fori_loop(0, tokens, advance, tuple(enter_ref[n] for n in range(STATES)), unroll=2)

    def columns(k, carry):
        cols = pl.ds(pl.multiple_of(k * lanes, lanes), lanes)
        gate = gate_ref[:, cols].astype(F32)
        out_ref[:, cols] = (y_ref[:, k, :] * (gate * jax.nn.sigmoid(gate))).astype(BF16)
        return carry

    lax.fori_loop(0, channels // lanes, columns, 0)


def entering_state(final, rate, ahead, after):
    along_x = lax.axis_index("seq") % SIDE
    along_y = lax.axis_index("seq") // SIDE

    def chain(earlier, latter):
        decay = jnp.exp2(rate * latter[1])
        return decay * earlier[0] + latter[0], earlier[1] + latter[1]

    def masked(pair, reached):
        return jnp.where(reached, pair[0], 0.0), jnp.where(reached, pair[1], 0.0)

    def split(packed):
        return packed[:STATES], packed[STATES]

    def spread(packed, axis, place):
        others = [split(shift(packed, axis, d)) for d in range(1, SIDE)]
        before = masked(others[2], place >= 3)
        for d in (2, 1):
            before = chain(before, masked(others[d - 1], place >= d))
        return before, others

    own = split(final)
    before_x, others = spread(final, "x", along_x)
    total = chain(before_x, own)
    for d in (3, 2, 1):
        total = chain(total, masked(others[d - 1], along_x < d))
    packed = jnp.concatenate([total[0], total[1][None]], 0)
    packed, after = lax.optimization_barrier((packed, after))
    far = shift(after, "x", 2)
    packed, ahead = lax.optimization_barrier((packed, ahead))
    before_y, _ = spread(packed, "y", along_y)
    return chain(before_y, before_x)[0], ahead, [after, far]


def mixer(
    mixer_in, gate_in, dt_raw, dt_bias, a_log, conv_weight, conv_bias, b_proj, c_proj, d_skip, w_out
):
    tokens, channels = mixer_in.shape
    count, index = lax.axis_size("seq"), lax.axis_index("seq")
    rim = lax.ppermute(mixer_in[tokens - 8 :], "seq", [(i, i + 1) for i in range(count - 1)])
    split = 7 * channels // 16
    low, high = w_out[:split], w_out[split:]
    low_pair = jnp.stack([low, shift(low, "x", 2)])
    dt_raw, low_pair = lax.optimization_barrier((dt_raw, low_pair))
    high_ring = ring_gather(high, "y")
    rate = (-LOG2E * jnp.exp(a_log)).T.reshape(STATES, 8, 128)
    smem = pl.BlockSpec(memory_space=pltpu.SMEM)
    wide = jax.ShapeDtypeStruct((tokens, 8, 128), F32)
    ends = jax.ShapeDtypeStruct((STATES + 1, 8, 128), F32)
    vmem = pl.BlockSpec(memory_space=pltpu.VMEM)
    stay = pl.BlockSpec(memory_space=pltpu.HBM)
    step, act, final = pl.pallas_call(
        first_pass,
        out_shape=(wide, wide, ends),
        in_specs=[stay] * 2 + [vmem] * 5 + [smem],
        out_specs=[vmem] * 3,
        scratch_shapes=[pltpu.VMEM((tokens + 8, channels), F32), *copies_of((mixer_in, dt_raw))],
        compiler_params=pltpu.CompilerParams(vmem_limit_bytes=58 << 20),
        name="scan_state",
    )(mixer_in, dt_raw, rim, dt_bias[None, :], conv_weight.T, conv_bias[None, :], rate, b_proj)
    final, high_ring = lax.optimization_barrier((final, high_ring))
    first = ring_gather(low_pair, "y")
    high_ring = jnp.stack(high_ring)
    enter, first, second = entering_state(final, rate, first, high_ring)
    mixed = pl.pallas_call(
        second_pass,
        out_shape=jax.ShapeDtypeStruct((tokens, channels), BF16),
        in_specs=[stay] * 3 + [vmem] * 3 + [smem] * 2,
        out_specs=vmem,
        scratch_shapes=[pltpu.VMEM((tokens, 8, 128), F32), *copies_of((step, act, gate_in))],
        compiler_params=pltpu.CompilerParams(vmem_limit_bytes=58 << 20),
        name="scan_output",
    )(step, act, gate_in, enter, rate, d_skip.reshape(8, 128), b_proj, c_proj)
    return mixed, (first, second)


def project_kernel(place_ref, *refs):
    count = SIDE + 2
    keep_ref, send_ref, first, second, semaphores = refs[-5:]
    rows_ref, fixed = refs[count], refs[count + 1 : -5]
    targets = [first.at[i] for i in range(SIDE)] + [second.at[j] for j in range(2)]
    split = first.shape[2]
    y, side = place_ref[0], place_ref[1]

    def one(i, carry):
        plane = lax.rem(y - i + SIDE, SIDE)
        for j, ref in ((side, keep_ref), (1 - side, send_ref)):
            total = jnp.dot(rows_ref[:, :split], first[i, j], preferred_element_type=F32)
            total += jnp.dot(rows_ref[:, split:], second[j, i], preferred_element_type=F32)
            if fixed:
                ref[plane, 1] = total.astype(BF16)
            else:
                ref[plane] = total.astype(BF16)
        return carry

    if fixed:
        copies = [
            pltpu.make_async_copy(refs[i], targets[i], semaphores.at[i])
            for i in (SIDE, SIDE + 1, *range(SIDE))
        ]
        for copy in copies:
            copy.start()
        keep_ref[:, 0] = fixed[0][...]
        send_ref[:, 0] = fixed[1][...]
        copies[0].wait()
        copies[1].wait()
        for i in range(SIDE):
            copies[2 + i].wait()
            one(i, 0)
    else:
        fetch(refs[:count], targets, semaphores)
        lax.fori_loop(0, SIDE, one, 0)


def project(mixed, weights):
    first, second = weights
    tokens, columns = mixed.shape[0], first[0].shape[2]
    index, core = lax.axis_index("seq"), lax.axis_index("exp") % 2
    place = jnp.stack([index // SIDE, (core + index % SIDE // 2) % 2]).astype(jnp.int32)
    vmem = pl.BlockSpec(memory_space=pltpu.VMEM)
    stay = pl.BlockSpec(memory_space=pltpu.HBM)

    def call(shape, *operands):
        return pl.pallas_call(
            project_kernel,
            out_shape=[jax.ShapeDtypeStruct(shape, BF16)] * 2,
            in_specs=[pl.BlockSpec(memory_space=pltpu.SMEM)]
            + [stay] * (SIDE + 2)
            + [vmem] * len(operands),
            out_specs=[vmem] * 2,
            scratch_shapes=[
                pltpu.VMEM((SIDE, *first[0].shape), BF16),
                pltpu.VMEM((2, *second[0].shape), BF16),
                pltpu.SemaphoreType.DMA((SIDE + 2,)),
            ],
            compiler_params=pltpu.CompilerParams(vmem_limit_bytes=58 << 20),
            name="project",
        )(place, *first, *second, *operands)

    other = partner(mixed)
    own = call((SIDE, tokens, columns), mixed)
    keep, send = call((SIDE, 2, tokens, columns), other, *own)
    members = range(2 * SIDE)
    come = lax.ppermute(send, "exp", [(i, i ^ 1) for i in members])
    partial = (keep.astype(F32) + come.astype(F32)).astype(BF16)
    planes = [[i for i in members if i % 2 == c] for c in range(2)]
    partial = lax.all_to_all(
        partial, "exp", split_axis=0, concat_axis=0, axis_index_groups=planes
    )
    total = jnp.sum(partial.astype(F32), axis=0)
    other = partner(total[1].astype(BF16)).astype(F32)
    is_even = lax.axis_index("seq") % 2 == 0
    return jnp.concatenate(
        [jnp.where(is_even, total[0], other), jnp.where(is_even, other, total[0])], axis=1
    )


def local(
    stream,
    mixer_in,
    gate_in,
    dt_raw,
    dt_bias,
    a_log,
    conv_weight,
    conv_bias,
    b_proj,
    c_proj,
    d_skip,
    w_out,
    expert_index,
    gate_weights,
    norm_gain,
    w_gate,
    w_up,
    w_down,
):
    tokens = mixer_in.shape[0]
    experts = lax.axis_size("exp")
    groups = lax.axis_size("seq")
    capacity = 3 * tokens // experts
    width = stream.shape[1]
    mixed, weights = mixer(
        mixer_in, gate_in, dt_raw, dt_bias, a_log, conv_weight, conv_bias, b_proj, c_proj, d_skip, w_out
    )
    projected = project(mixed, weights)
    middle = (stream.astype(F32) + projected).astype(BF16)

    flat_exp = expert_index.reshape(-1)
    onehot = (flat_exp[:, None] == jnp.arange(experts, dtype=jnp.int32)[None, :]).astype(jnp.int32)
    ranks = jnp.cumsum(onehot, axis=0) - onehot
    slots = jnp.sum(ranks * onehot, axis=1)
    slot_id = (flat_exp * capacity + slots).reshape(tokens, 2)
    places = jnp.arange(experts * capacity, dtype=jnp.int32)
    chosen = (
        (slot_id[:, 0][None, :] == places[:, None]) | (slot_id[:, 1][None, :] == places[:, None])
    ).astype(BF16)
    outgoing = jnp.dot(chosen, middle, preferred_element_type=F32).astype(BF16)
    outgoing = outgoing.reshape(experts, capacity, width)
    arrived = lax.all_to_all(outgoing, "exp", split_axis=0, concat_axis=2, tiled=True)[0].astype(F32)
    mean_square = jnp.mean(arrived * arrived, axis=1, keepdims=True)
    normed = (arrived * lax.rsqrt(mean_square + 1e-05) * norm_gain[None, :]).astype(BF16)

    half = capacity // 2
    first = grid_gather(normed[:half], "xy")
    second = grid_gather(normed[half:], "yx")

    def feed(offsets):
        rows = jnp.stack([part[k] for part in (first, second) for k in offsets])
        flat = rows.reshape(-1, rows.shape[-1])
        gate_proj = jnp.dot(flat, w_gate[0], preferred_element_type=F32)
        up_proj = jnp.dot(flat, w_up[0], preferred_element_type=F32)
        hidden = lax.optimization_barrier((jax.nn.silu(gate_proj) * up_proj).astype(BF16))
        out = jnp.dot(hidden, w_down[0], preferred_element_type=F32).astype(BF16)
        return out.reshape((2, len(offsets)) + rows.shape[1:])

    fed = {}
    for offsets in ((0,), (1, 3), (2,)):
        out = feed(offsets)
        for at, k in enumerate(offsets):
            fed[k] = out[:, at]
    sums = []
    for which, order in ((0, "yx"), (1, "xy")):
        near = relay_scatter([fed[k][which] for k in range(SIDE)], order[0])
        sums.append(ring_scatter([near[k] for k in range(SIDE)], order[1]))
    summed = jnp.concatenate(sums, 0).astype(BF16)
    summed = summed.reshape(capacity, experts, width).transpose(1, 0, 2)
    returned = lax.all_to_all(summed, "exp", split_axis=0, concat_axis=0)
    returned = returned.reshape(experts * capacity, width)
    expert_sum = 0.0
    for k in range(2):
        pick = (slot_id[:, k][:, None] == places[None, :]).astype(BF16)
        picked = jnp.dot(pick, returned, preferred_element_type=F32)
        expert_sum = expert_sum + gate_weights[:, k][:, None] * picked
    return (middle.astype(F32) + expert_sum).astype(BF16)


def solution(mesh):
    return jax.shard_map(
        local,
        mesh=mesh,
        in_specs=(
            P("seq", "exp"),
            P("seq", "exp"),
            P("seq", "exp"),
            P("seq", "exp"),
            P("exp"),
            P("exp", None),
            P("exp", None),
            P("exp"),
            P("seq", None),
            P("seq", None),
            P("exp"),
            P("exp", "seq"),
            P("seq", None),
            P("seq", None),
            P(),
            P("exp", None, "seq"),
            P("exp", None, "seq"),
            P("exp", "seq", None),
        ),
        out_specs=P("seq", "exp"),
        check_vma=False,
    )
```

```python
import jax
import jax.numpy as jnp
from jax import lax
from jax.experimental import pallas as pl
from jax.experimental.pallas import tpu as pltpu
from jax.sharding import PartitionSpec as P

KCONV = 4
SIDE = 4
STATES = 16
LOG2E = 1.4426950408889634
F32 = jnp.float32
BF16 = jnp.bfloat16


def shift(value, axis, distance):
    cells = [(y, x) for y in range(SIDE) for x in range(SIDE)]
    if axis == "x":
        route = [(y * SIDE + x, y * SIDE + (x + distance) % SIDE) for y, x in cells]
    else:
        route = [(y * SIDE + x, (y + distance) % SIDE * SIDE + x) for y, x in cells]
    return lax.ppermute(value, "seq", route)


def partner(value):
    cells = range(SIDE * SIDE)
    return lax.ppermute(value, "seq", [(i, i ^ 1) for i in cells])


def ring_gather(block, axis):
    return [block] + [shift(block, axis, distance) for distance in range(1, SIDE)]


def relay_gather(blocks, axis):
    half = blocks.shape[0] // 2
    before = shift(blocks, axis, 1)
    after = shift(blocks, axis, -1)
    far = [shift(before[:half], axis, 1), shift(after[half:], axis, -1)]
    return [blocks, before, jnp.concatenate(far), after]


def grid_gather(block, order):
    near = jnp.stack(ring_gather(block, order[0]))
    return relay_gather(near, order[1])


def ring_scatter(blocks, axis):
    total = blocks[0].astype(F32)
    for k in (1, 3, 2):
        total = total + shift(blocks[k].astype(BF16), axis, -k).astype(F32)
    return total


def relay_scatter(blocks, axis):
    own, minus, far, plus = blocks
    half = far.shape[0] // 2
    via_plus = shift(far[:half], axis, 1).astype(F32)
    via_minus = shift(far[half:], axis, -1).astype(F32)
    plus = jnp.concatenate([(plus[:half].astype(F32) + via_plus).astype(BF16), plus[half:]])
    minus = jnp.concatenate([minus[:half], (minus[half:].astype(F32) + via_minus).astype(BF16)])
    total = own.astype(F32) + shift(plus, axis, 1).astype(F32)
    return total + shift(minus, axis, -1).astype(F32)


def fetch(sources, targets, semaphores):
    copies = [
        pltpu.make_async_copy(source, target, semaphores.at[i])
        for i, (source, target) in enumerate(zip(sources, targets))
    ]
    for copy in copies:
        copy.start()
    for copy in copies:
        copy.wait()


def copies_of(arrays):
    return [pltpu.VMEM(array.shape, array.dtype) for array in arrays] + [
        pltpu.SemaphoreType.DMA((len(arrays),))
    ]


def first_pass(x_hbm, dt_hbm, rim_ref, dtb_ref, cw_ref, cb_ref, rate_ref, b_ref,
               step_ref, act_ref, fin_ref, pad_ref, x_ref, dt_ref, semaphores):
    tokens, channels = x_ref.shape
    fetch((x_hbm, dt_hbm), (x_ref, dt_ref), semaphores)
    lanes = 128
    pad_ref[8 : 8 + tokens, :] = x_ref[...].astype(F32)
    pad_ref[0:8, :] = rim_ref[...].astype(F32)

    def columns(k, carry):
        cols = pl.ds(pl.multiple_of(k * lanes, lanes), lanes)
        total = cb_ref[:, cols]
        for tap in range(KCONV):
            low = 8 - (KCONV - 1) + tap
            total = total + cw_ref[tap : tap + 1, cols] * pad_ref[low : low + tokens, cols]
        act_ref[:, k, :] = total * jax.nn.sigmoid(total)
        raw = dt_ref[:, cols].astype(F32) + dtb_ref[:, cols]
        step_ref[:, k, :] = jnp.maximum(raw, 0.0) + jnp.log1p(jnp.exp(-jnp.abs(raw)))
        return carry

    lax.fori_loop(0, channels // lanes, columns, 0)

    def advance(t, carry):
        states, summed = carry
        step = step_ref[t]
        source = step * act_ref[t]
        states = tuple(
            jnp.exp2(step * rate_ref[n]) * states[n] + b_ref[t, n] * source for n in range(STATES)
        )
        return states, summed + step

    zero = jnp.zeros((8, lanes), F32)
    states, summed = lax.fori_loop(0, tokens, advance, ((zero,) * STATES, zero), unroll=2)
    for n in range(STATES):
        fin_ref[n] = states[n]
    fin_ref[STATES] = summed


def second_pass(step_hbm, act_hbm, gate_hbm, enter_ref, rate_ref, skip_ref, b_ref, c_ref,
                out_ref, y_ref, step_ref, act_ref, gate_ref, semaphores):
    tokens, channels = gate_ref.shape
    fetch((step_hbm, act_hbm, gate_hbm), (step_ref, act_ref, gate_ref), semaphores)
    lanes = 128
    skip = skip_ref[...]

    def advance(t, states):
        step = step_ref[t]
        act = act_ref[t]
        source = step * act
        sums = [skip * act, None]
        after = []
        for n in range(STATES):
            state = jnp.exp2(step * rate_ref[n]) * states[n] + b_ref[t, n] * source
            term = c_ref[t, n] * state
            sums[n % 2] = term if sums[n % 2] is None else sums[n % 2] + term
            after.append(state)
        y_ref[t] = sums[0] + sums[1]
        return tuple(after)

    lax.fori_loop(0, tokens, advance, tuple(enter_ref[n] for n in range(STATES)), unroll=2)

    def columns(k, carry):
        cols = pl.ds(pl.multiple_of(k * lanes, lanes), lanes)
        gate = gate_ref[:, cols].astype(F32)
        out_ref[:, cols] = (y_ref[:, k, :] * (gate * jax.nn.sigmoid(gate))).astype(BF16)
        return carry

    lax.fori_loop(0, channels // lanes, columns, 0)


def entering_state(final, rate, ahead, after):
    along_x = lax.axis_index("seq") % SIDE
    along_y = lax.axis_index("seq") // SIDE

    def chain(earlier, latter):
        decay = jnp.exp2(rate * latter[1])
        return decay * earlier[0] + latter[0], earlier[1] + latter[1]

    def masked(pair, reached):
        return jnp.where(reached, pair[0], 0.0), jnp.where(reached, pair[1], 0.0)

    def split(packed):
        return packed[:STATES], packed[STATES]

    def spread(packed, axis, place):
        others = [split(shift(packed, axis, d)) for d in range(1, SIDE)]
        before = masked(others[2], place >= 3)
        for d in (2, 1):
            before = chain(before, masked(others[d - 1], place >= d))
        return before, others

    own = split(final)
    before_x, others = spread(final, "x", along_x)
    total = chain(before_x, own)
    for d in (3, 2, 1):
        total = chain(total, masked(others[d - 1], along_x < d))
    packed = jnp.concatenate([total[0], total[1][None]], 0)
    packed, after = lax.optimization_barrier((packed, after))
    far = shift(after, "x", 2)
    packed, ahead = lax.optimization_barrier((packed, ahead))
    before_y, _ = spread(packed, "y", along_y)
    return chain(before_y, before_x)[0], ahead, [after, far]


def mixer(
    mixer_in, gate_in, dt_raw, dt_bias, a_log, conv_weight, conv_bias, b_proj, c_proj, d_skip, w_out
):
    tokens, channels = mixer_in.shape
    count, index = lax.axis_size("seq"), lax.axis_index("seq")
    rim = lax.ppermute(mixer_in[tokens - 8 :], "seq", [(i, i + 1) for i in range(count - 1)])
    split = 7 * channels // 16
    low, high = w_out[:split], w_out[split:]
    low_pair = jnp.stack([low, shift(low, "x", 2)])
    dt_raw, low_pair = lax.optimization_barrier((dt_raw, low_pair))
    high_ring = ring_gather(high, "y")
    rate = (-LOG2E * jnp.exp(a_log)).T.reshape(STATES, 8, 128)
    smem = pl.BlockSpec(memory_space=pltpu.SMEM)
    wide = jax.ShapeDtypeStruct((tokens, 8, 128), F32)
    ends = jax.ShapeDtypeStruct((STATES + 1, 8, 128), F32)
    vmem = pl.BlockSpec(memory_space=pltpu.VMEM)
    stay = pl.BlockSpec(memory_space=pltpu.HBM)
    step, act, final = pl.pallas_call(
        first_pass,
        out_shape=(wide, wide, ends),
        in_specs=[stay] * 2 + [vmem] * 5 + [smem],
        out_specs=[vmem] * 3,
        scratch_shapes=[pltpu.VMEM((tokens + 8, channels), F32), *copies_of((mixer_in, dt_raw))],
        compiler_params=pltpu.CompilerParams(vmem_limit_bytes=58 << 20),
        name="scan_state",
    )(mixer_in, dt_raw, rim, dt_bias[None, :], conv_weight.T, conv_bias[None, :], rate, b_proj)
    final, high_ring = lax.optimization_barrier((final, high_ring))
    first = ring_gather(low_pair, "y")
    high_ring = jnp.stack(high_ring)
    enter, first, second = entering_state(final, rate, first, high_ring)
    mixed = pl.pallas_call(
        second_pass,
        out_shape=jax.ShapeDtypeStruct((tokens, channels), BF16),
        in_specs=[stay] * 3 + [vmem] * 3 + [smem] * 2,
        out_specs=vmem,
        scratch_shapes=[pltpu.VMEM((tokens, 8, 128), F32), *copies_of((step, act, gate_in))],
        compiler_params=pltpu.CompilerParams(vmem_limit_bytes=58 << 20),
        name="scan_output",
    )(step, act, gate_in, enter, rate, d_skip.reshape(8, 128), b_proj, c_proj)
    return mixed, (first, second)


def project_kernel(place_ref, *refs):
    count = SIDE + 2
    keep_ref, send_ref, first, second, semaphores = refs[-5:]
    rows_ref, fixed = refs[count], refs[count + 1 : -5]
    targets = [first.at[i] for i in range(SIDE)] + [second.at[j] for j in range(2)]
    split = first.shape[2]
    y, side = place_ref[0], place_ref[1]

    def one(i, carry):
        plane = lax.rem(y - i + SIDE, SIDE)
        for j, ref in ((side, keep_ref), (1 - side, send_ref)):
            total = jnp.dot(rows_ref[:, :split], first[i, j], preferred_element_type=F32)
            total += jnp.dot(rows_ref[:, split:], second[j, i], preferred_element_type=F32)
            if fixed:
                ref[plane, 1] = total.astype(BF16)
            else:
                ref[plane] = total.astype(BF16)
        return carry

    fetch(refs[:count], targets, semaphores)
    if fixed:
        keep_ref[:, 0] = fixed[0][...]
        send_ref[:, 0] = fixed[1][...]
    lax.fori_loop(0, SIDE, one, 0)


def project(mixed, weights):
    first, second = weights
    tokens, columns = mixed.shape[0], first[0].shape[2]
    index, core = lax.axis_index("seq"), lax.axis_index("exp") % 2
    place = jnp.stack([index // SIDE, (core + index % SIDE // 2) % 2]).astype(jnp.int32)
    vmem = pl.BlockSpec(memory_space=pltpu.VMEM)
    stay = pl.BlockSpec(memory_space=pltpu.HBM)

    def call(shape, *operands):
        return pl.pallas_call(
            project_kernel,
            out_shape=[jax.ShapeDtypeStruct(shape, BF16)] * 2,
            in_specs=[pl.BlockSpec(memory_space=pltpu.SMEM)]
            + [stay] * (SIDE + 2)
            + [vmem] * len(operands),
            out_specs=[vmem] * 2,
            scratch_shapes=[
                pltpu.VMEM((SIDE, *first[0].shape), BF16),
                pltpu.VMEM((2, *second[0].shape), BF16),
                pltpu.SemaphoreType.DMA((SIDE + 2,)),
            ],
            compiler_params=pltpu.CompilerParams(vmem_limit_bytes=58 << 20),
            name="project",
        )(place, *first, *second, *operands)

    other = partner(mixed)
    own = call((SIDE, tokens, columns), mixed)
    keep, send = call((SIDE, 2, tokens, columns), other, *own)
    members = range(2 * SIDE)
    come = lax.ppermute(send, "exp", [(i, i ^ 1) for i in members])
    partial = (keep.astype(F32) + come.astype(F32)).astype(BF16)
    planes = [[i for i in members if i % 2 == c] for c in range(2)]
    partial = lax.all_to_all(
        partial, "exp", split_axis=0, concat_axis=0, axis_index_groups=planes
    )
    total = jnp.sum(partial.astype(F32), axis=0)
    other = partner(total[1].astype(BF16)).astype(F32)
    is_even = lax.axis_index("seq") % 2 == 0
    return jnp.concatenate(
        [jnp.where(is_even, total[0], other), jnp.where(is_even, other, total[0])], axis=1
    )


def local(
    stream,
    mixer_in,
    gate_in,
    dt_raw,
    dt_bias,
    a_log,
    conv_weight,
    conv_bias,
    b_proj,
    c_proj,
    d_skip,
    w_out,
    expert_index,
    gate_weights,
    norm_gain,
    w_gate,
    w_up,
    w_down,
):
    tokens = mixer_in.shape[0]
    experts = lax.axis_size("exp")
    groups = lax.axis_size("seq")
    capacity = 3 * tokens // experts
    width = stream.shape[1]
    mixed, weights = mixer(
        mixer_in, gate_in, dt_raw, dt_bias, a_log, conv_weight, conv_bias, b_proj, c_proj, d_skip, w_out
    )
    projected = project(mixed, weights)
    middle = (stream.astype(F32) + projected).astype(BF16)

    flat_exp = expert_index.reshape(-1)
    onehot = (flat_exp[:, None] == jnp.arange(experts, dtype=jnp.int32)[None, :]).astype(jnp.int32)
    ranks = jnp.cumsum(onehot, axis=0) - onehot
    slots = jnp.sum(ranks * onehot, axis=1)
    slot_id = (flat_exp * capacity + slots).reshape(tokens, 2)
    places = jnp.arange(experts * capacity, dtype=jnp.int32)
    chosen = (
        (slot_id[:, 0][None, :] == places[:, None]) | (slot_id[:, 1][None, :] == places[:, None])
    ).astype(BF16)
    outgoing = jnp.dot(chosen, middle, preferred_element_type=F32).astype(BF16)
    outgoing = outgoing.reshape(experts, capacity, width)
    arrived = lax.all_to_all(outgoing, "exp", split_axis=0, concat_axis=2, tiled=True)[0].astype(F32)
    mean_square = jnp.mean(arrived * arrived, axis=1, keepdims=True)
    normed = (arrived * lax.rsqrt(mean_square + 1e-05) * norm_gain[None, :]).astype(BF16)

    half = capacity // 2
    first = grid_gather(normed[:half], "xy")
    second = grid_gather(normed[half:], "yx")

    def feed(offsets):
        rows = jnp.stack([part[k] for part in (first, second) for k in offsets])
        flat = rows.reshape(-1, rows.shape[-1])
        gate_proj = jnp.dot(flat, w_gate[0], preferred_element_type=F32)
        up_proj = jnp.dot(flat, w_up[0], preferred_element_type=F32)
        hidden = lax.optimization_barrier((jax.nn.silu(gate_proj) * up_proj).astype(BF16))
        out = jnp.dot(hidden, w_down[0], preferred_element_type=F32).astype(BF16)
        return out.reshape((2, len(offsets)) + rows.shape[1:])

    fed = {}
    for offsets in ((0,), (1, 3), (2,)):
        out = feed(offsets)
        for at, k in enumerate(offsets):
            fed[k] = out[:, at]
    sums = []
    for which, order in ((0, "yx"), (1, "xy")):
        near = relay_scatter([fed[k][which] for k in range(SIDE)], order[0])
        sums.append(ring_scatter([near[k] for k in range(SIDE)], order[1]))
    summed = jnp.concatenate(sums, 0).astype(BF16)
    summed = summed.reshape(capacity, experts, width).transpose(1, 0, 2)
    returned = lax.all_to_all(summed, "exp", split_axis=0, concat_axis=0)
    returned = returned.reshape(experts * capacity, width)
    expert_sum = 0.0
    for k in range(2):
        pick = (slot_id[:, k][:, None] == places[None, :]).astype(BF16)
        picked = jnp.dot(pick, returned, preferred_element_type=F32)
        expert_sum = expert_sum + gate_weights[:, k][:, None] * picked
    return (middle.astype(F32) + expert_sum).astype(BF16)


def solution(mesh):
    return jax.shard_map(
        local,
        mesh=mesh,
        in_specs=(
            P("seq", "exp"),
            P("seq", "exp"),
            P("seq", "exp"),
            P("seq", "exp"),
            P("exp"),
            P("exp", None),
            P("exp", None),
            P("exp"),
            P("seq", None),
            P("seq", None),
            P("exp"),
            P("exp", "seq"),
            P("seq", None),
            P("seq", None),
            P(),
            P("exp", None, "seq"),
            P("exp", None, "seq"),
            P("exp", "seq", None),
        ),
        out_specs=P("seq", "exp"),
        check_vma=False,
    )
```

```python
import jax
import jax.numpy as jnp
from jax import lax
from jax.experimental import pallas as pl
from jax.experimental.pallas import tpu as pltpu
from jax.sharding import PartitionSpec as P

KCONV = 4
SIDE = 4
STATES = 16
LOG2E = 1.4426950408889634
F32 = jnp.float32
BF16 = jnp.bfloat16


def shift(value, axis, distance):
    cells = [(y, x) for y in range(SIDE) for x in range(SIDE)]
    if axis == "x":
        route = [(y * SIDE + x, y * SIDE + (x + distance) % SIDE) for y, x in cells]
    else:
        route = [(y * SIDE + x, (y + distance) % SIDE * SIDE + x) for y, x in cells]
    return lax.ppermute(value, "seq", route)


def partner(value):
    cells = range(SIDE * SIDE)
    return lax.ppermute(value, "seq", [(i, i ^ 1) for i in cells])


def ring_gather(block, axis):
    return [block] + [shift(block, axis, distance) for distance in range(1, SIDE)]


def relay_gather(blocks, axis):
    half = blocks.shape[0] // 2
    before = shift(blocks, axis, 1)
    after = shift(blocks, axis, -1)
    far = [shift(before[:half], axis, 1), shift(after[half:], axis, -1)]
    return [blocks, before, jnp.concatenate(far), after]


def grid_gather(block, order):
    near = jnp.stack(ring_gather(block, order[0]))
    return relay_gather(near, order[1])


def ring_scatter(blocks, axis):
    total = blocks[0].astype(F32)
    for k in (1, 3, 2):
        total = total + shift(blocks[k].astype(BF16), axis, -k).astype(F32)
    return total


def relay_scatter(blocks, axis):
    own, minus, far, plus = blocks
    half = far.shape[0] // 2
    via_plus = shift(far[:half], axis, 1).astype(F32)
    via_minus = shift(far[half:], axis, -1).astype(F32)
    plus = jnp.concatenate([(plus[:half].astype(F32) + via_plus).astype(BF16), plus[half:]])
    minus = jnp.concatenate([minus[:half], (minus[half:].astype(F32) + via_minus).astype(BF16)])
    total = own.astype(F32) + shift(plus, axis, 1).astype(F32)
    return total + shift(minus, axis, -1).astype(F32)


def fetch(sources, targets, semaphores):
    copies = [
        pltpu.make_async_copy(source, target, semaphores.at[i])
        for i, (source, target) in enumerate(zip(sources, targets))
    ]
    for copy in copies:
        copy.start()
    for copy in copies:
        copy.wait()


def copies_of(arrays):
    return [pltpu.VMEM(array.shape, array.dtype) for array in arrays] + [
        pltpu.SemaphoreType.DMA((len(arrays),))
    ]


def first_pass(x_hbm, dt_hbm, rim_ref, dtb_ref, cw_ref, cb_ref, rate_ref, b_ref,
               step_ref, act_ref, fin_ref, pad_ref, x_ref, dt_ref, semaphores):
    tokens, channels = x_ref.shape
    fetch((x_hbm, dt_hbm), (x_ref, dt_ref), semaphores)
    lanes = 128
    pad_ref[8 : 8 + tokens, :] = x_ref[...].astype(F32)
    pad_ref[0:8, :] = rim_ref[...].astype(F32)

    def columns(k, carry):
        cols = pl.ds(pl.multiple_of(k * lanes, lanes), lanes)
        total = cb_ref[:, cols]
        for tap in range(KCONV):
            low = 8 - (KCONV - 1) + tap
            total = total + cw_ref[tap : tap + 1, cols] * pad_ref[low : low + tokens, cols]
        act_ref[:, k, :] = total * jax.nn.sigmoid(total)
        raw = dt_ref[:, cols].astype(F32) + dtb_ref[:, cols]
        step_ref[:, k, :] = jnp.maximum(raw, 0.0) + jnp.log1p(jnp.exp(-jnp.abs(raw)))
        return carry

    lax.fori_loop(0, channels // lanes, columns, 0)

    def advance(t, carry):
        states, summed = carry
        step = step_ref[t]
        source = step * act_ref[t]
        states = tuple(
            jnp.exp2(step * rate_ref[n]) * states[n] + b_ref[t, n] * source for n in range(STATES)
        )
        return states, summed + step

    zero = jnp.zeros((8, lanes), F32)
    states, summed = lax.fori_loop(0, tokens, advance, ((zero,) * STATES, zero), unroll=2)
    for n in range(STATES):
        fin_ref[n] = states[n]
    fin_ref[STATES] = summed


def second_pass(step_hbm, act_hbm, gate_hbm, enter_ref, rate_ref, skip_ref, b_ref, c_ref,
                out_ref, y_ref, step_ref, act_ref, gate_ref, semaphores):
    tokens, channels = gate_ref.shape
    fetch((step_hbm, act_hbm, gate_hbm), (step_ref, act_ref, gate_ref), semaphores)
    lanes = 128
    skip = skip_ref[...]

    def advance(t, states):
        step = step_ref[t]
        act = act_ref[t]
        source = step * act
        sums = [skip * act, None]
        after = []
        for n in range(STATES):
            state = jnp.exp2(step * rate_ref[n]) * states[n] + b_ref[t, n] * source
            term = c_ref[t, n] * state
            sums[n % 2] = term if sums[n % 2] is None else sums[n % 2] + term
            after.append(state)
        y_ref[t] = sums[0] + sums[1]
        return tuple(after)

    lax.fori_loop(0, tokens, advance, tuple(enter_ref[n] for n in range(STATES)), unroll=2)

    def columns(k, carry):
        cols = pl.ds(pl.multiple_of(k * lanes, lanes), lanes)
        gate = gate_ref[:, cols].astype(F32)
        out_ref[:, cols] = (y_ref[:, k, :] * (gate * jax.nn.sigmoid(gate))).astype(BF16)
        return carry

    lax.fori_loop(0, channels // lanes, columns, 0)


def entering_state(final, rate, ahead, after):
    along_x = lax.axis_index("seq") % SIDE
    along_y = lax.axis_index("seq") // SIDE

    def chain(earlier, latter):
        decay = jnp.exp2(rate * latter[1])
        return decay * earlier[0] + latter[0], earlier[1] + latter[1]

    def masked(pair, reached):
        return jnp.where(reached, pair[0], 0.0), jnp.where(reached, pair[1], 0.0)

    def split(packed):
        return packed[:STATES], packed[STATES]

    def spread(packed, axis, place):
        others = [split(shift(packed, axis, d)) for d in range(1, SIDE)]
        before = masked(others[2], place >= 3)
        for d in (2, 1):
            before = chain(before, masked(others[d - 1], place >= d))
        return before, others

    own = split(final)
    before_x, others = spread(final, "x", along_x)
    total = chain(before_x, own)
    for d in (3, 2, 1):
        total = chain(total, masked(others[d - 1], along_x < d))
    packed = jnp.concatenate([total[0], total[1][None]], 0)
    packed, after = lax.optimization_barrier((packed, after))
    far = shift(after, "x", 2)
    packed, ahead = lax.optimization_barrier((packed, ahead))
    before_y, _ = spread(packed, "y", along_y)
    return chain(before_y, before_x)[0], ahead, [after, far]


def mixer(
    mixer_in, gate_in, dt_raw, dt_bias, a_log, conv_weight, conv_bias, b_proj, c_proj, d_skip, w_out
):
    tokens, channels = mixer_in.shape
    count, index = lax.axis_size("seq"), lax.axis_index("seq")
    rim = lax.ppermute(mixer_in[tokens - 8 :], "seq", [(i, i + 1) for i in range(count - 1)])
    split = channels // 2
    low, high = w_out[:split], w_out[split:]
    low_pair = jnp.stack([low, shift(low, "x", 2)])
    dt_raw, low_pair = lax.optimization_barrier((dt_raw, low_pair))
    high_ring = ring_gather(high, "y")
    rate = (-LOG2E * jnp.exp(a_log)).T.reshape(STATES, 8, 128)
    smem = pl.BlockSpec(memory_space=pltpu.SMEM)
    wide = jax.ShapeDtypeStruct((tokens, 8, 128), F32)
    ends = jax.ShapeDtypeStruct((STATES + 1, 8, 128), F32)
    vmem = pl.BlockSpec(memory_space=pltpu.VMEM)
    stay = pl.BlockSpec(memory_space=pltpu.HBM)
    step, act, final = pl.pallas_call(
        first_pass,
        out_shape=(wide, wide, ends),
        in_specs=[stay] * 2 + [vmem] * 5 + [smem],
        out_specs=[vmem] * 3,
        scratch_shapes=[pltpu.VMEM((tokens + 8, channels), F32), *copies_of((mixer_in, dt_raw))],
        compiler_params=pltpu.CompilerParams(vmem_limit_bytes=58 << 20),
        name="scan_state",
    )(mixer_in, dt_raw, rim, dt_bias[None, :], conv_weight.T, conv_bias[None, :], rate, b_proj)
    final, high_ring = lax.optimization_barrier((final, high_ring))
    first = ring_gather(low_pair, "y")
    high_ring = jnp.stack(high_ring)
    enter, first, second = entering_state(final, rate, first, high_ring)
    mixed = pl.pallas_call(
        second_pass,
        out_shape=jax.ShapeDtypeStruct((tokens, channels), BF16),
        in_specs=[stay] * 3 + [vmem] * 3 + [smem] * 2,
        out_specs=vmem,
        scratch_shapes=[pltpu.VMEM((tokens, 8, 128), F32), *copies_of((step, act, gate_in))],
        compiler_params=pltpu.CompilerParams(vmem_limit_bytes=58 << 20),
        name="scan_output",
    )(step, act, gate_in, enter, rate, d_skip.reshape(8, 128), b_proj, c_proj)
    return mixed, (first, second)


def project_kernel(place_ref, *refs):
    count = SIDE + 2
    keep_ref, send_ref, first, second, semaphores = refs[-5:]
    rows_ref, fixed = refs[count], refs[count + 1 : -5]
    targets = [first.at[i] for i in range(SIDE)] + [second.at[j] for j in range(2)]
    split = first.shape[2]
    y, side = place_ref[0], place_ref[1]

    def one(i, carry):
        plane = lax.rem(y - i + SIDE, SIDE)
        for j, ref in ((side, keep_ref), (1 - side, send_ref)):
            total = jnp.dot(rows_ref[:, :split], first[i, j], preferred_element_type=F32)
            total += jnp.dot(rows_ref[:, split:], second[j, i], preferred_element_type=F32)
            if fixed:
                ref[plane, 1] = total.astype(BF16)
            else:
                ref[plane] = total.astype(BF16)
        return carry

    fetch(refs[:count], targets, semaphores)
    if fixed:
        keep_ref[:, 0] = fixed[0][...]
        send_ref[:, 0] = fixed[1][...]
    lax.fori_loop(0, SIDE, one, 0)


def project(mixed, weights):
    first, second = weights
    tokens, columns = mixed.shape[0], first[0].shape[2]
    index, core = lax.axis_index("seq"), lax.axis_index("exp") % 2
    place = jnp.stack([index // SIDE, (core + index % SIDE // 2) % 2]).astype(jnp.int32)
    vmem = pl.BlockSpec(memory_space=pltpu.VMEM)
    stay = pl.BlockSpec(memory_space=pltpu.HBM)

    def call(shape, *operands):
        return pl.pallas_call(
            project_kernel,
            out_shape=[jax.ShapeDtypeStruct(shape, BF16)] * 2,
            in_specs=[pl.BlockSpec(memory_space=pltpu.SMEM)]
            + [stay] * (SIDE + 2)
            + [vmem] * len(operands),
            out_specs=[vmem] * 2,
            scratch_shapes=[
                pltpu.VMEM((SIDE, *first[0].shape), BF16),
                pltpu.VMEM((2, *second[0].shape), BF16),
                pltpu.SemaphoreType.DMA((SIDE + 2,)),
            ],
            compiler_params=pltpu.CompilerParams(vmem_limit_bytes=58 << 20),
            name="project",
        )(place, *first, *second, *operands)

    other = partner(mixed)
    own = call((SIDE, tokens, columns), mixed)
    keep, send = call((SIDE, 2, tokens, columns), other, *own)
    members = range(2 * SIDE)
    come = lax.ppermute(send, "exp", [(i, i ^ 1) for i in members])
    partial = (keep.astype(F32) + come.astype(F32)).astype(BF16)
    planes = [[i for i in members if i % 2 == c] for c in range(2)]
    partial = lax.all_to_all(
        partial, "exp", split_axis=0, concat_axis=0, axis_index_groups=planes
    )
    total = jnp.sum(partial.astype(F32), axis=0)
    other = partner(total[1].astype(BF16)).astype(F32)
    is_even = lax.axis_index("seq") % 2 == 0
    return jnp.concatenate(
        [jnp.where(is_even, total[0], other), jnp.where(is_even, other, total[0])], axis=1
    )


def local(
    stream,
    mixer_in,
    gate_in,
    dt_raw,
    dt_bias,
    a_log,
    conv_weight,
    conv_bias,
    b_proj,
    c_proj,
    d_skip,
    w_out,
    expert_index,
    gate_weights,
    norm_gain,
    w_gate,
    w_up,
    w_down,
):
    tokens = mixer_in.shape[0]
    experts = lax.axis_size("exp")
    groups = lax.axis_size("seq")
    capacity = 3 * tokens // experts
    width = stream.shape[1]
    mixed, weights = mixer(
        mixer_in, gate_in, dt_raw, dt_bias, a_log, conv_weight, conv_bias, b_proj, c_proj, d_skip, w_out
    )
    projected = project(mixed, weights)
    middle = (stream.astype(F32) + projected).astype(BF16)

    flat_exp = expert_index.reshape(-1)
    onehot = (flat_exp[:, None] == jnp.arange(experts, dtype=jnp.int32)[None, :]).astype(jnp.int32)
    ranks = jnp.cumsum(onehot, axis=0) - onehot
    slots = jnp.sum(ranks * onehot, axis=1)
    slot_id = (flat_exp * capacity + slots).reshape(tokens, 2)
    places = jnp.arange(experts * capacity, dtype=jnp.int32)
    chosen = (
        (slot_id[:, 0][None, :] == places[:, None]) | (slot_id[:, 1][None, :] == places[:, None])
    ).astype(BF16)
    outgoing = jnp.dot(chosen, middle, preferred_element_type=F32).astype(BF16)
    outgoing = outgoing.reshape(experts, capacity, width)
    arrived = lax.all_to_all(outgoing, "exp", split_axis=0, concat_axis=2, tiled=True)[0].astype(F32)
    mean_square = jnp.mean(arrived * arrived, axis=1, keepdims=True)
    normed = (arrived * lax.rsqrt(mean_square + 1e-05) * norm_gain[None, :]).astype(BF16)

    half = capacity // 2
    first = grid_gather(normed[:half], "xy")
    second = grid_gather(normed[half:], "yx")

    def feed(offsets):
        rows = jnp.stack([part[k] for part in (first, second) for k in offsets])
        flat = rows.reshape(-1, rows.shape[-1])
        gate_proj = jnp.dot(flat, w_gate[0], preferred_element_type=F32)
        up_proj = jnp.dot(flat, w_up[0], preferred_element_type=F32)
        hidden = lax.optimization_barrier((jax.nn.silu(gate_proj) * up_proj).astype(BF16))
        out = jnp.dot(hidden, w_down[0], preferred_element_type=F32).astype(BF16)
        return out.reshape((2, len(offsets)) + rows.shape[1:])

    fed = {}
    for offsets in ((0,), (1, 3), (2,)):
        out = feed(offsets)
        for at, k in enumerate(offsets):
            fed[k] = out[:, at]
    sums = []
    for which, order in ((0, "yx"), (1, "xy")):
        near = relay_scatter([fed[k][which] for k in range(SIDE)], order[0])
        sums.append(ring_scatter([near[k] for k in range(SIDE)], order[1]))
    summed = jnp.concatenate(sums, 0).astype(BF16)
    summed = summed.reshape(capacity, experts, width).transpose(1, 0, 2)
    returned = lax.all_to_all(summed, "exp", split_axis=0, concat_axis=0)
    returned = returned.reshape(experts * capacity, width)
    expert_sum = 0.0
    for k in range(2):
        pick = (slot_id[:, k][:, None] == places[None, :]).astype(BF16)
        picked = jnp.dot(pick, returned, preferred_element_type=F32)
        expert_sum = expert_sum + gate_weights[:, k][:, None] * picked
    return (middle.astype(F32) + expert_sum).astype(BF16)


def solution(mesh):
    return jax.shard_map(
        local,
        mesh=mesh,
        in_specs=(
            P("seq", "exp"),
            P("seq", "exp"),
            P("seq", "exp"),
            P("seq", "exp"),
            P("exp"),
            P("exp", None),
            P("exp", None),
            P("exp"),
            P("seq", None),
            P("seq", None),
            P("exp"),
            P("exp", "seq"),
            P("seq", None),
            P("seq", None),
            P(),
            P("exp", None, "seq"),
            P("exp", None, "seq"),
            P("exp", "seq", None),
        ),
        out_specs=P("seq", "exp"),
        check_vma=False,
    )
```
